256 devices in a mesh: gx: 32 (over y, z), gy: 8 (over x, core).
Axes of the slice: x: 4, y: 4, z: 8, core: 2. Of those that a mesh axis runs over, the one named last changes fastest.
Arguments:
- couple_inner: float32 [32, 8, 256, 256], P('gx', 'gy'), may hold values from 0.000390625 to 0.003515625
- couple_cross: float32 [32, 8, 256, 256], P('gx', 'gy'), may hold values from 0.000390625 to 0.003515625
- couple_outer: float32 [32, 8, 256, 256], P('gx', 'gy'), may hold values from 0.000390625 to 0.003515625
- margin: float32 [32, 8, 512], P('gx', 'gy'), may hold values from 0.05 to 0.5
- sources: float32 [32, 8, 512, 128], P('gx', 'gy'), may hold values from -4 to 4
- top_values: float32 [256, 8192], P('gy', 'gx'), may hold values from -6 to 6
Outputs:
- interior_solution: float32 [32, 8, 256, 128], P('gx', 'gy')
- boundary_solution: float32 [32, 8, 256, 128], P('gx', 'gy')
The draws below stay inside these ranges and needn't reach their ends.
All inputs are finite; a program needn't handle non-finite values.
Results may differ from the reference program's by a relative error of at most 0.0001.
Values sent between devices are 32-bit elements; how exact they have to be, the bound alone decides.
A program may use at most 128 MiB of HBM per device.

```python
import math
import jax
import jax.numpy as jnp
import numpy as np
from jax import lax

SIDE = 64
INT = 256
COLS = 128
LEVELS = 2
UNK = 512
NX_BOX = 32
NY_BOX = 8
TOPX = 8
TOPY = 2
BTOP = 1024


def draw_sources(key, part):
    values = jax.random.normal(key, (NX_BOX, NY_BOX, UNK, COLS), jnp.float32)
    values = jnp.clip(values, -4.0, 4.0)
    return values


def level_of(own_key, dims, pieces, low, largest):
    gain = 1.0
    for axis_at, shards_of in pieces:
        steps = jax.random.uniform(jax.random.fold_in(jax.random.fold_in(own_key, 6), axis_at), (shards_of,), jnp.float32, low / len(pieces), largest / len(pieces))
        gain = gain * jnp.repeat(jnp.exp(steps), dims[axis_at] // shards_of).reshape((-1,) + (1,) * (len(dims) - 1 - axis_at))
    return gain


def normal_values(own_key, dims, deviation, limit, shards=(), kind=jnp.bfloat16):
    factor_of = level_of(own_key, dims, shards, -0.22, 0.18) if shards else 1.0
    array = jax.random.normal(own_key, dims, jnp.float32) * deviation * factor_of
    return jnp.minimum(jnp.maximum(array, -limit), limit).astype(kind)


def setup_inputs(seed: int = 0) -> dict:
    splits = jax.random.split(jax.random.key(seed), 7)
    couple_inner = jnp.clip(0.000390625 + 0.0031249999 * jax.random.uniform(splits[0], (NX_BOX, NY_BOX, INT, INT), jnp.float32) ** level_of(splits[0], (NX_BOX, NY_BOX, INT, INT), ((0, 32), (1, 8)), -0.2, 0.2), 0.000390625, 0.003515625)
    couple_cross = jnp.clip(0.000390625 + 0.0031249999 * jax.random.uniform(splits[1], (NX_BOX, NY_BOX, INT, 4 * SIDE), jnp.float32) ** level_of(splits[1], (NX_BOX, NY_BOX, INT, 4 * SIDE), ((0, 32), (1, 8)), -0.2, 0.2), 0.000390625, 0.003515625)
    couple_outer = jnp.clip(0.000390625 + 0.0031249999 * jax.random.uniform(splits[2], (NX_BOX, NY_BOX, 4 * SIDE, 4 * SIDE), jnp.float32) ** level_of(splits[2], (NX_BOX, NY_BOX, 4 * SIDE, 4 * SIDE), ((0, 32), (1, 8)), -0.2, 0.2), 0.000390625, 0.003515625)
    margin = jnp.clip(jnp.exp(math.log(0.5) - 2.3025851 * jax.random.uniform(splits[3], (NX_BOX, NY_BOX, UNK), jnp.float32) ** level_of(splits[3], (NX_BOX, NY_BOX, UNK), ((0, 32), (1, 8)), -0.2, 0.2)), 0.05, 0.5)
    sources = draw_sources(jax.random.fold_in(splits[6], 71), 0)
    top_values = normal_values(splits[5], (TOPY * COLS, TOPX * BTOP), 1.0, 6.0, ((0, 8), (1, 32)), jnp.float32)
    return {"couple_inner": couple_inner, "couple_cross": couple_cross, "couple_outer": couple_outer, "margin": margin, "sources": sources, "top_values": top_values}


PRECISE = lax.Precision.HIGHEST
SEGMENT_TABLE = ((4, 0, 8, 2), (0, 6, 9, 3), (5, 1, 2, 10), (1, 7, 3, 11))

def placement_table():
    placement = np.zeros((4, 12, 4), np.float32)
    for member in range(4):
        for border in range(4):
            placement[member, SEGMENT_TABLE[member][border], border] = 1.0
    return jnp.asarray(placement, dtype=jnp.float32)

def product(left_side, right_side):
    return jnp.einsum('...ij,...jk->...ik', left_side, right_side, precision=PRECISE)

def solve_factor(factor, right_side):
    lower_solved = jax.scipy.linalg.solve_triangular(factor, right_side, lower=True)
    return jax.scipy.linalg.solve_triangular(factor, lower_solved, lower=True, trans=1)

def symmetric_part(raw_matrix):
    order_count = raw_matrix.shape[-1]
    off_diagonal = 1.0 - jnp.eye(order_count, dtype=jnp.float32)
    return 0.5 * (raw_matrix + jnp.swapaxes(raw_matrix, -1, -2)) * off_diagonal

def leaf_reduce(couple_inner, couple_cross, couple_outer, margin, sources):
    inner_couple = symmetric_part(couple_inner)
    outer_couple = symmetric_part(couple_outer)
    interior = couple_inner.shape[-1]
    border_size = couple_outer.shape[-1]
    inner_rows = jnp.sum(inner_couple, -1) + jnp.sum(couple_cross, -1)
    outer_rows = jnp.sum(outer_couple, -1) + jnp.sum(couple_cross, -2)
    inner_matrix = jnp.eye(interior, dtype=jnp.float32) * (inner_rows * (1.0 + margin[..., :interior]))[..., None] - inner_couple
    outer_matrix = jnp.eye(border_size, dtype=jnp.float32) * (outer_rows * (1.0 + margin[..., interior:]))[..., None] - outer_couple
    cross_matrix = -couple_cross
    factor = jnp.linalg.cholesky(inner_matrix)
    solved = solve_factor(factor, jnp.concatenate([cross_matrix, sources[..., :interior, :]], -1))
    reduced = product(jnp.swapaxes(cross_matrix, -1, -2), solved)
    boundary_map = outer_matrix - reduced[..., :border_size]
    boundary_flux = sources[..., interior:, :] - reduced[..., border_size:]
    return (boundary_map, boundary_flux, solved)

def assemble(child_maps, child_fluxes):
    placement = placement_table()
    length = child_maps.shape[-1] // 4
    blocks = child_maps.reshape(child_maps.shape[:-2] + (4, length, 4, length))
    assembled = jnp.einsum('cps,c...sltm,cqt->...plqm', placement, blocks, placement, precision=PRECISE)
    assembled = assembled.reshape(assembled.shape[:-4] + (12 * length, 12 * length))
    flux_blocks = child_fluxes.reshape(child_fluxes.shape[:-2] + (4, length, child_fluxes.shape[-1]))
    assembled_flux = jnp.einsum('cps,c...slm->...plm', placement, flux_blocks, precision=PRECISE)
    assembled_flux = assembled_flux.reshape(assembled_flux.shape[:-3] + (12 * length, child_fluxes.shape[-1]))
    return (assembled, assembled_flux)

def merge_level(assembled, assembled_flux):
    inside = assembled.shape[-1] // 3
    outer_size = assembled.shape[-1] - inside
    factor = jnp.linalg.cholesky(assembled[..., :inside, :inside])
    solved = solve_factor(factor, jnp.concatenate([assembled[..., :inside, inside:], assembled_flux[..., :inside, :]], -1))
    reduced = product(assembled[..., inside:, :inside], solved)
    parent_map = assembled[..., inside:, inside:] - reduced[..., :outer_size]
    parent_flux = assembled_flux[..., inside:, :] - reduced[..., outer_size:]
    return (parent_map, parent_flux, solved)

def child_values(full_values, length):
    placement = placement_table()
    blocks = full_values.reshape(full_values.shape[:-2] + (12, length, full_values.shape[-1]))
    picked = jnp.einsum('cps,...plm->c...slm', placement, blocks, precision=PRECISE)
    return picked.reshape(picked.shape[:-3] + (4 * length, full_values.shape[-1]))

def split_children(layout):
    shaped = layout.reshape((layout.shape[0] // 2, 2, layout.shape[1] // 2, 2) + layout.shape[2:])
    return jnp.stack([shaped[:, 0, :, 0], shaped[:, 1, :, 0], shaped[:, 0, :, 1], shaped[:, 1, :, 1]])

def join_children(stacked):
    by_rows = stacked.reshape((2, 2) + stacked.shape[1:])
    rest = tuple(range(4, by_rows.ndim))
    reordered = jnp.transpose(by_rows, (2, 1, 3, 0) + rest)
    return reordered.reshape((reordered.shape[0] * 2, reordered.shape[2] * 2) + reordered.shape[4:])

def reference(couple_inner, couple_cross, couple_outer, margin, sources, top_values):
    maps_now, fluxes_now, leaf_solved = leaf_reduce(couple_inner, couple_cross, couple_outer, margin, sources)
    saved = []
    for level_index in range(1, LEVELS):
        assembled, assembled_flux = assemble(split_children(maps_now), split_children(fluxes_now))
        maps_now, fluxes_now, solved = merge_level(assembled, assembled_flux)
        saved.append(solved)
    assembled, assembled_flux = assemble(split_children(maps_now), split_children(fluxes_now))
    inside = assembled.shape[-1] // 3
    top_data = jnp.transpose(top_values.reshape(TOPY, COLS, TOPX, BTOP), (2, 0, 3, 1))
    factor = jnp.linalg.cholesky(assembled[..., :inside, :inside])
    right_side = assembled_flux[..., :inside, :] - product(assembled[..., :inside, inside:], top_data)
    inner_values = solve_factor(factor, right_side)
    values = join_children(child_values(jnp.concatenate([inner_values, top_data], -2), inside // 4))
    for solved in reversed(saved):
        outer_size = solved.shape[-1] - COLS
        inner_values = solved[..., outer_size:] - product(solved[..., :outer_size], values)
        values = join_children(child_values(jnp.concatenate([inner_values, values], -2), solved.shape[-2] // 4))
    border_size = values.shape[-2]
    interior_solution = leaf_solved[..., border_size:] - product(leaf_solved[..., :border_size], values)
    return (interior_solution, values)
```

```python
import jax
import jax.numpy as jnp
from jax import lax
from jax.experimental import pallas as pl
from jax.experimental.pallas import tpu as pltpu
from jax.sharding import PartitionSpec as P

F32 = jnp.float32
BF16 = jnp.bfloat16
MESH = pl.DeviceIdType.MESH

LEAF_RHO = (255 * 0.003515625) / (255 * 0.003515625 + 256 * 0.000390625) / 1.05
FACE_RHO = 1.0 / 1.05
LEAF_STEPS = 5
FACE_STEPS = 6


def split(x):
    high = x.astype(BF16)
    low = (x - high.astype(F32)).astype(BF16)
    return high, low


def dot(a, b):
    return jnp.dot(a, b, preferred_element_type=F32)


def mm_split(a, b):
    return dot(a[0], b[0]) + (dot(a[0], b[1]) + dot(a[1], b[0]))


def mm(a, b):
    return mm_split(split(a), split(b))


def eye_mask(n):
    return lax.broadcasted_iota(jnp.int32, (n, n), 0) == lax.broadcasted_iota(jnp.int32, (n, n), 1)


def inverse_of(h, rho, steps):
    n = h.shape[0]
    eye = jnp.where(eye_mask(n), 1.0, 0.0).astype(F32)
    t = 1.0 / rho
    s, r = None, h
    for k in range(steps):
        square = 2.0 * t * t
        alpha = square / (square - 1.0)
        last = k == steps - 1
        rs = split(r)
        if s is None:
            s = alpha * (eye + r)
            r = alpha * mm_split(rs, rs) - (alpha - 1.0) * eye
        elif not last:
            ss = split(s)
            p = mm_split((jnp.concatenate([ss[0], rs[0]], 0), jnp.concatenate([ss[1], rs[1]], 0)), rs)
            s = alpha * (s + p[:n])
            r = alpha * p[n:] - (alpha - 1.0) * eye
        else:
            s = alpha * (s + mm_split(split(s), rs))
        t = square - 1.0
    return s


def face_solve(v, right):
    n = v.shape[0]
    on = eye_mask(n)
    d = jnp.sum(jnp.where(on, v, 0.0), axis=1, keepdims=True)
    di = 1.0 / d
    h = jnp.where(on, 0.0, -v * di)
    return mm(inverse_of(h, FACE_RHO, FACE_STEPS), right * di)


def half_swap(x):
    return pltpu.roll(x, 64, 1)


def kernel(ci, cq, co, mg, src, top, out_in, out_b, mloc, gloc, zq, zf, ut, tv, s1m, s1g, st2, r2, st3, r3, st4, r4, ur, dn2, uyi, dn1, uloc,
           send, recv, tvrecv):
    gx, gy = lax.axis_index("gx"), lax.axis_index("gy")
    lx, ly = gx % 4, gy % 4
    x0, y0 = gx - lx, gy - ly
    bx, by, cx, cy = lx % 2, ly % 2, lx // 2, ly // 2
    px, py = (bx + cx) % 2, (by + cy) % 2

    def at(i, j):
        return (x0 + i, y0 + j)

    barrier = pltpu.get_barrier_semaphore()
    for i in range(4):
        for j in range(4):
            if i or j:
                pl.semaphore_signal(barrier, 1, device_id=at((lx + i) % 4, (ly + j) % 4), device_id_type=MESH)

    def remote(k, source, target, device):
        return pltpu.make_async_remote_copy(src_ref=source, dst_ref=target, send_sem=send.at[k], recv_sem=recv.at[k],
                                            device_id=device, device_id_type=MESH)

    mate = (gx, gy + 1 - 2 * by)
    pair = (gx + 1 - 2 * bx, gy)
    side_y = at(lx, 3 - ly)
    side_x = at(3 - lx, ly)

    on_x = 1 - lx // 2
    pl.semaphore_wait(barrier, 15)
    top_sends = []
    for k in range(4):
        dx = on_x * lx * 3 + (1 - on_x) * k
        dy = on_x * k + (1 - on_x) * (lx - 2) * 3
        away = (dx - lx) * (dx - lx) + (dy - ly) * (dy - ly) > 0
        half = pl.ds((k // 2) * 128, 128)
        slot = tv.at[lx // 2, pl.ds(pl.multiple_of(ly * 32, 32), 32), :]
        copy = pltpu.make_async_remote_copy(src_ref=top.at[:, half], dst_ref=slot, send_sem=send.at[k], recv_sem=tvrecv.at[lx // 2, ly],
                                            device_id=at(dx, dy), device_id_type=MESH)
        top_sends.append((away, copy))

        @pl.when(away)
        def _():
            copy.start()

        @pl.when(jnp.logical_not(away))
        def _():
            tv[lx // 2, pl.ds(pl.multiple_of(ly * 32, 32), 32), :] = top[:, half]

    on = eye_mask(256)
    a = ci[...]
    inner = jnp.where(on, 0.0, 0.5 * (a + a.T))
    o = co[...]
    outer = jnp.where(on, 0.0, 0.5 * (o + o.T))
    q = cq[...]
    qt = q.T
    margin = mg[...]
    m_in = jnp.sum(jnp.where(on, jnp.broadcast_to(margin[:, :256], (256, 256)), 0.0), axis=1, keepdims=True)
    m_out = jnp.sum(jnp.where(on, jnp.broadcast_to(margin[:, 256:], (256, 256)), 0.0), axis=1, keepdims=True)
    d_in = (jnp.sum(inner, 1, keepdims=True) + jnp.sum(q, 1, keepdims=True)) * (1.0 + m_in)
    d_out = (jnp.sum(outer, 1, keepdims=True) + jnp.sum(qt, 1, keepdims=True)) * (1.0 + m_out)
    e_out = jnp.where(on, d_out, -outer)
    di = 1.0 / d_in
    s = inverse_of(inner * di, LEAF_RHO, LEAF_STEPS)

    ut[...] = jnp.zeros_like(ut)
    for side in range(2):
        known = (1 - px) if side == 0 else (1 - py)

        @pl.when(known == 1)
        def _():
            origin = (cx if side == 0 else 2 + cy)
            for j in range(4):
                mine = (lx - origin) * (lx - origin) + (ly - j) * (ly - j) > 0

                @pl.when(mine)
                def _():
                    piece = tv.at[side, pl.ds(j * 32, 32), :]
                    pltpu.make_async_remote_copy(src_ref=piece, dst_ref=piece, send_sem=send.at[0], recv_sem=tvrecv.at[side, j],
                                                 device_id=mate, device_id_type=MESH).wait_recv()

            flipped = tv[side].T
            b = by if side == 0 else bx
            part = jnp.where(b == 0, flipped[:64], flipped[64:])
            start = 64 * bx if side == 0 else 128 + 64 * by
            ut[pl.ds(pl.multiple_of(start, 64), 64), :] = part

    u_known = ut[...]
    moved = mm(jnp.concatenate([q, -e_out], 0), u_known)
    f_in = src[:256, :] + moved[:256]
    f_out = src[256:, :] + moved[256:]

    z = mm(s, jnp.concatenate([q, f_in], 1) * di)
    zq[...] = z[:, :256]
    zf[...] = z[:, 256:]
    reduced = mm(qt, z)
    m = e_out - reduced[:, :256]
    g = f_out + reduced[:, 256:]
    t0, t1 = m[:, :128], m[:, 128:]
    t0 = jnp.where(bx == 0, half_swap(t0), t0)
    t1 = jnp.where(by == 0, half_swap(t1), t1)
    m = jnp.concatenate([t0, t1], 1)
    places = (64 * (1 - bx), 64 * bx, 128 + 64 * (1 - by), 128 + 64 * by)
    for k in range(4):
        rows = pl.ds(pl.multiple_of(places[k], 64), 64)
        mloc[rows, :] = m[64 * k : 64 * k + 64]
        gloc[rows, :] = g[64 * k : 64 * k + 64]

    up1 = [
        remote(4, mloc.at[pl.ds(0, 192), :], s1m, mate),
        remote(5, gloc.at[pl.ds(0, 192), :], s1g, mate),
    ]
    lane = lax.broadcasted_iota(jnp.int32, (64, 128), 1)
    left = lane < 64
    zero = jnp.zeros((64, 128), F32)

    down1 = [
        remote(14, ur.at[pl.ds(64, 64), :], dn1.at[pl.ds(0, 64), :], mate),
        remote(15, ur.at[pl.ds(192, 64), :], dn1.at[pl.ds(64, 64), :], mate),
        remote(16, uyi, dn1.at[pl.ds(128, 64), :], mate),
    ]

    @pl.when(py == 0)
    def _():
        for copy in up1:
            copy.start()
        for copy in down1:
            copy.wait_recv()
        uloc[pl.ds(0, 64), :] = dn1[0:64]
        uloc[pl.ds(64, 64), :] = dn1[64:128]
        uloc[pl.ds(128, 64), :] = dn1[128:192]
        uloc[pl.ds(192, 64), :] = zero
        for copy in up1:
            copy.wait_send()

    @pl.when(py == 1)
    def _():
        up1[0].wait_recv()
        up1[1].wait_recv()
        a0, a1 = mloc[:, :128], mloc[:, 128:]
        n0 = s1m[:, :128]

        def left_of(x):
            return jnp.where(left, x, 0.0)

        def wide_root(x0_, x1_):
            return jnp.concatenate([left_of(x0_), left_of(half_swap(x0_)), left_of(half_swap(x1_))], 1)

        def wide_mate(x0_):
            return jnp.concatenate([jnp.where(left, 0.0, half_swap(x0_)), jnp.where(left, 0.0, x0_), zero], 1)

        v1 = a1[128:192, :64] + s1m[128:192, 128:192]
        gt1 = wide_root(a0[128:192], a1[128:192]) + wide_mate(n0[128:192])
        h1 = gloc[128:192, :] + s1g[128:192, :]
        x1 = face_solve(v1, jnp.concatenate([gt1, h1], 1))
        x1r, b1 = x1[:, :384], x1[:, 384:]
        g1 = jnp.concatenate([mloc[0:64, 128:256], s1m[0:64, 128:256], mloc[64:128, 128:256], s1m[64:128, 128:256], mloc[192:256, 128:256]], 0)[:, :64]
        base1 = jnp.concatenate([
            wide_root(a0[0:64], a1[0:64]), wide_mate(n0[0:64]), wide_root(a0[64:128], a1[64:128]), wide_mate(n0[64:128]),
            wide_root(a0[192:256], a1[192:256])], 0)
        p1 = mm(g1, x1)
        m1 = base1 - p1[:, :384]
        h_r = jnp.concatenate([gloc[0:64, :], s1g[0:64, :], gloc[64:128, :], s1g[64:128, :], gloc[192:256, :]], 0)
        f1 = h_r - p1[:, 384:]

        up2 = [
            remote(6, st2.at[pl.ds(0, 128), :], r2.at[pl.ds(0, 128), :], pair),
            remote(7, st2.at[pl.ds(128, 320), :], r2.at[pl.ds(128, 320), :], pair),
        ]
        down2 = [
            remote(12, ur.at[pl.ds(0, 128), :], dn2.at[pl.ds(0, 128), :], pair),
            remote(13, st2.at[pl.ds(0, 64), :], dn2.at[pl.ds(128, 64), :], pair),
        ]

        @pl.when(px == 0)
        def _():
            st2[0:128, :] = m1[0:128, :128]
            up2[0].start()
            st2[128:256, :] = f1[0:128]
            st2[256:320, :] = m1[256:320, :128]
            st2[320:384, :] = half_swap(m1[256:320, 256:])
            st2[384:448, :] = f1[256:320]
            up2[1].start()
            down2[0].wait_recv()
            down2[1].wait_recv()
            ur[0:128, :] = dn2[0:128, :]
            ur[128:256, :] = jnp.zeros((128, 128), F32)
            ur[256:320, :] = dn2[128:192, :]
            up2[0].wait_send()
            up2[1].wait_send()

        @pl.when(px == 1)
        def _():
            up2[0].wait_recv()
            up2[1].wait_recv()
            v2 = m1[0:128, :128] + r2[0:128, :]
            w0 = r2[256:320, :]
            wt0 = jnp.concatenate([zero, w0], 0).T
            gt2 = jnp.concatenate([m1[0:128, 128:256], m1[0:128, 256:] + wt0], 1)
            x2 = face_solve(v2, jnp.concatenate([gt2, f1[0:128] + r2[128:256, :]], 1))
            x2r, b2 = x2[:, :256], x2[:, 256:]
            g2 = jnp.concatenate([m1[128:320, :128], w0], 0)
            base2 = jnp.concatenate([m1[128:320, 128:], jnp.concatenate([zero, r2[320:384, :]], 1)], 0)
            p2 = mm(g2, x2)
            m2 = base2 - p2[:, :256]
            f2 = jnp.concatenate([f1[128:320], r2[384:448, :]], 0) - p2[:, 256:]

            up3 = [remote(8, st3, r3, side_y)]
            st3[0:128, :] = m2[128:, 128:]
            st3[128:256, :] = m2[128:, :128]
            st3[256:384, :] = f2[128:]
            st3[384:512, :] = m2[:128, 128:]
            st3[512:640, :] = m2[:128, :128]
            st3[640:768, :] = f2[:128]
            up3[0].start()
            up3[0].wait_recv()
            v3 = m2[128:, 128:] + r3[0:128, :]
            x3 = face_solve(v3, jnp.concatenate([m2[128:, :128], r3[128:256, :], f2[128:] + r3[256:384, :]], 1))
            x3r, b3 = x3[:, :256], x3[:, 256:]
            p3 = mm(jnp.concatenate([m2[:128, 128:], r3[384:512, :]], 0), x3)
            f3 = jnp.concatenate([f2[:128], r3[640:768, :]], 0) - p3[:, 256:]
            square = jnp.zeros((128, 128), F32)
            base3 = jnp.concatenate([
                jnp.concatenate([m2[:128, :128], square], 1), jnp.concatenate([square, r3[512:640, :]], 1)], 0)
            m3 = base3 - p3[:, :256]

            up4 = [remote(9, st4, r4, side_x)]
            st4[0:256, :] = m3[:, :128]
            st4[256:512, :] = m3[:, 128:]
            st4[512:768, :] = f3
            up4[0].start()
            up4[0].wait_recv()
            v4 = m3 + jnp.concatenate([r4[0:256, :], r4[256:512, :]], 1)
            u_x = face_solve(v4, f3 + r4[512:768, :])
            u_y = b3 - mm(x3r, u_x)
            u_xi = b2 - mm(x2r, jnp.concatenate([u_x[:128], u_y], 0))
            ur[0:128, :] = u_xi
            down2[0].start()
            st2[0:64, :] = u_y[64:]
            down2[1].start()
            ur[128:256, :] = u_x[:128]
            ur[256:320, :] = u_y[:64]
            up3[0].wait_send()
            up4[0].wait_send()
            down2[0].wait_send()
            down2[1].wait_send()

        ur[320:384, :] = zero
        down1[0].start()
        down1[1].start()
        u_yi = b1 - mm(x1r, ur[...])
        uyi[...] = u_yi
        down1[2].start()
        uloc[0:64, :] = ur[0:64, :]
        uloc[64:128, :] = ur[128:192, :]
        uloc[128:192, :] = u_yi
        uloc[192:256, :] = ur[256:320, :]
        for copy in down1:
            copy.wait_send()

    u_free = jnp.concatenate([uloc[pl.ds(pl.multiple_of(p, 64), 64), :] for p in places], 0)
    out_b[...] = u_free + u_known
    out_in[...] = zf[...] + mm(zq[...], u_free)
    for away, copy in top_sends:

        @pl.when(away)
        def _():
            copy.wait_send()


def solution(mesh):
    def local(couple_inner, couple_cross, couple_outer, margin, sources, top_values):
        vmem = pl.BlockSpec(memory_space=pltpu.VMEM)
        interior, boundary = pl.pallas_call(
            kernel,
            out_shape=(jax.ShapeDtypeStruct((256, 128), F32), jax.ShapeDtypeStruct((256, 128), F32)),
            in_specs=[vmem] * 6,
            out_specs=(vmem, vmem),
            scratch_shapes=[
                pltpu.VMEM((256, 256), F32),
                pltpu.VMEM((256, 128), F32),
                pltpu.VMEM((256, 256), F32),
                pltpu.VMEM((256, 128), F32),
                pltpu.VMEM((256, 128), F32),
                pltpu.VMEM((2, 128, 128), F32),
                pltpu.VMEM((192, 256), F32),
                pltpu.VMEM((192, 128), F32),
                pltpu.VMEM((448, 128), F32),
                pltpu.VMEM((448, 128), F32),
                pltpu.VMEM((768, 128), F32),
                pltpu.VMEM((768, 128), F32),
                pltpu.VMEM((768, 128), F32),
                pltpu.VMEM((768, 128), F32),
                pltpu.VMEM((384, 128), F32),
                pltpu.VMEM((192, 128), F32),
                pltpu.VMEM((64, 128), F32),
                pltpu.VMEM((192, 128), F32),
                pltpu.VMEM((256, 128), F32),
                pltpu.SemaphoreType.DMA((17,)),
                pltpu.SemaphoreType.DMA((17,)),
                pltpu.SemaphoreType.DMA((2, 4)),
            ],
            compiler_params=pltpu.CompilerParams(collective_id=0, has_side_effects=True),
        )(
            couple_inner.reshape(256, 256),
            couple_cross.reshape(256, 256),
            couple_outer.reshape(256, 256),
            margin.reshape(1, 512),
            sources.reshape(512, 128),
            top_values,
        )
        return interior[None, None], boundary[None, None]

    spec = P("gx", "gy", None, None)
    return jax.shard_map(
        local,
        mesh=mesh,
        in_specs=(spec, spec, spec, P("gx", "gy", None), spec, P("gy", "gx")),
        out_specs=(spec, spec),
        check_vma=False,
    )
```

```python
import jax
import jax.numpy as jnp
from jax import lax
from jax.experimental import pallas as pl
from jax.experimental.pallas import tpu as pltpu
from jax.sharding import PartitionSpec as P

F32 = jnp.float32
BF16 = jnp.bfloat16
MESH = pl.DeviceIdType.MESH

LEAF_RHO = (255 * 0.003515625) / (255 * 0.003515625 + 256 * 0.000390625) / 1.05
FACE_RHO = 1.0 / 1.05
LEAF_STEPS = 5
FACE_STEPS = 6


def split(x):
    high = x.astype(BF16)
    low = (x - high.astype(F32)).astype(BF16)
    return high, low


def dot(a, b):
    return jnp.dot(a, b, preferred_element_type=F32)


def mm_split(a, b):
    return dot(a[0], b[0]) + (dot(a[0], b[1]) + dot(a[1], b[0]))


def mm(a, b):
    return mm_split(split(a), split(b))


def eye_mask(n):
    return lax.broadcasted_iota(jnp.int32, (n, n), 0) == lax.broadcasted_iota(jnp.int32, (n, n), 1)


def inverse_of(h, rho, steps):
    n = h.shape[0]
    eye = jnp.where(eye_mask(n), 1.0, 0.0).astype(F32)
    t = 1.0 / rho
    s, r = None, h
    for k in range(steps):
        square = 2.0 * t * t
        alpha = square / (square - 1.0)
        last = k == steps - 1
        rs = split(r)
        if s is None:
            s = alpha * (eye + r)
            r = alpha * mm_split(rs, rs) - (alpha - 1.0) * eye
        elif not last:
            ss = split(s)
            p = mm_split((jnp.concatenate([ss[0], rs[0]], 0), jnp.concatenate([ss[1], rs[1]], 0)), rs)
            s = alpha * (s + p[:n])
            r = alpha * p[n:] - (alpha - 1.0) * eye
        else:
            s = alpha * (s + mm_split(split(s), rs))
        t = square - 1.0
    return s


def face_inverse(v):
    n = v.shape[0]
    on = eye_mask(n)
    di = 1.0 / jnp.sum(jnp.where(on, v, 0.0), axis=1, keepdims=True)
    h = jnp.where(on, 0.0, -v * di)
    return inverse_of(h, FACE_RHO, FACE_STEPS), di


def half_swap(x):
    return pltpu.roll(x, 64, 1)


def cat(*parts, axis=0):
    return jnp.concatenate(parts, axis)


def kernel(ci_h, cq_h, co_h, mg_h, src_h, top, out_in, out_b, ci, cq, co, mg, src, mloc, gloc, ut, tv, s1m, s1g, st2, r2, st3, r3, st4, r4, ur,
           dnst, dn2, uyi, dn1, uloc, load, send, recv, tvrecv):
    gx, gy = lax.axis_index("gx"), lax.axis_index("gy")
    lx, ly = gx % 4, gy % 4
    x0, y0 = gx - lx, gy - ly
    bx, by, cx, cy = lx % 2, ly % 2, lx // 2, ly // 2
    px, py = (bx + cx) % 2, (by + cy) % 2

    def at(i, j):
        return (x0 + i, y0 + j)

    barrier = pltpu.get_barrier_semaphore()
    for i in range(4):
        for j in range(4):
            if i or j:
                pl.semaphore_signal(barrier, 1, device_id=at((lx + i) % 4, (ly + j) % 4), device_id_type=MESH)

    loads = [pltpu.make_async_copy(h, v, load.at[k]) for k, (h, v) in enumerate(((ci_h, ci), (cq_h, cq), (mg_h, mg), (co_h, co), (src_h, src)))]
    for copy in loads:
        copy.start()

    def remote(k, source, target, device):
        return pltpu.make_async_remote_copy(src_ref=source, dst_ref=target, send_sem=send.at[k], recv_sem=recv.at[k],
                                            device_id=device, device_id_type=MESH)

    def rows(ref, start, count):
        return ref.at[pl.ds(start, count), :]

    mate = (gx, gy + 1 - 2 * by)
    pair = (gx + 1 - 2 * bx, gy)
    side_y = at(lx, 3 - ly)
    side_x = at(3 - lx, ly)

    on = eye_mask(256)
    loads[0].wait()
    a = ci[...]
    inner = jnp.where(on, 0.0, 0.5 * (a + a.T))
    loads[1].wait()
    loads[2].wait()
    q = cq[...]
    margin = mg[...]
    m_in = jnp.sum(jnp.where(on, jnp.broadcast_to(margin[:, :256], (256, 256)), 0.0), axis=1, keepdims=True)
    m_out = jnp.sum(jnp.where(on, jnp.broadcast_to(margin[:, 256:], (256, 256)), 0.0), axis=1, keepdims=True)
    d_in = (jnp.sum(inner, 1, keepdims=True) + jnp.sum(q, 1, keepdims=True)) * (1.0 + m_in)
    di = 1.0 / d_in

    pl.semaphore_wait(barrier, 15)
    on_x = 1 - lx // 2
    top_sends = []
    for k in range(4):
        dx = on_x * lx * 3 + (1 - on_x) * k
        dy = on_x * k + (1 - on_x) * (lx - 2) * 3
        away = (dx - lx) * (dx - lx) + (dy - ly) * (dy - ly) > 0
        piece = top.at[:, pl.ds((k // 2) * 128, 128)]
        slot = tv.at[lx // 2, pl.ds(pl.multiple_of(ly * 32, 32), 32), :]
        copy = pltpu.make_async_remote_copy(src_ref=piece, dst_ref=slot, send_sem=send.at[k], recv_sem=tvrecv.at[lx // 2, ly],
                                            device_id=at(dx, dy), device_id_type=MESH)
        here = pltpu.make_async_copy(piece, slot, load.at[5])
        top_sends.append((away, copy, here))

        @pl.when(away)
        def _():
            copy.start()

        @pl.when(jnp.logical_not(away))
        def _():
            here.start()

    s = inverse_of(inner * di, LEAF_RHO, LEAF_STEPS)
    qt = q.T
    loads[3].wait()
    o = co[...]
    outer = jnp.where(on, 0.0, 0.5 * (o + o.T))
    d_out = (jnp.sum(outer, 1, keepdims=True) + jnp.sum(qt, 1, keepdims=True)) * (1.0 + m_out)
    e_out = jnp.where(on, d_out, -outer)
    zq = mm(s, q * di)
    m = e_out - mm(qt, zq)
    t0, t1 = m[:, :128], m[:, 128:]
    t0 = jnp.where(bx == 0, half_swap(t0), t0)
    t1 = jnp.where(by == 0, half_swap(t1), t1)
    places = [pl.multiple_of(p, 64) for p in (64 * (1 - bx), 64 * bx, 128 + 64 * (1 - by), 128 + 64 * by)]
    for k in range(4):
        mloc[pl.ds(places[k], 64), :] = cat(t0[64 * k : 64 * k + 64], t1[64 * k : 64 * k + 64], axis=1)

    def leaf_flux():
        ut[...] = jnp.zeros_like(ut)
        for away, _, here in top_sends:

            @pl.when(jnp.logical_not(away))
            def _():
                here.wait()

        for side in range(2):
            known = (1 - px) if side == 0 else (1 - py)

            @pl.when(known == 1)
            def _():
                origin = cx if side == 0 else 2 + cy
                for j in range(4):
                    mine = (lx - origin) * (lx - origin) + (ly - j) * (ly - j) > 0

                    @pl.when(mine)
                    def _():
                        piece = tv.at[side, pl.ds(j * 32, 32), :]
                        pltpu.make_async_remote_copy(src_ref=piece, dst_ref=piece, send_sem=send.at[0], recv_sem=tvrecv.at[side, j],
                                                     device_id=mate, device_id_type=MESH).wait_recv()

                flipped = tv[side].T
                b = by if side == 0 else bx
                part = jnp.where(b == 0, flipped[:64], flipped[64:])
                start = 64 * bx if side == 0 else 128 + 64 * by
                ut[pl.ds(pl.multiple_of(start, 64), 64), :] = part

        loads[4].wait()
        moved = mm(cat(q, -e_out), ut[...])
        z = mm(s, (src[:256, :] + moved[:256]) * di)
        g = src[256:, :] + moved[256:] + mm(qt, z)
        for k in range(4):
            gloc[pl.ds(places[k], 64), :] = g[64 * k : 64 * k + 64]
        src[:256, :] = z

    up1 = [
        remote(4, rows(mloc, 128, 64), rows(s1m, 128, 64), mate),
        remote(5, rows(mloc, 0, 128), rows(s1m, 0, 128), mate),
        remote(6, rows(gloc, 0, 192), s1g, mate),
    ]
    down1 = [
        remote(7, rows(ur, 64, 64), rows(dn1, 0, 64), mate),
        remote(8, rows(ur, 192, 64), rows(dn1, 64, 64), mate),
        remote(9, uyi, rows(dn1, 128, 64), mate),
    ]
    left = lax.broadcasted_iota(jnp.int32, (64, 128), 1) < 64
    zero = jnp.zeros((64, 128), F32)

    @pl.when(py == 0)
    def _():
        up1[0].start()
        up1[1].start()
        leaf_flux()
        up1[2].start()
        for copy in down1:
            copy.wait_recv()
        uloc[0:192, :] = dn1[...]
        uloc[192:256, :] = zero
        for copy in up1:
            copy.wait_send()

    @pl.when(py == 1)
    def _():
        up1[0].wait_recv()
        v1 = mloc[128:192, 128:256] + s1m[128:192, 128:256]
        k1, d1 = face_inverse(v1[:, :64])
        leaf_flux()
        up1[1].wait_recv()

        def left_of(x):
            return jnp.where(left, x, 0.0)

        def wide_root(k):
            x, y = mloc[k : k + 64, :128], mloc[k : k + 64, 128:]
            return cat(left_of(x), left_of(half_swap(x)), left_of(half_swap(y)), axis=1)

        def wide_mate(k):
            x = s1m[k : k + 64, :128]
            return cat(jnp.where(left, 0.0, half_swap(x)), jnp.where(left, 0.0, x), zero, axis=1)

        gt1 = wide_root(128) + wide_mate(128)
        g1 = cat(mloc[0:64, 128:256], s1m[0:64, 128:256], mloc[64:128, 128:256], s1m[64:128, 128:256], mloc[192:256, 128:256])[:, :64]
        base1 = cat(wide_root(0), wide_mate(0), wide_root(64), wide_mate(64), wide_root(192))
        up1[2].wait_recv()
        x1 = mm(k1, cat(gt1, gloc[128:192, :] + s1g[128:192, :], axis=1) * d1)
        x1r, b1 = x1[:, :384], x1[:, 384:]
        p1 = mm(g1, x1)
        m1 = base1 - p1[:, :384]
        f1 = cat(gloc[0:64, :], s1g[0:64, :], gloc[64:128, :], s1g[64:128, :], gloc[192:256, :]) - p1[:, 384:]

        up2 = [
            remote(10, rows(st2, 0, 128), rows(r2, 0, 128), pair),
            remote(11, rows(st2, 128, 128), rows(r2, 128, 128), pair),
            remote(12, rows(st2, 256, 192), rows(r2, 256, 192), pair),
        ]
        down2 = [remote(13, dnst, dn2, pair)]

        @pl.when(px == 0)
        def _():
            st2[0:128, :] = m1[0:128, :128]
            up2[0].start()
            st2[128:192, :] = m1[256:320, :128]
            st2[192:256, :] = half_swap(m1[256:320, 256:])
            up2[1].start()
            st2[256:384, :] = f1[0:128]
            st2[384:448, :] = f1[256:320]
            up2[2].start()
            down2[0].wait_recv()
            ur[0:128, :] = dn2[0:128, :]
            ur[128:256, :] = jnp.zeros((128, 128), F32)
            ur[256:320, :] = dn2[128:192, :]
            for copy in up2:
                copy.wait_send()

        @pl.when(px == 1)
        def _():
            up2[0].wait_recv()
            k2, d2 = face_inverse(m1[0:128, :128] + r2[0:128, :])
            up2[1].wait_recv()
            w0 = r2[128:192, :]
            gt2 = cat(m1[0:128, 128:256], m1[0:128, 256:] + cat(zero, w0).T, axis=1)
            base2 = cat(m1[128:320, 128:], cat(zero, r2[192:256, :], axis=1))
            up2[2].wait_recv()
            x2 = mm(k2, cat(gt2, f1[0:128] + r2[256:384, :], axis=1) * d2)
            x2r, b2 = x2[:, :256], x2[:, 256:]

            up3 = [
                remote(14, rows(st3, 0, 128), rows(r3, 0, 128), side_y),
                remote(15, rows(st3, 128, 256), rows(r3, 128, 256), side_y),
                remote(16, rows(st3, 384, 128), rows(r3, 384, 128), side_y),
                remote(17, rows(st3, 512, 128), rows(r3, 512, 128), side_y),
            ]
            p2y = mm(cat(m1[256:320, :128], w0), x2)
            m2y = base2[128:] - p2y[:, :256]
            f2y = cat(f1[256:320], r2[384:448, :]) - p2y[:, 256:]
            st3[0:128, :] = m2y[:, 128:]
            up3[0].start()
            st3[128:256, :] = m2y[:, :128]
            st3[256:384, :] = f2y
            up3[1].start()
            p2x = mm(m1[128:256, :128], x2)
            m2x = base2[:128] - p2x[:, :256]
            f2x = f1[128:256] - p2x[:, 256:]
            st3[384:512, :] = m2x[:, :128]
            up3[2].start()
            st3[512:640, :] = f2x
            up3[3].start()
            up3[0].wait_recv()
            k3, d3 = face_inverse(m2y[:, 128:] + r3[0:128, :])
            up3[1].wait_recv()
            yx = r3[128:256, :]
            x3 = mm(k3, cat(m2y[:, :128], yx, f2y + r3[256:384, :], axis=1) * d3)
            x3r, b3 = x3[:, :256], x3[:, 256:]
            p3 = mm(cat(m2x[:, 128:], yx.T), x3)
            up3[2].wait_recv()

            up4 = [
                remote(18, rows(st4, 0, 384), rows(r4, 0, 384), side_x),
                remote(19, rows(st4, 384, 256), rows(r4, 384, 256), side_x),
            ]
            m00, m01, m11 = m2x[:, :128] - p3[:128, :128], -p3[:128, 128:256], r3[384:512, :] - p3[128:, 128:256]
            st4[0:128, :] = m00
            st4[128:256, :] = m01
            st4[256:384, :] = m11
            up4[0].start()
            up3[3].wait_recv()
            f3 = cat(f2x, r3[512:640, :]) - p3[:, 256:]
            st4[384:640, :] = f3
            up4[1].start()
            back = mm(x2r[:, 128:], x3)
            down_map = cat(x3r, cat(x2r[:, :128], jnp.zeros((128, 128), F32), axis=1) - back[:, :256])
            down_free = cat(b3, b2 - back[:, 256:])
            up4[0].wait_recv()
            v01 = m01 + r4[128:256, :]
            k4, d4 = face_inverse(cat(cat(m00 + r4[0:128, :], v01, axis=1), cat(v01.T, m11 + r4[256:384, :], axis=1)))
            up4[1].wait_recv()
            u_x = mm(k4, (f3 + r4[384:640, :]) * d4)
            u_low = down_free - mm(down_map, u_x)
            dnst[0:128, :] = u_low[128:]
            dnst[128:192, :] = u_low[64:128]
            down2[0].start()
            ur[0:128, :] = u_low[128:]
            ur[128:256, :] = u_x[:128]
            ur[256:320, :] = u_low[:64]
            for copy in up3 + up4 + down2:
                copy.wait_send()

        ur[320:384, :] = zero
        down1[0].start()
        down1[1].start()
        u_yi = b1 - mm(x1r, ur[...])
        uyi[...] = u_yi
        down1[2].start()
        uloc[0:64, :] = ur[0:64, :]
        uloc[64:128, :] = ur[128:192, :]
        uloc[128:192, :] = u_yi
        uloc[192:256, :] = ur[256:320, :]
        for copy in down1:
            copy.wait_send()

    u_free = cat(*[uloc[pl.ds(p, 64), :] for p in places])
    out_b[...] = u_free + ut[...]
    out_in[...] = src[:256, :] + mm(zq, u_free)
    for away, copy, _ in top_sends:

        @pl.when(away)
        def _():
            copy.wait_send()


def solution(mesh):
    def local(couple_inner, couple_cross, couple_outer, margin, sources, top_values):
        vmem = pl.BlockSpec(memory_space=pltpu.VMEM)
        anywhere = pl.BlockSpec(memory_space=pl.ANY)
        shapes = [(256, 256)] * 3 + [(1, 512), (512, 128), (256, 256), (256, 128), (256, 128), (2, 128, 128), (192, 256), (192, 128),
                  (448, 128), (448, 128), (640, 128), (640, 128), (640, 128), (640, 128), (384, 128), (192, 128), (192, 128), (64, 128),
                  (192, 128), (256, 128)]
        dma = pltpu.SemaphoreType.DMA
        interior, boundary = pl.pallas_call(
            kernel,
            out_shape=(pltpu.VMEM((256, 128), F32), pltpu.VMEM((256, 128), F32)),
            in_specs=[anywhere] * 6,
            out_specs=(vmem, vmem),
            scratch_shapes=[pltpu.VMEM(shape, F32) for shape in shapes] + [dma((6,)), dma((20,)), dma((20,)), dma((2, 4))],
            compiler_params=pltpu.CompilerParams(collective_id=0, has_side_effects=True),
        )(
            couple_inner.reshape(256, 256),
            couple_cross.reshape(256, 256),
            couple_outer.reshape(256, 256),
            margin.reshape(1, 512),
            sources.reshape(512, 128),
            top_values,
        )
        return interior[None, None], boundary[None, None]

    spec = P("gx", "gy", None, None)
    return jax.shard_map(
        local,
        mesh=mesh,
        in_specs=(spec, spec, spec, P("gx", "gy", None), spec, P("gy", "gx")),
        out_specs=(spec, spec),
        check_vma=False,
    )
```

```python
import jax
import jax.numpy as jnp
from jax import lax
from jax.experimental import pallas as pl
from jax.experimental.pallas import tpu as pltpu
from jax.sharding import PartitionSpec as P

F32 = jnp.float32
BF16 = jnp.bfloat16
MESH = pl.DeviceIdType.MESH

LEAF_RHO = (255 * 0.003515625) / (255 * 0.003515625 + 256 * 0.000390625) / 1.05
FACE_RHO = 1.0 / 1.05
LEAF_STEPS = 5
FACE_STEPS = 6


def split(x):
    high = x.astype(BF16)
    low = (x - high.astype(F32)).astype(BF16)
    return high, low


def dot(a, b):
    return jnp.dot(a, b, preferred_element_type=F32)


def mm_split(a, b):
    if a[0].shape[1] % 128:
        return dot(a[0], b[0]) + (dot(a[0], b[1]) + dot(a[1], b[0]))
    return dot(jnp.concatenate([a[0], a[0], a[1]], 1), jnp.concatenate([b[0], b[1], b[0]], 0))


def mm(a, b):
    return mm_split(split(a), split(b))


def eye_mask(n):
    return lax.broadcasted_iota(jnp.int32, (n, n), 0) == lax.broadcasted_iota(jnp.int32, (n, n), 1)


def inverse_of(h, rho, steps):
    n = h.shape[0]
    eye = jnp.where(eye_mask(n), 1.0, 0.0).astype(F32)
    t = 1.0 / rho
    s, r = None, h
    for k in range(steps):
        square = 2.0 * t * t
        alpha = square / (square - 1.0)
        if k == steps - 1:
            s = alpha * (s + dot(s.astype(BF16), r.astype(BF16)))
        elif k == steps - 2:
            rs = split(r)
            p = mm_split(split(s), rs)
            r = alpha * dot(rs[0], rs[0]) - (alpha - 1.0) * eye
            s = alpha * (s + p)
        elif s is None:
            rs = split(r)
            s = alpha * (eye + r)
            r = alpha * mm_split(rs, rs) - (alpha - 1.0) * eye
        else:
            ss, rs = split(s), split(r)
            p = mm_split((jnp.concatenate([ss[0], rs[0]], 0), jnp.concatenate([ss[1], rs[1]], 0)), rs)
            s = alpha * (s + p[:n])
            r = alpha * p[n:] - (alpha - 1.0) * eye
        t = square - 1.0
    return s


def face_inverse(v):
    n = v.shape[0]
    on = eye_mask(n)
    di = 1.0 / jnp.sum(jnp.where(on, v, 0.0), axis=1, keepdims=True)
    h = jnp.where(on, 0.0, -v * di)
    return inverse_of(h, FACE_RHO, FACE_STEPS), di


def half_swap(x):
    return pltpu.roll(x, 64, 1)


def cat(*parts, axis=0):
    return jnp.concatenate(parts, axis)


def kernel(ci_h, cq_h, co_h, mg_h, src_h, top, out_in, out_b, ci, cq, co, mg, src, mloc, gloc, ut, tv, s1m, s1g, st2, r2, st3, r3, st4, r4, ur,
           dnst, dn2, uyi, dn1, uloc, x1b, load, send, recv, tvrecv):
    gx, gy = lax.axis_index("gx"), lax.axis_index("gy")
    lx, ly = gx % 4, gy % 4
    x0, y0 = gx - lx, gy - ly
    bx, by, cx, cy = lx % 2, ly % 2, lx // 2, ly // 2
    px, py = (bx + cx) % 2, (by + cy) % 2

    def at(i, j):
        return (x0 + i, y0 + j)

    barrier = pltpu.get_barrier_semaphore()
    for i in range(4):
        for j in range(4):
            if i or j:
                pl.semaphore_signal(barrier, 1, device_id=at((lx + i) % 4, (ly + j) % 4), device_id_type=MESH)

    loads = [pltpu.make_async_copy(h, v, load.at[k]) for k, (h, v) in enumerate(((ci_h, ci), (cq_h, cq), (mg_h, mg), (co_h, co), (src_h, src)))]
    for copy in loads:
        copy.start()

    def remote(k, source, target, device):
        return pltpu.make_async_remote_copy(src_ref=source, dst_ref=target, send_sem=send.at[k], recv_sem=recv.at[k],
                                            device_id=device, device_id_type=MESH)

    def rows(ref, start, count):
        return ref.at[pl.ds(start, count), :]

    mate = (gx, gy + 1 - 2 * by)
    pair = (gx + 1 - 2 * bx, gy)
    side_y = at(lx, 3 - ly)
    side_x = at(3 - lx, ly)

    on = eye_mask(256)
    loads[0].wait()
    a = ci[...]
    inner = jnp.where(on, 0.0, 0.5 * (a + a.T))
    loads[1].wait()
    loads[2].wait()
    q = cq[...]
    margin = mg[...]
    m_in = jnp.sum(jnp.where(on, jnp.broadcast_to(margin[:, :256], (256, 256)), 0.0), axis=1, keepdims=True)
    m_out = jnp.sum(jnp.where(on, jnp.broadcast_to(margin[:, 256:], (256, 256)), 0.0), axis=1, keepdims=True)
    d_in = (jnp.sum(inner, 1, keepdims=True) + jnp.sum(q, 1, keepdims=True)) * (1.0 + m_in)
    di = 1.0 / d_in

    s = inverse_of(inner * di, LEAF_RHO, LEAF_STEPS)

    pl.semaphore_wait(barrier, 15)
    on_x = 1 - lx // 2
    top_sends = []
    for k in range(4):
        dx = on_x * lx * 3 + (1 - on_x) * k
        dy = on_x * k + (1 - on_x) * (lx - 2) * 3
        away = (dx - lx) * (dx - lx) + (dy - ly) * (dy - ly) > 0
        piece = top.at[:, pl.ds((k // 2) * 128, 128)]
        slot = tv.at[lx // 2, pl.ds(pl.multiple_of(ly * 32, 32), 32), :]
        copy = pltpu.make_async_remote_copy(src_ref=piece, dst_ref=slot, send_sem=send.at[k], recv_sem=tvrecv.at[lx // 2, ly],
                                            device_id=at(dx, dy), device_id_type=MESH)
        here = pltpu.make_async_copy(piece, slot, load.at[5])
        top_sends.append((away, copy, here))

        @pl.when(away)
        def _():
            copy.start()

        @pl.when(jnp.logical_not(away))
        def _():
            here.start()

    qt = q.T
    loads[3].wait()
    o = co[...]
    outer = jnp.where(on, 0.0, 0.5 * (o + o.T))
    d_out = (jnp.sum(outer, 1, keepdims=True) + jnp.sum(qt, 1, keepdims=True)) * (1.0 + m_out)
    e_out = jnp.where(on, d_out, -outer)
    zq = mm(s, q * di)
    m = e_out - mm(qt, zq)
    t0, t1 = m[:, :128], m[:, 128:]
    t0 = jnp.where(bx == 0, half_swap(t0), t0)
    t1 = jnp.where(by == 0, half_swap(t1), t1)
    places = [pl.multiple_of(p, 64) for p in (64 * (1 - bx), 64 * bx, 128 + 64 * (1 - by), 128 + 64 * by)]
    for k in range(4):
        mloc[pl.ds(places[k], 64), :] = cat(t0[64 * k : 64 * k + 64], t1[64 * k : 64 * k + 64], axis=1)

    def leaf_flux():
        ut[...] = jnp.zeros_like(ut)
        for away, _, here in top_sends:

            @pl.when(jnp.logical_not(away))
            def _():
                here.wait()

        for side in range(2):
            known = (1 - px) if side == 0 else (1 - py)

            @pl.when(known == 1)
            def _():
                origin = cx if side == 0 else 2 + cy
                for j in range(4):
                    mine = (lx - origin) * (lx - origin) + (ly - j) * (ly - j) > 0

                    @pl.when(mine)
                    def _():
                        piece = tv.at[side, pl.ds(j * 32, 32), :]
                        pltpu.make_async_remote_copy(src_ref=piece, dst_ref=piece, send_sem=send.at[0], recv_sem=tvrecv.at[side, j],
                                                     device_id=mate, device_id_type=MESH).wait_recv()

                flipped = tv[side].T
                b = by if side == 0 else bx
                part = jnp.where(b == 0, flipped[:64], flipped[64:])
                start = 64 * bx if side == 0 else 128 + 64 * by
                ut[pl.ds(pl.multiple_of(start, 64), 64), :] = part

        loads[4].wait()
        moved = mm(cat(q, -e_out), ut[...])
        z = mm(s, (src[:256, :] + moved[:256]) * di)
        g = src[256:, :] + moved[256:] + mm(qt, z)
        for k in range(4):
            gloc[pl.ds(places[k], 64), :] = g[64 * k : 64 * k + 64]
        src[:256, :] = z

    up1 = [
        remote(4, rows(mloc, 128, 64), rows(s1m, 128, 64), mate),
        remote(5, rows(mloc, 0, 128), rows(s1m, 0, 128), mate),
        remote(6, rows(gloc, 0, 192), s1g, mate),
    ]
    down1 = [
        remote(7, rows(ur, 64, 64), rows(dn1, 0, 64), mate),
        remote(8, rows(ur, 192, 64), rows(dn1, 64, 64), mate),
        remote(9, uyi, rows(dn1, 128, 64), mate),
    ]
    left = lax.broadcasted_iota(jnp.int32, (64, 128), 1) < 64
    zero = jnp.zeros((64, 128), F32)

    @pl.when(py == 0)
    def _():
        up1[0].start()
        up1[1].start()
        leaf_flux()
        up1[2].start()
        for copy in down1:
            copy.wait_recv()
        uloc[0:192, :] = dn1[...]
        uloc[192:256, :] = zero
        for copy in up1:
            copy.wait_send()

    @pl.when(py == 1)
    def _():
        up1[0].wait_recv()
        v1 = mloc[128:192, 128:256] + s1m[128:192, 128:256]
        k1, d1 = face_inverse(v1[:, :64])
        up1[1].wait_recv()

        def left_of(x):
            return jnp.where(left, x, 0.0)

        def wide_root(k):
            x, y = mloc[k : k + 64, :128], mloc[k : k + 64, 128:]
            return cat(left_of(x), left_of(half_swap(x)), left_of(half_swap(y)), axis=1)

        def wide_mate(k):
            x = s1m[k : k + 64, :128]
            return cat(jnp.where(left, 0.0, half_swap(x)), jnp.where(left, 0.0, x), zero, axis=1)

        gt1 = wide_root(128) + wide_mate(128)
        g1 = cat(mloc[0:64, 128:256], s1m[0:64, 128:256], mloc[64:128, 128:256], s1m[64:128, 128:256], mloc[192:256, 128:256])[:, :64]
        base1 = cat(wide_root(0), wide_mate(0), wide_root(64), wide_mate(64), wide_root(192))
        x1r = mm(k1, gt1 * d1)
        m1 = base1 - mm(g1, x1r)

        def flux1():
            leaf_flux()
            up1[2].wait_recv()
            b1 = mm(k1, (gloc[128:192, :] + s1g[128:192, :]) * d1)
            x1b[...] = b1
            return cat(gloc[0:64, :], s1g[0:64, :], gloc[64:128, :], s1g[64:128, :], gloc[192:256, :]) - mm(g1, b1)

        up2 = [
            remote(10, rows(st2, 0, 128), rows(r2, 0, 128), pair),
            remote(11, rows(st2, 128, 128), rows(r2, 128, 128), pair),
            remote(12, rows(st2, 256, 192), rows(r2, 256, 192), pair),
        ]
        down2 = [remote(13, dnst, dn2, pair)]

        @pl.when(px == 0)
        def _():
            st2[0:128, :] = m1[0:128, :128]
            up2[0].start()
            st2[128:192, :] = m1[256:320, :128]
            st2[192:256, :] = half_swap(m1[256:320, 256:])
            up2[1].start()
            f1 = flux1()
            st2[256:384, :] = f1[0:128]
            st2[384:448, :] = f1[256:320]
            up2[2].start()
            down2[0].wait_recv()
            ur[0:128, :] = dn2[0:128, :]
            ur[128:256, :] = jnp.zeros((128, 128), F32)
            ur[256:320, :] = dn2[128:192, :]
            for copy in up2:
                copy.wait_send()

        @pl.when(px == 1)
        def _():
            f1 = flux1()
            up2[0].wait_recv()
            k2, d2 = face_inverse(m1[0:128, :128] + r2[0:128, :])
            up2[1].wait_recv()
            w0 = r2[128:192, :]
            gt2 = cat(m1[0:128, 128:256], m1[0:128, 256:] + cat(zero, w0).T, axis=1)
            x2r = mm(k2, gt2 * d2)

            up3 = [
                remote(14, rows(st3, 0, 128), rows(r3, 0, 128), side_y),
                remote(15, rows(st3, 128, 128), rows(r3, 128, 128), side_y),
                remote(16, rows(st3, 256, 128), rows(r3, 256, 128), side_y),
                remote(17, rows(st3, 384, 256), rows(r3, 384, 256), side_y),
            ]
            g2y = cat(m1[256:320, :128], w0)
            m2y = cat(m1[256:320, 128:], cat(zero, r2[192:256, :], axis=1)) - mm(g2y, x2r)
            st3[0:128, :] = m2y[:, 128:]
            up3[0].start()
            st3[128:256, :] = m2y[:, :128]
            up3[1].start()
            g2x = m1[128:256, :128]
            m2x = m1[128:256, 128:] - mm(g2x, x2r)
            st3[256:384, :] = m2x[:, :128]
            up3[2].start()
            up2[2].wait_recv()
            b2 = mm(k2, (f1[0:128] + r2[256:384, :]) * d2)
            f2y = cat(f1[256:320], r2[384:448, :]) - mm(g2y, b2)
            f2x = f1[128:256] - mm(g2x, b2)
            st3[384:512, :] = f2y
            st3[512:640, :] = f2x
            up3[3].start()
            up3[0].wait_recv()
            k3, d3 = face_inverse(m2y[:, 128:] + r3[0:128, :])
            up3[1].wait_recv()
            yx = r3[128:256, :]
            x3r = mm(k3, cat(m2y[:, :128], yx, axis=1) * d3)
            g3 = cat(m2x[:, 128:], yx.T)
            p3 = mm(g3, x3r)
            up3[2].wait_recv()

            up4 = [
                remote(18, rows(st4, 0, 384), rows(r4, 0, 384), side_x),
                remote(19, rows(st4, 384, 256), rows(r4, 384, 256), side_x),
            ]
            m00, m01, m11 = m2x[:, :128] - p3[:128, :128], -p3[:128, 128:], r3[256:384, :] - p3[128:, 128:]
            st4[0:128, :] = m00
            st4[128:256, :] = m01
            st4[256:384, :] = m11
            up4[0].start()
            up3[3].wait_recv()
            b3 = mm(k3, (f2y + r3[384:512, :]) * d3)
            f3 = cat(f2x, r3[512:640, :]) - mm(g3, b3)
            st4[384:640, :] = f3
            up4[1].start()
            back = mm(x2r[:, 128:], cat(x3r, b3, axis=1))
            down_map = cat(x3r, cat(x2r[:, :128], jnp.zeros((128, 128), F32), axis=1) - back[:, :256])
            down_free = cat(b3, b2 - back[:, 256:])
            up4[0].wait_recv()
            v01 = m01 + r4[128:256, :]
            k4, d4 = face_inverse(cat(cat(m00 + r4[0:128, :], v01, axis=1), cat(v01.T, m11 + r4[256:384, :], axis=1)))
            up4[1].wait_recv()
            u_x = mm(k4, (f3 + r4[384:640, :]) * d4)
            u_low = down_free - mm(down_map, u_x)
            dnst[0:128, :] = u_low[128:]
            dnst[128:192, :] = u_low[64:128]
            down2[0].start()
            ur[0:128, :] = u_low[128:]
            ur[128:256, :] = u_x[:128]
            ur[256:320, :] = u_low[:64]
            for copy in up3 + up4 + down2:
                copy.wait_send()

        ur[320:384, :] = zero
        down1[0].start()
        down1[1].start()
        u_yi = x1b[...] - mm(x1r, ur[...])
        uyi[...] = u_yi
        down1[2].start()
        uloc[0:64, :] = ur[0:64, :]
        uloc[64:128, :] = ur[128:192, :]
        uloc[128:192, :] = u_yi
        uloc[192:256, :] = ur[256:320, :]
        for copy in down1:
            copy.wait_send()

    u_free = cat(*[uloc[pl.ds(p, 64), :] for p in places])
    out_b[...] = u_free + ut[...]
    out_in[...] = src[:256, :] + mm(zq, u_free)
    for away, copy, _ in top_sends:

        @pl.when(away)
        def _():
            copy.wait_send()


def solution(mesh):
    def local(couple_inner, couple_cross, couple_outer, margin, sources, top_values):
        vmem = pl.BlockSpec(memory_space=pltpu.VMEM)
        anywhere = pl.BlockSpec(memory_space=pl.ANY)
        shapes = [(256, 256)] * 3 + [(1, 512), (512, 128), (256, 256), (256, 128), (256, 128), (2, 128, 128), (192, 256), (192, 128),
                  (448, 128), (448, 128), (640, 128), (640, 128), (640, 128), (640, 128), (384, 128), (192, 128), (192, 128), (64, 128),
                  (192, 128), (256, 128), (64, 128)]
        dma = pltpu.SemaphoreType.DMA
        interior, boundary = pl.pallas_call(
            kernel,
            out_shape=(pltpu.VMEM((256, 128), F32), pltpu.VMEM((256, 128), F32)),
            in_specs=[anywhere] * 6,
            out_specs=(vmem, vmem),
            scratch_shapes=[pltpu.VMEM(shape, F32) for shape in shapes] + [dma((6,)), dma((20,)), dma((20,)), dma((2, 4))],
            compiler_params=pltpu.CompilerParams(collective_id=0, has_side_effects=True),
        )(
            couple_inner.reshape(256, 256),
            couple_cross.reshape(256, 256),
            couple_outer.reshape(256, 256),
            margin.reshape(1, 512),
            sources.reshape(512, 128),
            top_values,
        )
        return interior[None, None], boundary[None, None]

    spec = P("gx", "gy", None, None)
    return jax.shard_map(
        local,
        mesh=mesh,
        in_specs=(spec, spec, spec, P("gx", "gy", None), spec, P("gy", "gx")),
        out_specs=(spec, spec),
        check_vma=False,
    )
```

```python
import jax
import jax.numpy as jnp
from jax import lax
from jax.experimental import pallas as pl
from jax.experimental.pallas import tpu as pltpu
from jax.sharding import PartitionSpec as P

F32 = jnp.float32
BF16 = jnp.bfloat16
MESH = pl.DeviceIdType.MESH

LEAF_RHO = (255 * 0.003515625) / (255 * 0.003515625 + 256 * 0.000390625) / 1.05
FACE_RHO = 1.0 / 1.05
LEAF_STEPS = 5
FACE_STEPS = 6


def split(x):
    high = x.astype(BF16)
    low = (x - high.astype(F32)).astype(BF16)
    return high, low


def dot(a, b):
    return jnp.dot(a, b, preferred_element_type=F32)


def mm_split(a, b):
    depth, width = b[0].shape
    if depth % 128:
        return dot(a[0], b[0]) + (dot(a[0], b[1]) + dot(a[1], b[0]))
    if width == 128 and depth == 128:
        wide = jnp.concatenate([b[0], b[1]], 1)
        out = dot(jnp.concatenate([a[0], a[1]], 1), jnp.concatenate([wide, wide], 0))
        return out[:, :128] + out[:, 128:]
    if width == 128:
        out = dot(a[0], jnp.concatenate([b[0], b[1]], 1))
        return out[:, :128] + (out[:, 128:] + dot(a[1], b[0]))
    return dot(jnp.concatenate([a[0], a[0], a[1]], 1), jnp.concatenate([b[0], b[1], b[0]], 0))


def mm(a, b):
    return mm_split(split(a), split(b))


def eye_mask(n):
    return lax.broadcasted_iota(jnp.int32, (n, n), 0) == lax.broadcasted_iota(jnp.int32, (n, n), 1)


def inverse_of(h, rho, steps):
    n = h.shape[0]
    eye = jnp.where(eye_mask(n), 1.0, 0.0).astype(F32)
    t = 1.0 / rho
    s, r = None, h
    for k in range(steps):
        square = 2.0 * t * t
        alpha = square / (square - 1.0)
        if k == steps - 1:
            s = alpha * (s + dot(s.astype(BF16), r.astype(BF16)))
        elif k == steps - 2:
            rs = split(r)
            p = mm_split(split(s), rs)
            r = alpha * dot(rs[0], rs[0]) - (alpha - 1.0) * eye
            s = alpha * (s + p)
        elif s is None:
            rs = split(r)
            s = alpha * (eye + r)
            r = alpha * mm_split(rs, rs) - (alpha - 1.0) * eye
        else:
            ss, rs = split(s), split(r)
            p = mm_split((jnp.concatenate([ss[0], rs[0]], 0), jnp.concatenate([ss[1], rs[1]], 0)), rs)
            s = alpha * (s + p[:n])
            r = alpha * p[n:] - (alpha - 1.0) * eye
        t = square - 1.0
    return s


def face_inverse(v, rho=FACE_RHO, steps=FACE_STEPS):
    n = v.shape[0]
    on = eye_mask(n)
    di = 1.0 / jnp.sum(jnp.where(on, v, 0.0), axis=1, keepdims=True)
    h = jnp.where(on, 0.0, -v * di)
    return inverse_of(h, rho, steps), di


def half_swap(x):
    return pltpu.roll(x, 64, 1)


def cat(*parts, axis=0):
    return jnp.concatenate(parts, axis)


def kernel(ci_h, cq_h, co_h, mg_h, src_h, top, out_in, out_b, ci, cq, co, mg, src, mloc, gloc, ut, tv, s1m, s1g, st2, r2, st3, r3, st4, r4, ur,
           dnst, dn2, uyi, dn1, uloc, x1b, load, send, recv, tvrecv):
    loads = [pltpu.make_async_copy(h, v, load.at[k]) for k, (h, v) in enumerate(((ci_h, ci), (cq_h, cq), (mg_h, mg), (co_h, co), (src_h, src)))]
    for copy in loads:
        copy.start()

    gx, gy = lax.axis_index("gx"), lax.axis_index("gy")
    lx, ly = gx % 4, gy % 4
    x0, y0 = gx - lx, gy - ly
    bx, by, cx, cy = lx % 2, ly % 2, lx // 2, ly // 2
    px, py = (bx + cx) % 2, (by + cy) % 2

    def at(i, j):
        return (x0 + i, y0 + j)

    barrier = pltpu.get_barrier_semaphore()
    for i in range(4):
        for j in range(4):
            if i or j:
                pl.semaphore_signal(barrier, 1, device_id=at((lx + i) % 4, (ly + j) % 4), device_id_type=MESH)

    def remote(k, source, target, device):
        return pltpu.make_async_remote_copy(src_ref=source, dst_ref=target, send_sem=send.at[k], recv_sem=recv.at[k],
                                            device_id=device, device_id_type=MESH)

    def rows(ref, start, count):
        return ref.at[pl.ds(start, count), :]

    mate = (gx, gy + 1 - 2 * by)
    pair = (gx + 1 - 2 * bx, gy)
    side_y = at(lx, 3 - ly)
    side_x = at(3 - lx, ly)

    on = eye_mask(256)
    loads[0].wait()
    a = ci[...]
    inner = jnp.where(on, 0.0, 0.5 * (a + a.T))
    loads[1].wait()
    loads[2].wait()
    q = cq[...]
    margin = mg[...]
    m_in = jnp.sum(jnp.where(on, jnp.broadcast_to(margin[:, :256], (256, 256)), 0.0), axis=1, keepdims=True)
    m_out = jnp.sum(jnp.where(on, jnp.broadcast_to(margin[:, 256:], (256, 256)), 0.0), axis=1, keepdims=True)
    d_in = (jnp.sum(inner, 1, keepdims=True) + jnp.sum(q, 1, keepdims=True)) * (1.0 + m_in)
    di = 1.0 / d_in

    qt = q.T
    loads[3].wait()
    o = co[...]
    outer = jnp.where(on, 0.0, 0.5 * (o + o.T))
    d_out = (jnp.sum(outer, 1, keepdims=True) + jnp.sum(qt, 1, keepdims=True)) * (1.0 + m_out)
    e_out = jnp.where(on, d_out, -outer)

    di0 = di[:128]
    s0 = inverse_of(inner[:128, :128] * di0, LEAF_RHO, LEAF_STEPS)
    first = mm(s0, cat(inner[:128, 128:], q[:128], axis=1) * di0)
    across, across_t = first[:, :128], inner[128:, :128]
    second = mm(across_t, first)

    pl.semaphore_wait(barrier, 15)
    on_x = 1 - lx // 2
    top_sends = []
    for k in range(4):
        dx = on_x * lx * 3 + (1 - on_x) * k
        dy = on_x * k + (1 - on_x) * (lx - 2) * 3
        away = (dx - lx) * (dx - lx) + (dy - ly) * (dy - ly) > 0
        piece = top.at[:, pl.ds((k // 2) * 128, 128)]
        slot = tv.at[lx // 2, pl.ds(pl.multiple_of(ly * 32, 32), 32), :]
        copy = pltpu.make_async_remote_copy(src_ref=piece, dst_ref=slot, send_sem=send.at[k], recv_sem=tvrecv.at[lx // 2, ly],
                                            device_id=at(dx, dy), device_id_type=MESH)
        here = pltpu.make_async_copy(piece, slot, load.at[5])
        top_sends.append((away, copy, here))

        @pl.when(away)
        def _():
            copy.start()

        @pl.when(jnp.logical_not(away))
        def _():
            here.start()

    s1, di1 = face_inverse(jnp.where(on[:128, :128], d_in[128:], 0.0) - inner[128:, 128:] - second[:, :128], LEAF_RHO, LEAF_STEPS)

    def leaf_solve(y0, rest):
        z1 = mm(s1, rest * di1)
        return cat(y0 + mm(across, z1), z1)

    zq = leaf_solve(first[:, 128:], q[128:] + second[:, 128:])
    m = e_out - mm(qt, zq)
    t0, t1 = m[:, :128], m[:, 128:]
    t0 = jnp.where(bx == 0, half_swap(t0), t0)
    t1 = jnp.where(by == 0, half_swap(t1), t1)
    places = [pl.multiple_of(p, 64) for p in (64 * (1 - bx), 64 * bx, 128 + 64 * (1 - by), 128 + 64 * by)]
    for k in range(4):
        mloc[pl.ds(places[k], 64), :] = cat(t0[64 * k : 64 * k + 64], t1[64 * k : 64 * k + 64], axis=1)

    up1 = [
        remote(4, rows(mloc, 128, 64), rows(s1m, 128, 64), mate),
        remote(5, rows(mloc, 0, 128), rows(s1m, 0, 128), mate),
        remote(6, rows(gloc, 0, 192), s1g, mate),
    ]
    down1 = [
        remote(7, rows(ur, 64, 64), rows(dn1, 0, 64), mate),
        remote(8, rows(ur, 192, 64), rows(dn1, 64, 64), mate),
        remote(9, uyi, rows(dn1, 128, 64), mate),
    ]
    left = lax.broadcasted_iota(jnp.int32, (64, 128), 1) < 64
    zero = jnp.zeros((64, 128), F32)

    @pl.when(py == 0)
    def _():
        up1[0].start()
        up1[1].start()

    def leaf_flux():
        loads[4].wait()
        y0 = mm(s0, src[:128, :] * di0)
        z = leaf_solve(y0, src[128:256, :] + mm(across_t, y0))
        g = src[256:, :] + mm(qt, z)
        for k in range(4):
            gloc[pl.ds(places[k], 64), :] = g[64 * k : 64 * k + 64]
        src[:256, :] = z
        ut[...] = jnp.zeros_like(ut)
        for away, _, here in top_sends:

            @pl.when(jnp.logical_not(away))
            def _():
                here.wait()

        for side in range(2):
            known = (1 - px) if side == 0 else (1 - py)

            @pl.when(known == 1)
            def _():
                origin = cx if side == 0 else 2 + cy
                for j in range(4):
                    mine = (lx - origin) * (lx - origin) + (ly - j) * (ly - j) > 0

                    @pl.when(mine)
                    def _():
                        piece = tv.at[side, pl.ds(j * 32, 32), :]
                        pltpu.make_async_remote_copy(src_ref=piece, dst_ref=piece, send_sem=send.at[0], recv_sem=tvrecv.at[side, j],
                                                     device_id=mate, device_id_type=MESH).wait_recv()

                flipped = tv[side].T
                b = by if side == 0 else bx
                ut[64 + 128 * side : 128 + 128 * side, :] = jnp.where(b == 0, flipped[:64], flipped[64:])

        gloc[...] = gloc[...] - mm(mloc[...], ut[...])

    @pl.when(py == 0)
    def _():
        leaf_flux()
        up1[2].start()
        for copy in down1:
            copy.wait_recv()
        uloc[0:192, :] = dn1[...]
        uloc[192:256, :] = zero
        for copy in up1:
            copy.wait_send()

    @pl.when(py == 1)
    def _():
        up1[0].wait_recv()
        v1 = mloc[128:192, 128:256] + s1m[128:192, 128:256]
        k1, d1 = face_inverse(v1[:, :64])
        up1[1].wait_recv()

        def left_of(x):
            return jnp.where(left, x, 0.0)

        def wide_root(k):
            x, y = mloc[k : k + 64, :128], mloc[k : k + 64, 128:]
            return cat(left_of(x), left_of(half_swap(x)), left_of(half_swap(y)), axis=1)

        def wide_mate(k):
            x = s1m[k : k + 64, :128]
            return cat(jnp.where(left, 0.0, half_swap(x)), jnp.where(left, 0.0, x), zero, axis=1)

        gt1 = wide_root(128) + wide_mate(128)
        g1 = cat(mloc[0:64, 128:256], s1m[0:64, 128:256], mloc[64:128, 128:256], s1m[64:128, 128:256], mloc[192:256, 128:256])[:, :64]
        base1 = cat(wide_root(0), wide_mate(0), wide_root(64), wide_mate(64), wide_root(192))
        x1r = mm(k1, gt1 * d1)
        m1 = base1 - mm(g1, x1r)

        def flux1():
            leaf_flux()
            up1[2].wait_recv()
            b1 = mm(k1, (gloc[128:192, :] + s1g[128:192, :]) * d1)
            x1b[...] = b1
            return cat(gloc[0:64, :], s1g[0:64, :], gloc[64:128, :], s1g[64:128, :], gloc[192:256, :]) - mm(g1, b1)

        up2 = [
            remote(10, rows(st2, 0, 128), rows(r2, 0, 128), pair),
            remote(11, rows(st2, 128, 128), rows(r2, 128, 128), pair),
            remote(12, rows(st2, 256, 192), rows(r2, 256, 192), pair),
        ]
        down2 = [remote(13, dnst, dn2, pair)]

        @pl.when(px == 0)
        def _():
            st2[0:128, :] = m1[0:128, :128]
            up2[0].start()
            st2[128:192, :] = m1[256:320, :128]
            st2[192:256, :] = half_swap(m1[256:320, 256:])
            up2[1].start()
            f1 = flux1()
            st2[256:384, :] = f1[0:128]
            st2[384:448, :] = f1[256:320]
            up2[2].start()
            down2[0].wait_recv()
            ur[0:128, :] = dn2[0:128, :]
            ur[128:256, :] = jnp.zeros((128, 128), F32)
            ur[256:320, :] = dn2[128:192, :]
            for copy in up2:
                copy.wait_send()

        @pl.when(px == 1)
        def _():
            f1 = flux1()
            up2[0].wait_recv()
            k2, d2 = face_inverse(m1[0:128, :128] + r2[0:128, :])
            up2[1].wait_recv()
            w0 = r2[128:192, :]
            gt2 = cat(m1[0:128, 128:256], m1[0:128, 256:] + cat(zero, w0).T, axis=1)
            x2r = mm(k2, gt2 * d2)

            up3 = [
                remote(14, rows(st3, 0, 128), rows(r3, 0, 128), side_y),
                remote(15, rows(st3, 128, 128), rows(r3, 128, 128), side_y),
                remote(16, rows(st3, 256, 128), rows(r3, 256, 128), side_y),
                remote(17, rows(st3, 384, 256), rows(r3, 384, 256), side_y),
            ]
            g2y = cat(m1[256:320, :128], w0)
            m2y = cat(m1[256:320, 128:], cat(zero, r2[192:256, :], axis=1)) - mm(g2y, x2r)
            st3[0:128, :] = m2y[:, 128:]
            up3[0].start()
            st3[128:256, :] = m2y[:, :128]
            up3[1].start()
            g2x = m1[128:256, :128]
            m2x = m1[128:256, 128:] - mm(g2x, x2r)
            st3[256:384, :] = m2x[:, :128]
            up3[2].start()
            up2[2].wait_recv()
            b2 = mm(k2, (f1[0:128] + r2[256:384, :]) * d2)
            f2y = cat(f1[256:320], r2[384:448, :]) - mm(g2y, b2)
            f2x = f1[128:256] - mm(g2x, b2)
            st3[384:512, :] = f2y
            st3[512:640, :] = f2x
            up3[3].start()
            up3[0].wait_recv()
            k3, d3 = face_inverse(m2y[:, 128:] + r3[0:128, :])
            up3[1].wait_recv()
            yx = r3[128:256, :]
            x3r = mm(k3, cat(m2y[:, :128], yx, axis=1) * d3)
            g3 = cat(m2x[:, 128:], yx.T)
            p3 = mm(g3, x3r)

            up4 = [
                remote(18, rows(st4, 0, 136), rows(r4, 0, 136), side_x),
                remote(19, rows(st4, 136, 128), rows(r4, 136, 128), side_x),
                remote(20, rows(st4, 264, 256), rows(r4, 264, 256), side_x),
            ]
            m00, m01 = m2x[:, :128] - p3[:128, :128], -p3[:128, 128:]
            st4[136:264, :] = m01
            up3[2].wait_recv()
            m11 = r3[256:384, :] - p3[128:, 128:]
            on128 = eye_mask(128)
            lower = lax.broadcasted_iota(jnp.int32, (128, 128), 0) >= lax.broadcasted_iota(jnp.int32, (128, 128), 1)
            st4[0:128, :] = jnp.where(lower, m00, m11)
            st4[128:136, :] = jnp.broadcast_to(jnp.sum(jnp.where(on128, m11, 0.0), axis=0, keepdims=True), (8, 128))
            up4[0].start()
            up4[1].start()
            up3[3].wait_recv()
            b3 = mm(k3, (f2y + r3[384:512, :]) * d3)
            f3 = cat(f2x, r3[512:640, :]) - mm(g3, b3)
            st4[264:520, :] = f3
            up4[2].start()
            back = mm(x2r[:, 128:], cat(x3r, b3, axis=1))
            near_map = cat(x3r[:, :128], x2r[:, :128] - back[:, :128])
            far_map = cat(x3r[:, 128:], -back[:, 128:256])
            down_free = cat(b3, b2 - back[:, 256:])
            up4[0].wait_recv()
            mix = r4[0:128, :]
            mix_t = mix.T
            k4, d4 = face_inverse(m00 + jnp.where(lower, mix, mix_t))
            up4[1].wait_recv()
            v01 = m01 + r4[136:264, :]
            v10 = v01.T
            x4 = mm(k4, v01 * d4)
            far_block = m11 + jnp.where(on128, jnp.broadcast_to(r4[128:129, :], (128, 128)), jnp.where(lower, mix_t, mix))
            k5, d5 = face_inverse(far_block - mm(v10, x4))
            x4t = x4.T
            far_map = far_map - mm(near_map, x4)
            up4[2].wait_recv()
            h4 = f3[:128] + r4[264:392, :]
            y4 = mm(k4, h4 * d4)
            u_far = mm(k5, (f3[128:] + r4[392:520, :] - mm(x4t, h4)) * d5)
            u_near = y4 - mm(x4, u_far)
            u_low = down_free - mm(near_map, y4) - mm(far_map, u_far)
            dnst[0:128, :] = u_low[128:]
            dnst[128:192, :] = u_low[64:128]
            down2[0].start()
            ur[0:128, :] = u_low[128:]
            ur[128:256, :] = u_near
            ur[256:320, :] = u_low[:64]
            for copy in up3 + up4 + down2:
                copy.wait_send()

        ur[320:384, :] = zero
        down1[0].start()
        down1[1].start()
        u_yi = x1b[...] - mm(x1r, ur[...])
        uyi[...] = u_yi
        down1[2].start()
        uloc[0:64, :] = ur[0:64, :]
        uloc[64:128, :] = ur[128:192, :]
        uloc[128:192, :] = u_yi
        uloc[192:256, :] = ur[256:320, :]
        for copy in down1:
            copy.wait_send()

    uloc[...] = uloc[...] + ut[...]
    u_b = cat(*[uloc[pl.ds(p, 64), :] for p in places])
    out_b[...] = u_b
    out_in[...] = src[:256, :] + mm(zq, u_b)
    for away, copy, _ in top_sends:

        @pl.when(away)
        def _():
            copy.wait_send()


def store(a, b, out_a, out_b, sem):
    copies = [pltpu.make_async_copy(x, y, sem.at[k]) for k, (x, y) in enumerate(((a, out_a), (b, out_b)))]
    for copy in copies:
        copy.start()
    for copy in copies:
        copy.wait()


def solution(mesh):
    def local(couple_inner, couple_cross, couple_outer, margin, sources, top_values):
        vmem = pl.BlockSpec(memory_space=pltpu.VMEM)
        anywhere = pl.BlockSpec(memory_space=pl.ANY)
        shapes = [(256, 256)] * 3 + [(1, 512), (512, 128), (256, 256), (256, 128), (256, 128), (2, 128, 128), (192, 256), (192, 128),
                  (448, 128), (448, 128), (640, 128), (640, 128), (640, 128), (640, 128), (384, 128), (192, 128), (192, 128), (64, 128),
                  (192, 128), (256, 128), (64, 128)]
        dma = pltpu.SemaphoreType.DMA
        interior, boundary = pl.pallas_call(
            kernel,
            out_shape=(pltpu.VMEM((256, 128), F32), pltpu.VMEM((256, 128), F32)),
            in_specs=[anywhere] * 6,
            out_specs=(vmem, vmem),
            scratch_shapes=[pltpu.VMEM(shape, F32) for shape in shapes] + [dma((6,)), dma((22,)), dma((22,)), dma((2, 4))],
            compiler_params=pltpu.CompilerParams(collective_id=0, has_side_effects=True),
        )(
            couple_inner.reshape(256, 256),
            couple_cross.reshape(256, 256),
            couple_outer.reshape(256, 256),
            margin.reshape(1, 512),
            sources.reshape(512, 128),
            top_values,
        )
        interior, boundary = pl.pallas_call(
            store,
            out_shape=(jax.ShapeDtypeStruct((256, 128), F32),) * 2,
            in_specs=[vmem, vmem],
            out_specs=(anywhere, anywhere),
            scratch_shapes=[dma((2,))],
        )(pltpu.with_memory_space_constraint(interior, pltpu.VMEM), pltpu.with_memory_space_constraint(boundary, pltpu.VMEM))
        return interior[None, None], boundary[None, None]

    spec = P("gx", "gy", None, None)
    return jax.shard_map(
        local,
        mesh=mesh,
        in_specs=(spec, spec, spec, P("gx", "gy", None), spec, P("gy", "gx")),
        out_specs=(spec, spec),
        check_vma=False,
    )
```

```python
import jax
import jax.numpy as jnp
from jax import lax
from jax.experimental import pallas as pl
from jax.experimental.pallas import tpu as pltpu
from jax.sharding import PartitionSpec as P

F32 = jnp.float32
BF16 = jnp.bfloat16
MESH = pl.DeviceIdType.MESH

LEAF_RHO = (255 * 0.003515625) / (255 * 0.003515625 + 256 * 0.000390625) / 1.05
FACE_RHO = 1.0 / 1.05
LEAF_STEPS = 5
FACE_STEPS = 6


def split(x):
    high = x.astype(BF16)
    low = (x - high.astype(F32)).astype(BF16)
    return high, low


def dot(a, b):
    return jnp.dot(a, b, preferred_element_type=F32)


def mm_split(a, b):
    depth, width = b[0].shape
    if depth % 128:
        return dot(a[0], b[0]) + (dot(a[0], b[1]) + dot(a[1], b[0]))
    if width == 128 and depth == 128:
        wide = jnp.concatenate([b[0], b[1]], 1)
        out = dot(jnp.concatenate([a[0], a[1]], 1), jnp.concatenate([wide, wide], 0))
        return out[:, :128] + out[:, 128:]
    if width == 128:
        out = dot(a[0], jnp.concatenate([b[0], b[1]], 1))
        return out[:, :128] + (out[:, 128:] + dot(a[1], b[0]))
    return dot(jnp.concatenate([a[0], a[0], a[1]], 1), jnp.concatenate([b[0], b[1], b[0]], 0))


def mm(a, b):
    return mm_split(split(a), split(b))


def eye_mask(n):
    return lax.broadcasted_iota(jnp.int32, (n, n), 0) == lax.broadcasted_iota(jnp.int32, (n, n), 1)


def inverse_of(h, rho, steps):
    n = h.shape[0]
    eye = jnp.where(eye_mask(n), 1.0, 0.0).astype(F32)
    t = 1.0 / rho
    s, r = None, h
    for k in range(steps):
        square = 2.0 * t * t
        alpha = square / (square - 1.0)
        if k == steps - 1:
            s = alpha * (s + dot(s.astype(BF16), r.astype(BF16)))
        elif k == steps - 2:
            rs = split(r)
            p = mm_split(split(s), rs)
            r = alpha * dot(rs[0], rs[0]) - (alpha - 1.0) * eye
            s = alpha * (s + p)
        elif s is None:
            rs = split(r)
            s = alpha * (eye + r)
            r = alpha * mm_split(rs, rs) - (alpha - 1.0) * eye
        else:
            ss, rs = split(s), split(r)
            p = mm_split((jnp.concatenate([rs[0], ss[0]], 0), jnp.concatenate([rs[1], ss[1]], 0)), rs)
            r = alpha * p[:n] - (alpha - 1.0) * eye
            s = alpha * (s + p[n:])
        t = square - 1.0
    return s


def face_inverse(v, rho=FACE_RHO, steps=FACE_STEPS):
    n = v.shape[0]
    on = eye_mask(n)
    di = 1.0 / jnp.sum(jnp.where(on, v, 0.0), axis=1, keepdims=True)
    h = jnp.where(on, 0.0, -v * di)
    return inverse_of(h, rho, steps), di


def half_swap(x):
    return pltpu.roll(x, 64, 1)


def cat(*parts, axis=0):
    return jnp.concatenate(parts, axis)


def kernel(ci_h, cq_h, co_h, mg_h, src_h, top, out_in, out_b, ci, cq, co, mg, src, mloc, gloc, ut, tv, s1m, s1g, st2, r2, st3, r3, st4, r4, ur,
           dnst, dn2, uyi, dn1, uloc, x1b, load, send, recv, tvrecv):
    loads = [pltpu.make_async_copy(h, v, load.at[k]) for k, (h, v) in enumerate(((ci_h, ci), (cq_h, cq), (mg_h, mg), (co_h, co), (src_h, src)))]
    for copy in loads:
        copy.start()

    gx, gy = lax.axis_index("gx"), lax.axis_index("gy")
    lx, ly = gx % 4, gy % 4
    x0, y0 = gx - lx, gy - ly
    bx, by, cx, cy = lx % 2, ly % 2, lx // 2, ly // 2
    px, py = (bx + cx) % 2, (by + cy) % 2

    def at(i, j):
        return (x0 + i, y0 + j)

    barrier = pltpu.get_barrier_semaphore()
    for i in range(4):
        for j in range(4):
            if i or j:
                pl.semaphore_signal(barrier, 1, device_id=at((lx + i) % 4, (ly + j) % 4), device_id_type=MESH)

    def remote(k, source, target, device):
        return pltpu.make_async_remote_copy(src_ref=source, dst_ref=target, send_sem=send.at[k], recv_sem=recv.at[k],
                                            device_id=device, device_id_type=MESH)

    def rows(ref, start, count):
        return ref.at[pl.ds(start, count), :]

    mate = (gx, gy + 1 - 2 * by)
    pair = (gx + 1 - 2 * bx, gy)
    side_y = at(lx, 3 - ly)
    side_x = at(3 - lx, ly)

    on = eye_mask(256)
    loads[0].wait()
    a = ci[...]
    inner = jnp.where(on, 0.0, 0.5 * (a + a.T))
    loads[1].wait()
    loads[2].wait()
    q = cq[...]
    margin = mg[...]
    m_in = jnp.sum(jnp.where(on, jnp.broadcast_to(margin[:, :256], (256, 256)), 0.0), axis=1, keepdims=True)
    m_out = jnp.sum(jnp.where(on, jnp.broadcast_to(margin[:, 256:], (256, 256)), 0.0), axis=1, keepdims=True)
    d_in = (jnp.sum(inner, 1, keepdims=True) + jnp.sum(q, 1, keepdims=True)) * (1.0 + m_in)
    di = 1.0 / d_in

    di0 = di[:128]
    s0 = inverse_of(inner[:128, :128] * di0, LEAF_RHO, LEAF_STEPS)
    first = mm(s0, cat(inner[:128, 128:], q[:128], axis=1) * di0)
    across, across_t = first[:, :128], inner[128:, :128]
    second = mm(across_t, first)

    pl.semaphore_wait(barrier, 15)
    on_x = 1 - lx // 2
    top_sends = []
    for k in range(4):
        dx = on_x * lx * 3 + (1 - on_x) * k
        dy = on_x * k + (1 - on_x) * (lx - 2) * 3
        away = (dx - lx) * (dx - lx) + (dy - ly) * (dy - ly) > 0
        piece = top.at[:, pl.ds((k // 2) * 128, 128)]
        slot = tv.at[lx // 2, pl.ds(pl.multiple_of(ly * 32, 32), 32), :]
        copy = pltpu.make_async_remote_copy(src_ref=piece, dst_ref=slot, send_sem=send.at[k], recv_sem=tvrecv.at[lx // 2, ly],
                                            device_id=at(dx, dy), device_id_type=MESH)
        here = pltpu.make_async_copy(piece, slot, load.at[5])
        top_sends.append((away, copy, here))

        @pl.when(away)
        def _():
            copy.start()

        @pl.when(jnp.logical_not(away))
        def _():
            here.start()

    qt = q.T
    loads[3].wait()
    o = co[...]
    outer = jnp.where(on, 0.0, 0.5 * (o + o.T))
    d_out = (jnp.sum(outer, 1, keepdims=True) + jnp.sum(qt, 1, keepdims=True)) * (1.0 + m_out)
    e_out = jnp.where(on, d_out, -outer)
    s1, di1 = face_inverse(jnp.where(on[:128, :128], d_in[128:], 0.0) - inner[128:, 128:] - second[:, :128], LEAF_RHO, LEAF_STEPS)

    def leaf_solve(y0, rest):
        z1 = mm(s1, rest * di1)
        return cat(y0 + mm(across, z1), z1)

    zq = leaf_solve(first[:, 128:], q[128:] + second[:, 128:])
    m = e_out - mm(qt, zq)
    t0, t1 = m[:, :128], m[:, 128:]
    t0 = jnp.where(bx == 0, half_swap(t0), t0)
    t1 = jnp.where(by == 0, half_swap(t1), t1)
    places = [pl.multiple_of(p, 64) for p in (64 * (1 - bx), 64 * bx, 128 + 64 * (1 - by), 128 + 64 * by)]
    for k in range(4):
        mloc[pl.ds(places[k], 64), :] = cat(t0[64 * k : 64 * k + 64], t1[64 * k : 64 * k + 64], axis=1)

    up1 = [
        remote(4, rows(mloc, 128, 64), rows(s1m, 128, 64), mate),
        remote(5, rows(mloc, 0, 128), rows(s1m, 0, 128), mate),
        remote(6, rows(gloc, 0, 192), s1g, mate),
    ]
    down1 = [
        remote(7, rows(ur, 64, 64), rows(dn1, 0, 64), mate),
        remote(8, rows(ur, 192, 64), rows(dn1, 64, 64), mate),
        remote(9, uyi, rows(dn1, 128, 64), mate),
    ]
    left = lax.broadcasted_iota(jnp.int32, (64, 128), 1) < 64
    zero = jnp.zeros((64, 128), F32)

    @pl.when(py == 0)
    def _():
        up1[0].start()
        up1[1].start()

    def leaf_flux():
        loads[4].wait()
        y0 = mm(s0, src[:128, :] * di0)
        z = leaf_solve(y0, src[128:256, :] + mm(across_t, y0))
        g = src[256:, :] + mm(qt, z)
        for k in range(4):
            gloc[pl.ds(places[k], 64), :] = g[64 * k : 64 * k + 64]
        src[:256, :] = z
        ut[...] = jnp.zeros_like(ut)
        for away, _, here in top_sends:

            @pl.when(jnp.logical_not(away))
            def _():
                here.wait()

        for side in range(2):
            known = (1 - px) if side == 0 else (1 - py)

            @pl.when(known == 1)
            def _():
                origin = cx if side == 0 else 2 + cy
                for j in range(4):
                    mine = (lx - origin) * (lx - origin) + (ly - j) * (ly - j) > 0

                    @pl.when(mine)
                    def _():
                        piece = tv.at[side, pl.ds(j * 32, 32), :]
                        pltpu.make_async_remote_copy(src_ref=piece, dst_ref=piece, send_sem=send.at[0], recv_sem=tvrecv.at[side, j],
                                                     device_id=mate, device_id_type=MESH).wait_recv()

                flipped = tv[side].T
                b = by if side == 0 else bx
                ut[64 + 128 * side : 128 + 128 * side, :] = jnp.where(b == 0, flipped[:64], flipped[64:])

        gloc[...] = gloc[...] - mm(mloc[...], ut[...])

    @pl.when(py == 0)
    def _():
        leaf_flux()
        up1[2].start()
        for copy in down1:
            copy.wait_recv()
        uloc[0:192, :] = dn1[...]
        uloc[192:256, :] = zero
        for copy in up1:
            copy.wait_send()

    @pl.when(py == 1)
    def _():
        up1[0].wait_recv()
        v1 = mloc[128:192, 128:256] + s1m[128:192, 128:256]
        k1, d1 = face_inverse(v1[:, :64])
        up1[1].wait_recv()

        def left_of(x):
            return jnp.where(left, x, 0.0)

        def wide_root(k):
            x, y = mloc[k : k + 64, :128], mloc[k : k + 64, 128:]
            return cat(left_of(x), left_of(half_swap(x)), left_of(half_swap(y)), axis=1)

        def wide_mate(k):
            x = s1m[k : k + 64, :128]
            return cat(jnp.where(left, 0.0, half_swap(x)), jnp.where(left, 0.0, x), zero, axis=1)

        gt1 = (wide_root(128) + wide_mate(128)) * d1
        g1 = cat(mloc[0:64, 128:256], s1m[0:64, 128:256], mloc[64:128, 128:256], s1m[64:128, 128:256], mloc[192:256, 128:256])[:, :64]
        x1a = mm(k1, gt1[:, :128])
        shared1 = cat(wide_root(0)[:, :128], wide_mate(0)[:, :128]) - mm(g1[:128], x1a)
        up2 = [
            remote(10, rows(st2, 0, 128), rows(r2, 0, 128), pair),
            remote(11, rows(st2, 128, 128), rows(r2, 128, 128), pair),
            remote(12, rows(st2, 256, 192), rows(r2, 256, 192), pair),
        ]

        @pl.when(px == 0)
        def _():
            st2[0:128, :] = shared1
            up2[0].start()

        x1b_ = mm(k1, gt1[:, 128:])
        x1r = cat(x1a, x1b_, axis=1)
        p1l, p1r = mm(g1[128:], x1a), mm(g1, x1b_)
        m1 = cat(
            cat(shared1, cat(wide_root(64)[:, :128], wide_mate(64)[:, :128], wide_root(192)[:, :128]) - p1l),
            cat(*[w[:, 128:] for w in (wide_root(0), wide_mate(0), wide_root(64), wide_mate(64), wide_root(192))]) - p1r,
            axis=1)

        def flux1():
            leaf_flux()
            up1[2].wait_recv()
            b1 = mm(k1, (gloc[128:192, :] + s1g[128:192, :]) * d1)
            x1b[...] = b1
            return cat(gloc[0:64, :], s1g[0:64, :], gloc[64:128, :], s1g[64:128, :], gloc[192:256, :]) - mm(g1, b1)

        down2 = [remote(13, dnst, dn2, pair)]

        @pl.when(px == 0)
        def _():
            st2[128:192, :] = m1[256:320, :128]
            st2[192:256, :] = half_swap(m1[256:320, 256:])
            up2[1].start()
            f1 = flux1()
            st2[256:384, :] = f1[0:128]
            st2[384:448, :] = f1[256:320]
            up2[2].start()
            down2[0].wait_recv()
            ur[0:128, :] = dn2[0:128, :]
            ur[128:256, :] = jnp.zeros((128, 128), F32)
            ur[256:320, :] = dn2[128:192, :]
            for copy in up2:
                copy.wait_send()

        @pl.when(px == 1)
        def _():
            f1 = flux1()
            up2[0].wait_recv()
            k2, d2 = face_inverse(m1[0:128, :128] + r2[0:128, :])
            up2[1].wait_recv()
            w0 = r2[128:192, :]
            gt2 = cat(m1[0:128, 128:256], m1[0:128, 256:] + cat(zero, w0).T, axis=1)
            x2y = mm(k2, gt2[:, 128:] * d2)

            up3 = [
                remote(14, rows(st3, 0, 128), rows(r3, 0, 128), side_y),
                remote(15, rows(st3, 128, 128), rows(r3, 128, 128), side_y),
                remote(16, rows(st3, 256, 128), rows(r3, 256, 128), side_y),
                remote(17, rows(st3, 384, 256), rows(r3, 384, 256), side_y),
            ]
            g2y = cat(m1[256:320, :128], w0)
            base2y = cat(m1[256:320, 128:], cat(zero, r2[192:256, :], axis=1))
            m2yy = base2y[:, 128:] - mm(g2y, x2y)
            st3[0:128, :] = m2yy
            up3[0].start()
            x2x = mm(k2, gt2[:, :128] * d2)
            x2r = cat(x2x, x2y, axis=1)
            m2yx = base2y[:, :128] - mm(g2y, x2x)
            st3[128:256, :] = m2yx
            up3[1].start()
            g2x = m1[128:256, :128]
            m2x = m1[128:256, 128:] - mm(g2x, x2r)
            st3[256:384, :] = m2x[:, :128]
            up3[2].start()
            up2[2].wait_recv()
            b2 = mm(k2, (f1[0:128] + r2[256:384, :]) * d2)
            f2y = cat(f1[256:320], r2[384:448, :]) - mm(g2y, b2)
            f2x = f1[128:256] - mm(g2x, b2)
            st3[384:512, :] = f2y
            st3[512:640, :] = f2x
            up3[3].start()
            up3[0].wait_recv()
            k3, d3 = face_inverse(m2yy + r3[0:128, :])
            up3[1].wait_recv()
            yx = r3[128:256, :]
            x3r = mm(k3, cat(m2yx, yx, axis=1) * d3)
            g3 = cat(m2x[:, 128:], yx.T)
            p3 = mm(g3, x3r)

            up4 = [
                remote(18, rows(st4, 0, 136), rows(r4, 0, 136), side_x),
                remote(19, rows(st4, 136, 128), rows(r4, 136, 128), side_x),
                remote(20, rows(st4, 264, 256), rows(r4, 264, 256), side_x),
            ]
            m00, m01 = m2x[:, :128] - p3[:128, :128], -p3[:128, 128:]
            st4[136:264, :] = m01
            up3[2].wait_recv()
            m11 = r3[256:384, :] - p3[128:, 128:]
            on128 = eye_mask(128)
            lower = lax.broadcasted_iota(jnp.int32, (128, 128), 0) >= lax.broadcasted_iota(jnp.int32, (128, 128), 1)
            st4[0:128, :] = jnp.where(lower, m00, m11)
            st4[128:136, :] = jnp.broadcast_to(jnp.sum(jnp.where(on128, m11, 0.0), axis=0, keepdims=True), (8, 128))
            up4[0].start()
            up4[1].start()
            up3[3].wait_recv()
            b3 = mm(k3, (f2y + r3[384:512, :]) * d3)
            f3 = cat(f2x, r3[512:640, :]) - mm(g3, b3)
            st4[264:520, :] = f3
            up4[2].start()
            back = mm(x2r[:, 128:], cat(x3r, b3, axis=1))
            near_map = cat(x3r[:, :128], x2r[:, :128] - back[:, :128])
            far_map = cat(x3r[:, 128:], -back[:, 128:256])
            down_free = cat(b3, b2 - back[:, 256:])
            up4[0].wait_recv()
            mix = r4[0:128, :]
            mix_t = mix.T
            k4, d4 = face_inverse(m00 + jnp.where(lower, mix, mix_t))
            up4[1].wait_recv()
            v01 = m01 + r4[136:264, :]
            v10 = v01.T
            x4 = mm(k4, v01 * d4)
            far_block = m11 + jnp.where(on128, jnp.broadcast_to(r4[128:129, :], (128, 128)), jnp.where(lower, mix_t, mix))
            k5, d5 = face_inverse(far_block - mm(v10, x4))
            x4t = x4.T
            far_map = far_map - mm(near_map, x4)
            up4[2].wait_recv()
            h4 = f3[:128] + r4[264:392, :]
            y4 = mm(k4, h4 * d4)
            u_far = mm(k5, (f3[128:] + r4[392:520, :] - mm(x4t, h4)) * d5)
            u_near = y4 - mm(x4, u_far)
            u_low = down_free - mm(near_map, y4) - mm(far_map, u_far)
            dnst[0:128, :] = u_low[128:]
            dnst[128:192, :] = u_low[64:128]
            down2[0].start()
            ur[0:128, :] = u_low[128:]
            ur[128:256, :] = u_near
            ur[256:320, :] = u_low[:64]
            for copy in up3 + up4 + down2:
                copy.wait_send()

        ur[320:384, :] = zero
        down1[0].start()
        down1[1].start()
        u_yi = x1b[...] - mm(x1r, ur[...])
        uyi[...] = u_yi
        down1[2].start()
        uloc[0:64, :] = ur[0:64, :]
        uloc[64:128, :] = ur[128:192, :]
        uloc[128:192, :] = u_yi
        uloc[192:256, :] = ur[256:320, :]
        for copy in down1:
            copy.wait_send()

    uloc[...] = uloc[...] + ut[...]
    u_b = cat(*[uloc[pl.ds(p, 64), :] for p in places])
    out_b[...] = u_b
    out_in[...] = src[:256, :] + mm(zq, u_b)
    for away, copy, _ in top_sends:

        @pl.when(away)
        def _():
            copy.wait_send()


def store(a, b, out_a, out_b, sem):
    copies = [pltpu.make_async_copy(x, y, sem.at[k]) for k, (x, y) in enumerate(((a, out_a), (b, out_b)))]
    for copy in copies:
        copy.start()
    for copy in copies:
        copy.wait()


def solution(mesh):
    def local(couple_inner, couple_cross, couple_outer, margin, sources, top_values):
        vmem = pl.BlockSpec(memory_space=pltpu.VMEM)
        anywhere = pl.BlockSpec(memory_space=pl.ANY)
        shapes = [(256, 256)] * 3 + [(1, 512), (512, 128), (256, 256), (256, 128), (256, 128), (2, 128, 128), (192, 256), (192, 128),
                  (448, 128), (448, 128), (640, 128), (640, 128), (640, 128), (640, 128), (384, 128), (192, 128), (192, 128), (64, 128),
                  (192, 128), (256, 128), (64, 128)]
        dma = pltpu.SemaphoreType.DMA
        interior, boundary = pl.pallas_call(
            kernel,
            out_shape=(pltpu.VMEM((256, 128), F32), pltpu.VMEM((256, 128), F32)),
            in_specs=[anywhere] * 6,
            out_specs=(vmem, vmem),
            scratch_shapes=[pltpu.VMEM(shape, F32) for shape in shapes] + [dma((6,)), dma((22,)), dma((22,)), dma((2, 4))],
            compiler_params=pltpu.CompilerParams(collective_id=0, has_side_effects=True),
        )(
            couple_inner.reshape(256, 256),
            couple_cross.reshape(256, 256),
            couple_outer.reshape(256, 256),
            margin.reshape(1, 512),
            sources.reshape(512, 128),
            top_values,
        )
        interior, boundary = pl.pallas_call(
            store,
            out_shape=(jax.ShapeDtypeStruct((256, 128), F32),) * 2,
            in_specs=[vmem, vmem],
            out_specs=(anywhere, anywhere),
            scratch_shapes=[dma((2,))],
        )(pltpu.with_memory_space_constraint(interior, pltpu.VMEM), pltpu.with_memory_space_constraint(boundary, pltpu.VMEM))
        return interior[None, None], boundary[None, None]

    spec = P("gx", "gy", None, None)
    return jax.shard_map(
        local,
        mesh=mesh,
        in_specs=(spec, spec, spec, P("gx", "gy", None), spec, P("gy", "gx")),
        out_specs=(spec, spec),
        check_vma=False,
    )
```

```python
import jax
import jax.numpy as jnp
from jax import lax
from jax.experimental import pallas as pl
from jax.experimental.pallas import tpu as pltpu
from jax.sharding import PartitionSpec as P

F32 = jnp.float32
BF16 = jnp.bfloat16
MESH = pl.DeviceIdType.MESH

LEAF_RHO = (255 * 0.003515625) / (255 * 0.003515625 + 256 * 0.000390625) / 1.05
FACE_RHO = 1.0 / 1.05
FIRST_RHO = (64 * 9) / (64 * 9 + 192) / 1.05
SECOND_RHO = (64 * 9) / (64 * 9 + 128) / 1.05
THIRD_RHO = (64 * 9) / (64 * 9 + 64) / 1.05
NEAR_STEPS = 5
LEAF_STEPS = 5
FACE_STEPS = 6


def split(x):
    high = x.astype(BF16)
    low = (x - high.astype(F32)).astype(BF16)
    return high, low


def dot(a, b):
    return jnp.dot(a, b, preferred_element_type=F32)


def mm_split(a, b):
    depth, width = b[0].shape
    if depth % 128:
        return dot(a[0], b[0]) + (dot(a[0], b[1]) + dot(a[1], b[0]))
    if width == 128 and depth == 128:
        wide = jnp.concatenate([b[0], b[1]], 1)
        out = dot(jnp.concatenate([a[0], a[1]], 1), jnp.concatenate([wide, wide], 0))
        return out[:, :128] + out[:, 128:]
    if width == 128:
        out = dot(a[0], jnp.concatenate([b[0], b[1]], 1))
        return out[:, :128] + (out[:, 128:] + dot(a[1], b[0]))
    return dot(jnp.concatenate([a[0], a[0], a[1]], 1), jnp.concatenate([b[0], b[1], b[0]], 0))


def mm(a, b):
    return mm_split(split(a), split(b))


def eye_mask(n):
    return lax.broadcasted_iota(jnp.int32, (n, n), 0) == lax.broadcasted_iota(jnp.int32, (n, n), 1)


def inverse_of(h, rho, steps):
    n = h.shape[0]
    eye = jnp.where(eye_mask(n), 1.0, 0.0).astype(F32)
    t = 1.0 / rho
    s, r = None, h
    for k in range(steps):
        square = 2.0 * t * t
        alpha = square / (square - 1.0)
        if k == steps - 1:
            s = alpha * (s + dot(s.astype(BF16), r.astype(BF16)))
        elif k == steps - 2:
            rs = split(r)
            p = mm_split(split(s), rs)
            r = alpha * dot(rs[0], rs[0]) - (alpha - 1.0) * eye
            s = alpha * (s + p)
        elif s is None:
            rs = split(r)
            s = alpha * (eye + r)
            r = alpha * mm_split(rs, rs) - (alpha - 1.0) * eye
        else:
            ss, rs = split(s), split(r)
            p = mm_split((jnp.concatenate([rs[0], ss[0]], 0), jnp.concatenate([rs[1], ss[1]], 0)), rs)
            r = alpha * p[:n] - (alpha - 1.0) * eye
            s = alpha * (s + p[n:])
        t = square - 1.0
    return s


def face_inverse(v, rho=FACE_RHO, steps=FACE_STEPS):
    n = v.shape[0]
    on = eye_mask(n)
    di = 1.0 / jnp.sum(jnp.where(on, v, 0.0), axis=1, keepdims=True)
    h = jnp.where(on, 0.0, -v * di)
    return inverse_of(h, rho, steps), di


def half_swap(x):
    return pltpu.roll(x, 64, 1)


def cat(*parts, axis=0):
    return jnp.concatenate(parts, axis)


def kernel(ci_h, cq_h, co_h, mg_h, src_h, top, out_in, out_b, ci, cq, co, mg, src, mloc, gloc, ut, tv, s1m, s1g, st2, r2, st3, r3, st4, r4, ur,
           dnst, dn2, uyi, dn1, uloc, x1b, load, send, recv, tvrecv):
    loads = [pltpu.make_async_copy(h, v, load.at[k]) for k, (h, v) in enumerate(((ci_h, ci), (cq_h, cq), (mg_h, mg), (co_h, co), (src_h, src)))]
    for copy in loads:
        copy.start()

    gx, gy = lax.axis_index("gx"), lax.axis_index("gy")
    lx, ly = gx % 4, gy % 4
    x0, y0 = gx - lx, gy - ly
    bx, by, cx, cy = lx % 2, ly % 2, lx // 2, ly // 2
    px, py = (bx + cx) % 2, (by + cy) % 2

    def at(i, j):
        return (x0 + i, y0 + j)

    barrier = pltpu.get_barrier_semaphore()
    for i in range(4):
        for j in range(4):
            if i or j:
                pl.semaphore_signal(barrier, 1, device_id=at((lx + i) % 4, (ly + j) % 4), device_id_type=MESH)

    def remote(k, source, target, device):
        return pltpu.make_async_remote_copy(src_ref=source, dst_ref=target, send_sem=send.at[k], recv_sem=recv.at[k],
                                            device_id=device, device_id_type=MESH)

    def rows(ref, start, count):
        return ref.at[pl.ds(start, count), :]

    mate = (gx, gy + 1 - 2 * by)
    pair = (gx + 1 - 2 * bx, gy)
    cross = (gx + 1 - 2 * bx, gy + 1 - 2 * by)
    side_y = at(lx, 3 - ly)
    side_x = at(3 - lx, ly)

    on = eye_mask(256)
    loads[0].wait()
    a = ci[...]
    inner = jnp.where(on, 0.0, 0.5 * (a + a.T))
    loads[1].wait()
    loads[2].wait()
    q = cq[...]
    margin = mg[...]
    m_in = jnp.sum(jnp.where(on, jnp.broadcast_to(margin[:, :256], (256, 256)), 0.0), axis=1, keepdims=True)
    m_out = jnp.sum(jnp.where(on, jnp.broadcast_to(margin[:, 256:], (256, 256)), 0.0), axis=1, keepdims=True)
    d_in = (jnp.sum(inner, 1, keepdims=True) + jnp.sum(q, 1, keepdims=True)) * (1.0 + m_in)
    di = 1.0 / d_in

    di0 = di[:128]
    s0 = inverse_of(inner[:128, :128] * di0, LEAF_RHO, LEAF_STEPS)
    first = mm(s0, cat(inner[:128, 128:], q[:128], axis=1) * di0)
    across, across_t = first[:, :128], inner[128:, :128]
    second = mm(across_t, first)

    pl.semaphore_wait(barrier, 15)
    on_x = 1 - lx // 2
    top_sends = []
    for k in range(4):
        dx = on_x * lx * 3 + (1 - on_x) * k
        dy = on_x * k + (1 - on_x) * (lx - 2) * 3
        away = (dx - lx) * (dx - lx) + (dy - ly) * (dy - ly) > 0
        piece = top.at[:, pl.ds((k // 2) * 128, 128)]
        slot = tv.at[lx // 2, pl.ds(pl.multiple_of(ly * 32, 32), 32), :]
        copy = pltpu.make_async_remote_copy(src_ref=piece, dst_ref=slot, send_sem=send.at[k], recv_sem=tvrecv.at[lx // 2, ly],
                                            device_id=at(dx, dy), device_id_type=MESH)
        here = pltpu.make_async_copy(piece, slot, load.at[5])
        top_sends.append((away, copy, here))

        @pl.when(away)
        def _():
            copy.start()

        @pl.when(jnp.logical_not(away))
        def _():
            here.start()

    qt = q.T
    loads[3].wait()
    o = co[...]
    outer = jnp.where(on, 0.0, 0.5 * (o + o.T))
    d_out = (jnp.sum(outer, 1, keepdims=True) + jnp.sum(qt, 1, keepdims=True)) * (1.0 + m_out)
    e_out = jnp.where(on, d_out, -outer)
    s1, di1 = face_inverse(jnp.where(on[:128, :128], d_in[128:], 0.0) - inner[128:, 128:] - second[:, :128], LEAF_RHO, LEAF_STEPS)

    def leaf_solve(y0, rest):
        z1 = mm(s1, rest * di1)
        return cat(y0 + mm(across, z1), z1)

    zq = leaf_solve(first[:, 128:], q[128:] + second[:, 128:])
    m = e_out - mm(qt, zq)
    t0, t1 = m[:, :128], m[:, 128:]
    t0 = jnp.where(bx == 0, half_swap(t0), t0)
    t1 = jnp.where(by == 0, half_swap(t1), t1)
    places = [pl.multiple_of(p, 64) for p in (64 * (1 - bx), 64 * bx, 128 + 64 * (1 - by), 128 + 64 * by)]
    for k in range(4):
        mloc[pl.ds(places[k], 64), :] = cat(t0[64 * k : 64 * k + 64], t1[64 * k : 64 * k + 64], axis=1)

    up1 = [
        remote(4, rows(mloc, 128, 64), rows(s1m, 128, 64), mate),
        remote(5, rows(mloc, 0, 128), rows(s1m, 0, 128), mate),
        remote(6, rows(gloc, 0, 192), s1g, mate),
    ]
    down1 = [
        remote(7, rows(ur, 64, 64), rows(dn1, 0, 64), mate),
        remote(8, rows(ur, 192, 64), rows(dn1, 64, 64), mate),
        remote(9, uyi, rows(dn1, 128, 64), mate),
    ]
    down2 = [
        remote(13, rows(dnst, 0, 64), uyi, pair),
        remote(22, rows(dnst, 64, 64), rows(dn1, 0, 64), cross),
        remote(23, rows(dnst, 128, 128), dn2, pair),
    ]
    left = lax.broadcasted_iota(jnp.int32, (64, 128), 1) < 64
    zero = jnp.zeros((64, 128), F32)

    @pl.when(py == 0)
    def _():
        up1[0].start()
        up1[1].start()

    def leaf_flux():
        loads[4].wait()
        y0 = mm(s0, src[:128, :] * di0)
        z = leaf_solve(y0, src[128:256, :] + mm(across_t, y0))
        g = src[256:, :] + mm(qt, z)
        for k in range(4):
            gloc[pl.ds(places[k], 64), :] = g[64 * k : 64 * k + 64]
        src[:256, :] = z
        ut[...] = jnp.zeros_like(ut)
        for away, _, here in top_sends:

            @pl.when(jnp.logical_not(away))
            def _():
                here.wait()

        for side in range(2):
            known = (1 - px) if side == 0 else (1 - py)

            @pl.when(known == 1)
            def _():
                origin = cx if side == 0 else 2 + cy
                for j in range(4):
                    mine = (lx - origin) * (lx - origin) + (ly - j) * (ly - j) > 0

                    @pl.when(mine)
                    def _():
                        piece = tv.at[side, pl.ds(j * 32, 32), :]
                        pltpu.make_async_remote_copy(src_ref=piece, dst_ref=piece, send_sem=send.at[0], recv_sem=tvrecv.at[side, j],
                                                     device_id=mate, device_id_type=MESH).wait_recv()

                flipped = tv[side].T
                b = by if side == 0 else bx
                ut[64 + 128 * side : 128 + 128 * side, :] = jnp.where(b == 0, flipped[:64], flipped[64:])

        gloc[...] = gloc[...] - mm(mloc[...], ut[...])

    @pl.when(py == 0)
    def _():
        leaf_flux()
        up1[2].start()

        @pl.when(px == 1)
        def _():
            down1[0].wait_recv()
            down1[1].wait_recv()
            uloc[64:128, :] = dn1[64:128, :]

        @pl.when(px == 0)
        def _():
            down2[1].wait_recv()
            uloc[64:128, :] = zero

        down1[2].wait_recv()
        uloc[0:64, :] = dn1[0:64, :]
        uloc[128:192, :] = dn1[128:192, :]
        uloc[192:256, :] = zero
        for copy in up1:
            copy.wait_send()

    @pl.when(py == 1)
    def _():
        up1[0].wait_recv()
        v1 = mloc[128:192, 128:256] + s1m[128:192, 128:256]
        k1, d1 = face_inverse(v1[:, :64], FIRST_RHO, NEAR_STEPS)
        up1[1].wait_recv()

        def left_of(x):
            return jnp.where(left, x, 0.0)

        def wide_root(k):
            x, y = mloc[k : k + 64, :128], mloc[k : k + 64, 128:]
            return cat(left_of(x), left_of(half_swap(x)), left_of(half_swap(y)), axis=1)

        def wide_mate(k):
            x = s1m[k : k + 64, :128]
            return cat(jnp.where(left, 0.0, half_swap(x)), jnp.where(left, 0.0, x), zero, axis=1)

        gt1 = (wide_root(128) + wide_mate(128)) * d1
        g1 = cat(mloc[0:64, 128:256], s1m[0:64, 128:256], mloc[64:128, 128:256], s1m[64:128, 128:256], mloc[192:256, 128:256])[:, :64]
        x1a = mm(k1, gt1[:, :128])
        shared1 = cat(wide_root(0)[:, :128], wide_mate(0)[:, :128]) - mm(g1[:128], x1a)
        up2 = [
            remote(10, rows(st2, 0, 128), rows(r2, 0, 128), pair),
            remote(11, rows(st2, 128, 128), rows(r2, 128, 128), pair),
            remote(12, rows(st2, 256, 192), rows(r2, 256, 192), pair),
            remote(21, rows(st2, 448, 192), rows(r2, 448, 192), pair),
        ]

        @pl.when(px == 0)
        def _():
            st2[0:128, :] = shared1
            up2[0].start()

        x1b_ = mm(k1, gt1[:, 128:])
        x1r = cat(x1a, x1b_, axis=1)
        p1l, p1r = mm(g1[128:], x1a), mm(g1, x1b_)
        m1 = cat(
            cat(shared1, cat(wide_root(64)[:, :128], wide_mate(64)[:, :128], wide_root(192)[:, :128]) - p1l),
            cat(*[w[:, 128:] for w in (wide_root(0), wide_mate(0), wide_root(64), wide_mate(64), wide_root(192))]) - p1r,
            axis=1)

        def flux1():
            leaf_flux()
            up1[2].wait_recv()
            b1 = mm(k1, (gloc[128:192, :] + s1g[128:192, :]) * d1)
            x1b[...] = b1
            return cat(gloc[0:64, :], s1g[0:64, :], gloc[64:128, :], s1g[64:128, :], gloc[192:256, :]) - mm(g1, b1)

        @pl.when(px == 0)
        def _():
            st2[128:192, :] = m1[256:320, :128]
            st2[192:256, :] = half_swap(m1[256:320, 256:])
            up2[1].start()
            f1 = flux1()
            st2[256:384, :] = f1[0:128]
            st2[384:448, :] = f1[256:320]
            up2[2].start()
            st2[448:512, :] = x1a
            st2[512:576, :] = half_swap(x1r[:, 256:])
            st2[576:640, :] = x1b[...]
            up2[3].start()
            down2[0].wait_recv()
            down1[2].start()
            down2[2].wait_recv()
            uloc[0:64, :] = dn2[0:64, :]
            uloc[64:128, :] = zero
            uloc[128:192, :] = uyi[...]
            uloc[192:256, :] = dn2[64:128, :]
            down1[2].wait_send()
            for copy in up2:
                copy.wait_send()

        @pl.when(px == 1)
        def _():
            f1 = flux1()
            up2[0].wait_recv()
            k2, d2 = face_inverse(m1[0:128, :128] + r2[0:128, :], SECOND_RHO, NEAR_STEPS)
            up2[1].wait_recv()
            w0 = r2[128:192, :]
            gt2 = cat(m1[0:128, 128:256], m1[0:128, 256:] + cat(zero, w0).T, axis=1)
            x2y = mm(k2, gt2[:, 128:] * d2)

            up3 = [
                remote(14, rows(st3, 0, 128), rows(r3, 0, 128), side_y),
                remote(15, rows(st3, 128, 128), rows(r3, 128, 128), side_y),
                remote(16, rows(st3, 256, 128), rows(r3, 256, 128), side_y),
                remote(17, rows(st3, 384, 256), rows(r3, 384, 256), side_y),
            ]
            g2y = cat(m1[256:320, :128], w0)
            base2y = cat(m1[256:320, 128:], cat(zero, r2[192:256, :], axis=1))
            m2yy = base2y[:, 128:] - mm(g2y, x2y)
            st3[0:128, :] = m2yy
            up3[0].start()
            x2x = mm(k2, gt2[:, :128] * d2)
            x2r = cat(x2x, x2y, axis=1)
            m2yx = base2y[:, :128] - mm(g2y, x2x)
            st3[128:256, :] = m2yx
            up3[1].start()
            g2x = m1[128:256, :128]
            m2x = m1[128:256, 128:] - mm(g2x, x2r)
            st3[256:384, :] = m2x[:, :128]
            up3[2].start()
            up2[2].wait_recv()
            b2 = mm(k2, (f1[0:128] + r2[256:384, :]) * d2)
            f2y = cat(f1[256:320], r2[384:448, :]) - mm(g2y, b2)
            f2x = f1[128:256] - mm(g2x, b2)
            st3[384:512, :] = f2y
            st3[512:640, :] = f2x
            up3[3].start()
            up3[0].wait_recv()
            k3, d3 = face_inverse(m2yy + r3[0:128, :], THIRD_RHO, NEAR_STEPS)
            up3[1].wait_recv()
            yx = r3[128:256, :]
            x3r = mm(k3, cat(m2yx, yx, axis=1) * d3)
            g3 = cat(m2x[:, 128:], yx.T)
            p3 = mm(g3, x3r)

            up4 = [
                remote(18, rows(st4, 0, 136), rows(r4, 0, 136), side_x),
                remote(19, rows(st4, 136, 128), rows(r4, 136, 128), side_x),
                remote(20, rows(st4, 264, 256), rows(r4, 264, 256), side_x),
            ]
            m00, m01 = m2x[:, :128] - p3[:128, :128], -p3[:128, 128:]
            st4[136:264, :] = m01
            up3[2].wait_recv()
            m11 = r3[256:384, :] - p3[128:, 128:]
            on128 = eye_mask(128)
            lower = lax.broadcasted_iota(jnp.int32, (128, 128), 0) >= lax.broadcasted_iota(jnp.int32, (128, 128), 1)
            st4[0:128, :] = jnp.where(lower, m00, m11)
            st4[128:136, :] = jnp.broadcast_to(jnp.sum(jnp.where(on128, m11, 0.0), axis=0, keepdims=True), (8, 128))
            up4[0].start()
            up4[1].start()
            up3[3].wait_recv()
            b3 = mm(k3, (f2y + r3[384:512, :]) * d3)
            f3 = cat(f2x, r3[512:640, :]) - mm(g3, b3)
            st4[264:520, :] = f3
            up4[2].start()
            back = mm(x2r[:, 128:], cat(x3r, b3, axis=1))
            near_map = cat(x3r[:, :128], x2r[:, :128] - back[:, :128])
            far_map = cat(x3r[:, 128:], -back[:, 128:256])
            down_free = cat(b3, b2 - back[:, 256:])
            up2[3].wait_recv()
            outer_map = cat(r2[512:576, :], r2[448:512, :], axis=1)
            outer_part = mm(outer_map, cat(near_map, far_map, down_free, axis=1))
            near_map = cat(near_map, -outer_part[:, :128])
            far_map = cat(far_map, -outer_part[:, 128:256])
            down_free = cat(down_free, r2[576:640, :] - outer_part[:, 256:])
            up4[0].wait_recv()
            mix = r4[0:128, :]
            mix_t = mix.T
            k4, d4 = face_inverse(m00 + jnp.where(lower, mix, mix_t))
            up4[1].wait_recv()
            v01 = m01 + r4[136:264, :]
            v10 = v01.T
            x4 = mm(k4, v01 * d4)
            far_block = m11 + jnp.where(on128, jnp.broadcast_to(r4[128:129, :], (128, 128)), jnp.where(lower, mix_t, mix))
            k5, d5 = face_inverse(far_block - mm(v10, x4))
            x4t = x4.T
            far_map = far_map - mm(near_map, x4)
            up4[2].wait_recv()
            h4 = f3[:128] + r4[264:392, :]
            y4 = mm(k4, h4 * d4)
            u_far = mm(k5, (f3[128:] + r4[392:520, :] - mm(x4t, h4)) * d5)
            u_near = y4 - mm(x4, u_far)
            u_low = down_free - mm(near_map, y4) - mm(far_map, u_far)
            dnst[0:64, :] = u_low[256:]
            down2[0].start()
            dnst[64:128, :] = u_low[192:256]
            down2[1].start()
            dnst[128:192, :] = u_low[128:192]
            dnst[192:256, :] = u_low[64:128]
            down2[2].start()
            ur[0:128, :] = u_low[128:256]
            ur[128:256, :] = u_near
            ur[256:320, :] = u_low[:64]
            ur[320:384, :] = zero
            down1[0].start()
            down1[1].start()
            u_yi = x1b[...] - mm(x1r, ur[...])
            uyi[...] = u_yi
            down1[2].start()
            uloc[0:64, :] = ur[0:64, :]
            uloc[64:128, :] = ur[128:192, :]
            uloc[128:192, :] = u_yi
            uloc[192:256, :] = ur[256:320, :]
            for copy in up3 + up4 + down2 + down1:
                copy.wait_send()

    uloc[...] = uloc[...] + ut[...]
    u_b = cat(*[uloc[pl.ds(p, 64), :] for p in places])
    out_b[...] = u_b
    out_in[...] = src[:256, :] + mm(zq, u_b)
    for away, copy, _ in top_sends:

        @pl.when(away)
        def _():
            copy.wait_send()


def store(a, b, out_a, out_b, sem):
    copies = [pltpu.make_async_copy(x, y, sem.at[k]) for k, (x, y) in enumerate(((a, out_a), (b, out_b)))]
    for copy in copies:
        copy.start()
    for copy in copies:
        copy.wait()


def solution(mesh):
    def local(couple_inner, couple_cross, couple_outer, margin, sources, top_values):
        vmem = pl.BlockSpec(memory_space=pltpu.VMEM)
        anywhere = pl.BlockSpec(memory_space=pl.ANY)
        shapes = [(256, 256)] * 3 + [(1, 512), (512, 128), (256, 256), (256, 128), (256, 128), (2, 128, 128), (192, 256), (192, 128),
                  (640, 128), (640, 128), (640, 128), (640, 128), (640, 128), (640, 128), (384, 128), (256, 128), (128, 128), (64, 128),
                  (192, 128), (256, 128), (64, 128)]
        dma = pltpu.SemaphoreType.DMA
        interior, boundary = pl.pallas_call(
            kernel,
            out_shape=(pltpu.VMEM((256, 128), F32), pltpu.VMEM((256, 128), F32)),
            in_specs=[anywhere] * 6,
            out_specs=(vmem, vmem),
            scratch_shapes=[pltpu.VMEM(shape, F32) for shape in shapes] + [dma((6,)), dma((24,)), dma((24,)), dma((2, 4))],
            compiler_params=pltpu.CompilerParams(collective_id=0, has_side_effects=True),
        )(
            couple_inner.reshape(256, 256),
            couple_cross.reshape(256, 256),
            couple_outer.reshape(256, 256),
            margin.reshape(1, 512),
            sources.reshape(512, 128),
            top_values,
        )
        interior, boundary = pl.pallas_call(
            store,
            out_shape=(jax.ShapeDtypeStruct((256, 128), F32),) * 2,
            in_specs=[vmem, vmem],
            out_specs=(anywhere, anywhere),
            scratch_shapes=[dma((2,))],
        )(pltpu.with_memory_space_constraint(interior, pltpu.VMEM), pltpu.with_memory_space_constraint(boundary, pltpu.VMEM))
        return interior[None, None], boundary[None, None]

    spec = P("gx", "gy", None, None)
    return jax.shard_map(
        local,
        mesh=mesh,
        in_specs=(spec, spec, spec, P("gx", "gy", None), spec, P("gy", "gx")),
        out_specs=(spec, spec),
        check_vma=False,
    )
```

```python
import jax
import jax.numpy as jnp
from jax import lax
from jax.experimental import pallas as pl
from jax.experimental.pallas import tpu as pltpu
from jax.sharding import PartitionSpec as P

F32 = jnp.float32
BF16 = jnp.bfloat16
MESH = pl.DeviceIdType.MESH

LEAF_RHO = (255 * 0.003515625) / (255 * 0.003515625 + 256 * 0.000390625) / 1.05
FACE_RHO = 1.0 / 1.05
FIRST_RHO = (64 * 9) / (64 * 9 + 192) / 1.05
SECOND_RHO = (64 * 9) / (64 * 9 + 128) / 1.05
THIRD_RHO = (64 * 9) / (64 * 9 + 64) / 1.05
NEAR_STEPS = 5
LEAF_STEPS = 5
FACE_STEPS = 6


def split(x):
    high = x.astype(BF16)
    low = (x - high.astype(F32)).astype(BF16)
    return high, low


def dot(a, b):
    return jnp.dot(a, b, preferred_element_type=F32)


def mm_split(a, b):
    depth, width = b[0].shape
    if depth % 128:
        return dot(a[0], b[0]) + (dot(a[0], b[1]) + dot(a[1], b[0]))
    if width == 128 and depth == 128:
        wide = jnp.concatenate([b[0], b[1]], 1)
        out = dot(jnp.concatenate([a[0], a[1]], 1), jnp.concatenate([wide, wide], 0))
        return out[:, :128] + out[:, 128:]
    if width == 128:
        out = dot(a[0], jnp.concatenate([b[0], b[1]], 1))
        return out[:, :128] + (out[:, 128:] + dot(a[1], b[0]))
    return dot(jnp.concatenate([a[0], a[0], a[1]], 1), jnp.concatenate([b[0], b[1], b[0]], 0))


def mm(a, b):
    return mm_split(split(a), split(b))


def eye_mask(n):
    return lax.broadcasted_iota(jnp.int32, (n, n), 0) == lax.broadcasted_iota(jnp.int32, (n, n), 1)


def inverse_of(h, rho, steps):
    n = h.shape[0]
    eye = jnp.where(eye_mask(n), 1.0, 0.0).astype(F32)
    t = 1.0 / rho
    s, r = None, h
    for k in range(steps):
        square = 2.0 * t * t
        alpha = square / (square - 1.0)
        if k == steps - 1:
            return s, r, alpha
        if k == steps - 2:
            rs = split(r)
            p = mm_split(split(s), rs)
            r = alpha * dot(rs[0], rs[0]) - (alpha - 1.0) * eye
            s = alpha * (s + p)
        elif s is None:
            rs = split(r)
            s = alpha * (eye + r)
            r = alpha * mm_split(rs, rs) - (alpha - 1.0) * eye
        else:
            ss, rs = split(s), split(r)
            p = mm_split((jnp.concatenate([rs[0], ss[0]], 0), jnp.concatenate([rs[1], ss[1]], 0)), rs)
            r = alpha * p[:n] - (alpha - 1.0) * eye
            s = alpha * (s + p[n:])
        t = square - 1.0


def lift(r, x):
    return x + dot(r.astype(BF16), x.astype(BF16))


def closed(s, r, alpha):
    return alpha * (s + dot(s.astype(BF16), r.astype(BF16)))


def face_inverse(v, rho=FACE_RHO, steps=FACE_STEPS):
    n = v.shape[0]
    on = eye_mask(n)
    di = 1.0 / jnp.sum(jnp.where(on, v, 0.0), axis=1, keepdims=True)
    h = jnp.where(on, 0.0, -v * di)
    return inverse_of(h, rho, steps), di


def half_swap(x):
    return pltpu.roll(x, 64, 1)


def cat(*parts, axis=0):
    return jnp.concatenate(parts, axis)


def kernel(ci_h, cq_h, co_h, mg_h, src_h, top, out_in, out_b, ci, cq, co, mg, src, mloc, gloc, zq, ut, tv, s1m, s1g, st2, r2, st3, r3, st4, r4, ur,
           dnst, dn2, uyi, dn1, uloc, x1b, load, send, recv, tvrecv):
    loads = [pltpu.make_async_copy(h, v, load.at[k]) for k, (h, v) in enumerate(((ci_h, ci), (cq_h, cq), (mg_h, mg), (co_h, co), (src_h, src)))]
    for copy in loads:
        copy.start()

    gx, gy = lax.axis_index("gx"), lax.axis_index("gy")
    lx, ly = gx % 4, gy % 4
    x0, y0 = gx - lx, gy - ly
    bx, by, cx, cy = lx % 2, ly % 2, lx // 2, ly // 2
    px, py = (bx + cx) % 2, (by + cy) % 2

    def at(i, j):
        return (x0 + i, y0 + j)

    barrier = pltpu.get_barrier_semaphore()
    for i in range(4):
        for j in range(4):
            if i or j:
                pl.semaphore_signal(barrier, 1, device_id=at((lx + i) % 4, (ly + j) % 4), device_id_type=MESH)

    def remote(k, source, target, device):
        return pltpu.make_async_remote_copy(src_ref=source, dst_ref=target, send_sem=send.at[k], recv_sem=recv.at[k],
                                            device_id=device, device_id_type=MESH)

    def rows(ref, start, count):
        return ref.at[pl.ds(start, count), :]

    mate = (gx, gy + 1 - 2 * by)
    pair = (gx + 1 - 2 * bx, gy)
    cross = (gx + 1 - 2 * bx, gy + 1 - 2 * by)
    side_y = at(lx, 3 - ly)
    side_x = at(3 - lx, ly)

    on = eye_mask(256)
    loads[0].wait()
    a = ci[...]
    inner = jnp.where(on, 0.0, 0.5 * (a + a.T))
    loads[1].wait()
    loads[2].wait()
    q = cq[...]
    margin = mg[...]
    m_in = jnp.sum(jnp.where(on, jnp.broadcast_to(margin[:, :256], (256, 256)), 0.0), axis=1, keepdims=True)
    m_out = jnp.sum(jnp.where(on, jnp.broadcast_to(margin[:, 256:], (256, 256)), 0.0), axis=1, keepdims=True)
    d_in = (jnp.sum(inner, 1, keepdims=True) + jnp.sum(q, 1, keepdims=True)) * (1.0 + m_in)
    di = 1.0 / d_in

    di0 = di[:128]
    open0 = inverse_of(inner[:128, :128] * di0, LEAF_RHO, LEAF_STEPS)
    across_t = inner[128:, :128]
    lifted0 = lift(open0[1], cat(inner[:128, 128:], q[:128], axis=1) * di0)
    second = open0[2] * mm(mm(across_t, open0[0]), lifted0)
    rest = q[128:] + second[:, 128:]

    pl.semaphore_wait(barrier, 15)
    on_x = 1 - lx // 2
    top_sends = []
    for k in range(4):
        dx = on_x * lx * 3 + (1 - on_x) * k
        dy = on_x * k + (1 - on_x) * (lx - 2) * 3
        away = (dx - lx) * (dx - lx) + (dy - ly) * (dy - ly) > 0
        piece = top.at[:, pl.ds((k // 2) * 128, 128)]
        slot = tv.at[lx // 2, pl.ds(pl.multiple_of(ly * 32, 32), 32), :]
        copy = pltpu.make_async_remote_copy(src_ref=piece, dst_ref=slot, send_sem=send.at[k], recv_sem=tvrecv.at[lx // 2, ly],
                                            device_id=at(dx, dy), device_id_type=MESH)
        here = pltpu.make_async_copy(piece, slot, load.at[5])
        top_sends.append((away, copy, here))

        @pl.when(away)
        def _():
            copy.start()

        @pl.when(jnp.logical_not(away))
        def _():
            here.start()

    qt = q.T
    loads[3].wait()
    o = co[...]
    outer = jnp.where(on, 0.0, 0.5 * (o + o.T))
    d_out = (jnp.sum(outer, 1, keepdims=True) + jnp.sum(qt, 1, keepdims=True)) * (1.0 + m_out)
    e_out = jnp.where(on, d_out, -outer)
    first = open0[2] * mm(open0[0], lifted0)
    across, y_q = first[:, :128], first[:, 128:]
    e_out = e_out - mm(qt[:, :128], y_q)
    open1, di1 = face_inverse(jnp.where(on[:128, :128], d_in[128:], 0.0) - inner[128:, 128:] - second[:, :128], LEAF_RHO, LEAF_STEPS)
    lifted1 = lift(open1[1], rest * di1)
    m = e_out - open1[2] * mm(mm(rest.T, open1[0]), lifted1)
    t0, t1 = m[:, :128], m[:, 128:]
    t0 = jnp.where(bx == 0, half_swap(t0), t0)
    t1 = jnp.where(by == 0, half_swap(t1), t1)
    places = [pl.multiple_of(p, 64) for p in (64 * (1 - bx), 64 * bx, 128 + 64 * (1 - by), 128 + 64 * by)]
    for k in range(4):
        mloc[pl.ds(places[k], 64), :] = cat(t0[64 * k : 64 * k + 64], t1[64 * k : 64 * k + 64], axis=1)

    up1 = [
        remote(4, rows(mloc, 128, 64), rows(s1m, 128, 64), mate),
        remote(5, rows(mloc, 0, 128), rows(s1m, 0, 128), mate),
        remote(6, rows(gloc, 0, 192), s1g, mate),
    ]
    down1 = [
        remote(7, rows(ur, 64, 64), rows(dn1, 0, 64), mate),
        remote(8, rows(ur, 192, 64), rows(dn1, 64, 64), mate),
        remote(9, uyi, rows(dn1, 128, 64), mate),
    ]
    down2 = [
        remote(13, rows(dnst, 0, 64), uyi, pair),
        remote(22, rows(dnst, 64, 64), rows(dn1, 0, 64), cross),
        remote(23, rows(dnst, 128, 128), dn2, pair),
    ]
    left = lax.broadcasted_iota(jnp.int32, (64, 128), 1) < 64
    zero = jnp.zeros((64, 128), F32)

    @pl.when(py == 0)
    def _():
        up1[0].start()
        up1[1].start()

    def leaf_flux():
        s0, s1 = closed(*open0), closed(*open1)
        z1 = open1[2] * mm(open1[0], lifted1)
        zq[0:128, :] = y_q + mm(across, z1)
        zq[128:256, :] = z1
        loads[4].wait()
        y0 = mm(s0, src[:128, :] * di0)
        z1 = mm(s1, (src[128:256, :] + mm(across_t, y0)) * di1)
        z = cat(y0 + mm(across, z1), z1)
        g = src[256:, :] + mm(qt, z)
        for k in range(4):
            gloc[pl.ds(places[k], 64), :] = g[64 * k : 64 * k + 64]
        src[:256, :] = z
        ut[...] = jnp.zeros_like(ut)
        for away, _, here in top_sends:

            @pl.when(jnp.logical_not(away))
            def _():
                here.wait()

        for side in range(2):
            known = (1 - px) if side == 0 else (1 - py)

            @pl.when(known == 1)
            def _():
                origin = cx if side == 0 else 2 + cy
                for j in range(4):
                    mine = (lx - origin) * (lx - origin) + (ly - j) * (ly - j) > 0

                    @pl.when(mine)
                    def _():
                        piece = tv.at[side, pl.ds(j * 32, 32), :]
                        pltpu.make_async_remote_copy(src_ref=piece, dst_ref=piece, send_sem=send.at[0], recv_sem=tvrecv.at[side, j],
                                                     device_id=mate, device_id_type=MESH).wait_recv()

                flipped = tv[side].T
                b = by if side == 0 else bx
                ut[64 + 128 * side : 128 + 128 * side, :] = jnp.where(b == 0, flipped[:64], flipped[64:])

        gloc[...] = gloc[...] - mm(mloc[...], ut[...])

    @pl.when(py == 0)
    def _():
        leaf_flux()
        up1[2].start()

        @pl.when(px == 1)
        def _():
            down1[0].wait_recv()
            down1[1].wait_recv()
            uloc[64:128, :] = dn1[64:128, :]

        @pl.when(px == 0)
        def _():
            down2[1].wait_recv()
            uloc[64:128, :] = zero

        down1[2].wait_recv()
        uloc[0:64, :] = dn1[0:64, :]
        uloc[128:192, :] = dn1[128:192, :]
        uloc[192:256, :] = zero
        for copy in up1:
            copy.wait_send()

    @pl.when(py == 1)
    def _():
        up1[0].wait_recv()
        v1 = mloc[128:192, 128:256] + s1m[128:192, 128:256]
        open_1, d1 = face_inverse(v1[:, :64], FIRST_RHO, NEAR_STEPS)
        up1[1].wait_recv()

        def left_of(x):
            return jnp.where(left, x, 0.0)

        def wide_root(k):
            x, y = mloc[k : k + 64, :128], mloc[k : k + 64, 128:]
            return cat(left_of(x), left_of(half_swap(x)), left_of(half_swap(y)), axis=1)

        def wide_mate(k):
            x = s1m[k : k + 64, :128]
            return cat(jnp.where(left, 0.0, half_swap(x)), jnp.where(left, 0.0, x), zero, axis=1)

        gt1 = (wide_root(128) + wide_mate(128)) * d1
        g1 = cat(mloc[0:64, 128:256], s1m[0:64, 128:256], mloc[64:128, 128:256], s1m[64:128, 128:256], mloc[192:256, 128:256])[:, :64]
        half1 = open_1[2] * mm(g1, open_1[0])
        lifted1a = lift(open_1[1], gt1[:, :128])
        shared1 = cat(wide_root(0)[:, :128], wide_mate(0)[:, :128]) - mm(half1[:128], lifted1a)
        up2 = [
            remote(10, rows(st2, 0, 128), rows(r2, 0, 128), pair),
            remote(11, rows(st2, 128, 128), rows(r2, 128, 128), pair),
            remote(12, rows(st2, 256, 192), rows(r2, 256, 192), pair),
            remote(21, rows(st2, 448, 192), rows(r2, 448, 192), pair),
        ]

        @pl.when(px == 0)
        def _():
            st2[0:128, :] = shared1
            up2[0].start()

        lifted1b = lift(open_1[1], gt1[:, 128:])
        p1l, p1r = mm(half1[128:], lifted1a), mm(half1, lifted1b)
        k1 = closed(*open_1)
        x1a = mm(k1, gt1[:, :128])
        x1r = cat(x1a, mm(k1, gt1[:, 128:]), axis=1)
        m1 = cat(
            cat(shared1, cat(wide_root(64)[:, :128], wide_mate(64)[:, :128], wide_root(192)[:, :128]) - p1l),
            cat(*[w[:, 128:] for w in (wide_root(0), wide_mate(0), wide_root(64), wide_mate(64), wide_root(192))]) - p1r,
            axis=1)

        def flux1():
            leaf_flux()
            up1[2].wait_recv()
            b1 = mm(k1, (gloc[128:192, :] + s1g[128:192, :]) * d1)
            x1b[...] = b1
            return cat(gloc[0:64, :], s1g[0:64, :], gloc[64:128, :], s1g[64:128, :], gloc[192:256, :]) - mm(g1, b1)

        @pl.when(px == 0)
        def _():
            st2[128:192, :] = m1[256:320, :128]
            st2[192:256, :] = half_swap(m1[256:320, 256:])
            up2[1].start()
            f1 = flux1()
            st2[256:384, :] = f1[0:128]
            st2[384:448, :] = f1[256:320]
            up2[2].start()
            st2[448:512, :] = x1a
            st2[512:576, :] = half_swap(x1r[:, 256:])
            st2[576:640, :] = x1b[...]
            up2[3].start()
            down2[0].wait_recv()
            down1[2].start()
            down2[2].wait_recv()
            uloc[0:64, :] = dn2[0:64, :]
            uloc[64:128, :] = zero
            uloc[128:192, :] = uyi[...]
            uloc[192:256, :] = dn2[64:128, :]
            down1[2].wait_send()
            for copy in up2:
                copy.wait_send()

        @pl.when(px == 1)
        def _():
            f1 = flux1()
            up2[0].wait_recv()
            open_2, d2 = face_inverse(m1[0:128, :128] + r2[0:128, :], SECOND_RHO, NEAR_STEPS)
            up2[1].wait_recv()
            w0 = r2[128:192, :]
            gt2 = cat(m1[0:128, 128:256], m1[0:128, 256:] + cat(zero, w0).T, axis=1)
            gt2 = gt2 * d2
            lifted2y = lift(open_2[1], gt2[:, 128:])

            up3 = [
                remote(14, rows(st3, 0, 128), rows(r3, 0, 128), side_y),
                remote(15, rows(st3, 128, 128), rows(r3, 128, 128), side_y),
                remote(16, rows(st3, 256, 128), rows(r3, 256, 128), side_y),
                remote(17, rows(st3, 384, 256), rows(r3, 384, 256), side_y),
            ]
            g2y = cat(m1[256:320, :128], w0)
            base2y = cat(m1[256:320, 128:], cat(zero, r2[192:256, :], axis=1))
            half2y = open_2[2] * mm(g2y, open_2[0])
            m2yy = base2y[:, 128:] - mm(half2y, lifted2y)
            st3[0:128, :] = m2yy
            up3[0].start()
            m2yx = base2y[:, :128] - mm(half2y, lift(open_2[1], gt2[:, :128]))
            st3[128:256, :] = m2yx
            up3[1].start()
            k2 = closed(*open_2)
            x2r = mm(k2, gt2)
            g2x = m1[128:256, :128]
            m2x = m1[128:256, 128:] - mm(g2x, x2r)
            st3[256:384, :] = m2x[:, :128]
            up3[2].start()
            up2[2].wait_recv()
            b2 = mm(k2, (f1[0:128] + r2[256:384, :]) * d2)
            f2y = cat(f1[256:320], r2[384:448, :]) - mm(g2y, b2)
            f2x = f1[128:256] - mm(g2x, b2)
            st3[384:512, :] = f2y
            st3[512:640, :] = f2x
            up3[3].start()
            up3[0].wait_recv()
            open_3, d3 = face_inverse(m2yy + r3[0:128, :], THIRD_RHO, NEAR_STEPS)
            up3[1].wait_recv()
            yx = r3[128:256, :]
            gt3 = cat(m2yx, yx, axis=1) * d3
            g3 = cat(m2x[:, 128:], yx.T)
            p3 = open_3[2] * mm(mm(g3, open_3[0]), lift(open_3[1], gt3))

            up4 = [
                remote(18, rows(st4, 0, 136), rows(r4, 0, 136), side_x),
                remote(19, rows(st4, 136, 128), rows(r4, 136, 128), side_x),
                remote(20, rows(st4, 264, 256), rows(r4, 264, 256), side_x),
            ]
            m00, m01 = m2x[:, :128] - p3[:128, :128], -p3[:128, 128:]
            st4[136:264, :] = m01
            up3[2].wait_recv()
            m11 = r3[256:384, :] - p3[128:, 128:]
            on128 = eye_mask(128)
            lower = lax.broadcasted_iota(jnp.int32, (128, 128), 0) >= lax.broadcasted_iota(jnp.int32, (128, 128), 1)
            st4[0:128, :] = jnp.where(lower, m00, m11)
            st4[128:136, :] = jnp.broadcast_to(jnp.sum(jnp.where(on128, m11, 0.0), axis=0, keepdims=True), (8, 128))
            up4[0].start()
            up4[1].start()
            up3[3].wait_recv()
            k3 = closed(*open_3)
            x3r = mm(k3, gt3)
            b3 = mm(k3, (f2y + r3[384:512, :]) * d3)
            f3 = cat(f2x, r3[512:640, :]) - mm(g3, b3)
            st4[264:520, :] = f3
            up4[2].start()
            back = mm(x2r[:, 128:], cat(x3r, b3, axis=1))
            near_map = cat(x3r[:, :128], x2r[:, :128] - back[:, :128])
            far_map = cat(x3r[:, 128:], -back[:, 128:256])
            down_free = cat(b3, b2 - back[:, 256:])
            up2[3].wait_recv()
            outer_map = cat(r2[512:576, :], r2[448:512, :], axis=1)
            outer_part = mm(outer_map, cat(near_map, far_map, down_free, axis=1))
            near_map = cat(near_map, -outer_part[:, :128])
            far_map = cat(far_map, -outer_part[:, 128:256])
            down_free = cat(down_free, r2[576:640, :] - outer_part[:, 256:])
            up4[0].wait_recv()
            mix = r4[0:128, :]
            mix_t = mix.T
            open_4, d4 = face_inverse(m00 + jnp.where(lower, mix, mix_t))
            up4[1].wait_recv()
            v01 = m01 + r4[136:264, :]
            v10 = v01.T
            lifted4 = lift(open_4[1], v01 * d4)
            far_block = m11 + jnp.where(on128, jnp.broadcast_to(r4[128:129, :], (128, 128)), jnp.where(lower, mix_t, mix))
            open_5, d5 = face_inverse(far_block - open_4[2] * mm(mm(v10, open_4[0]), lifted4))
            k4, k5 = closed(*open_4), closed(*open_5)
            x4 = open_4[2] * mm(open_4[0], lifted4)
            x4t = x4.T
            far_map = far_map - mm(near_map, x4)
            up4[2].wait_recv()
            h4 = f3[:128] + r4[264:392, :]
            y4 = mm(k4, h4 * d4)
            u_far = mm(k5, (f3[128:] + r4[392:520, :] - mm(x4t, h4)) * d5)
            u_near = y4 - mm(x4, u_far)
            u_low = down_free - mm(near_map, y4) - mm(far_map, u_far)
            dnst[0:64, :] = u_low[256:]
            down2[0].start()
            dnst[64:128, :] = u_low[192:256]
            down2[1].start()
            dnst[128:192, :] = u_low[128:192]
            dnst[192:256, :] = u_low[64:128]
            down2[2].start()
            ur[0:128, :] = u_low[128:256]
            ur[128:256, :] = u_near
            ur[256:320, :] = u_low[:64]
            ur[320:384, :] = zero
            down1[0].start()
            down1[1].start()
            u_yi = x1b[...] - mm(x1r, ur[...])
            uyi[...] = u_yi
            down1[2].start()
            uloc[0:64, :] = ur[0:64, :]
            uloc[64:128, :] = ur[128:192, :]
            uloc[128:192, :] = u_yi
            uloc[192:256, :] = ur[256:320, :]
            for copy in up3 + up4 + down2 + down1:
                copy.wait_send()

    uloc[...] = uloc[...] + ut[...]
    u_b = cat(*[uloc[pl.ds(p, 64), :] for p in places])
    out_b[...] = u_b
    out_in[...] = src[:256, :] + mm(zq[...], u_b)
    for away, copy, _ in top_sends:

        @pl.when(away)
        def _():
            copy.wait_send()


def store(a, b, out_a, out_b, sem):
    copies = [pltpu.make_async_copy(x, y, sem.at[k]) for k, (x, y) in enumerate(((a, out_a), (b, out_b)))]
    for copy in copies:
        copy.start()
    for copy in copies:
        copy.wait()


def solution(mesh):
    def local(couple_inner, couple_cross, couple_outer, margin, sources, top_values):
        vmem = pl.BlockSpec(memory_space=pltpu.VMEM)
        anywhere = pl.BlockSpec(memory_space=pl.ANY)
        shapes = [(256, 256)] * 3 + [(1, 512), (512, 128), (256, 256), (256, 128), (256, 256), (256, 128), (2, 128, 128), (192, 256), (192, 128),
                  (640, 128), (640, 128), (640, 128), (640, 128), (640, 128), (640, 128), (384, 128), (256, 128), (128, 128), (64, 128),
                  (192, 128), (256, 128), (64, 128)]
        dma = pltpu.SemaphoreType.DMA
        interior, boundary = pl.pallas_call(
            kernel,
            out_shape=(pltpu.VMEM((256, 128), F32), pltpu.VMEM((256, 128), F32)),
            in_specs=[anywhere] * 6,
            out_specs=(vmem, vmem),
            scratch_shapes=[pltpu.VMEM(shape, F32) for shape in shapes] + [dma((6,)), dma((24,)), dma((24,)), dma((2, 4))],
            compiler_params=pltpu.CompilerParams(collective_id=0, has_side_effects=True),
        )(
            couple_inner.reshape(256, 256),
            couple_cross.reshape(256, 256),
            couple_outer.reshape(256, 256),
            margin.reshape(1, 512),
            sources.reshape(512, 128),
            top_values,
        )
        interior, boundary = pl.pallas_call(
            store,
            out_shape=(jax.ShapeDtypeStruct((256, 128), F32),) * 2,
            in_specs=[vmem, vmem],
            out_specs=(anywhere, anywhere),
            scratch_shapes=[dma((2,))],
        )(pltpu.with_memory_space_constraint(interior, pltpu.VMEM), pltpu.with_memory_space_constraint(boundary, pltpu.VMEM))
        return interior[None, None], boundary[None, None]

    spec = P("gx", "gy", None, None)
    return jax.shard_map(
        local,
        mesh=mesh,
        in_specs=(spec, spec, spec, P("gx", "gy", None), spec, P("gy", "gx")),
        out_specs=(spec, spec),
        check_vma=False,
    )
```

```python
import jax
import jax.numpy as jnp
from jax import lax
from jax.experimental import pallas as pl
from jax.experimental.pallas import tpu as pltpu
from jax.sharding import PartitionSpec as P

F32 = jnp.float32
BF16 = jnp.bfloat16
MESH = pl.DeviceIdType.MESH

LEAF_RHO = (255 * 0.003515625) / (255 * 0.003515625 + 256 * 0.000390625) / 1.05
FACE_RHO = 1.0 / 1.05
FIRST_RHO = (64 * 9) / (64 * 9 + 192) / 1.05
SECOND_RHO = (64 * 9) / (64 * 9 + 128) / 1.05
THIRD_RHO = (64 * 9) / (64 * 9 + 64) / 1.05
NEAR_STEPS = 5
LEAF_STEPS = 5
FACE_STEPS = 6


def split(x):
    high = x.astype(BF16)
    low = (x - high.astype(F32)).astype(BF16)
    return high, low


def dot(a, b):
    return jnp.dot(a, b, preferred_element_type=F32)


def mm_split(a, b):
    depth, width = b[0].shape
    if depth % 128:
        return dot(a[0], b[0]) + (dot(a[0], b[1]) + dot(a[1], b[0]))
    if width == 128 and depth == 128:
        wide = jnp.concatenate([b[0], b[1]], 1)
        out = dot(jnp.concatenate([a[0], a[1]], 1), jnp.concatenate([wide, wide], 0))
        return out[:, :128] + out[:, 128:]
    if width == 128:
        out = dot(a[0], jnp.concatenate([b[0], b[1]], 1))
        return out[:, :128] + (out[:, 128:] + dot(a[1], b[0]))
    return dot(jnp.concatenate([a[0], a[0], a[1]], 1), jnp.concatenate([b[0], b[1], b[0]], 0))


def mm(a, b):
    return mm_split(split(a), split(b))


def eye_mask(n):
    return lax.broadcasted_iota(jnp.int32, (n, n), 0) == lax.broadcasted_iota(jnp.int32, (n, n), 1)


def inverse_of(h, rho, steps):
    n = h.shape[0]
    eye = jnp.where(eye_mask(n), 1.0, 0.0).astype(F32)
    t = 1.0 / rho
    s, r = None, h
    for k in range(steps):
        square = 2.0 * t * t
        alpha = square / (square - 1.0)
        if k == steps - 1:
            return s, r, alpha
        if k == steps - 2:
            rs = split(r)
            p = mm_split(split(s), rs)
            r = alpha * dot(rs[0], rs[0]) - (alpha - 1.0) * eye
            s = alpha * (s + p)
        elif s is None:
            rs = split(r)
            s = alpha * (eye + r)
            r = alpha * mm_split(rs, rs) - (alpha - 1.0) * eye
        else:
            ss, rs = split(s), split(r)
            p = mm_split((jnp.concatenate([rs[0], ss[0]], 0), jnp.concatenate([rs[1], ss[1]], 0)), rs)
            r = alpha * p[:n] - (alpha - 1.0) * eye
            s = alpha * (s + p[n:])
        t = square - 1.0


def lift(r, x):
    return x + dot(r.astype(BF16), x.astype(BF16))


def closed(s, r, alpha):
    return alpha * (s + dot(s.astype(BF16), r.astype(BF16)))


def face_inverse(v, rho=FACE_RHO, steps=FACE_STEPS):
    n = v.shape[0]
    on = eye_mask(n)
    di = 1.0 / jnp.sum(jnp.where(on, v, 0.0), axis=1, keepdims=True)
    h = jnp.where(on, 0.0, -v * di)
    return inverse_of(h, rho, steps), di


def half_swap(x):
    return pltpu.roll(x, 64, 1)


def cat(*parts, axis=0):
    return jnp.concatenate(parts, axis)


def kernel(ci_h, cq_h, co_h, mg_h, src_h, top, out_in, out_b, ci, cq, co, mg, src, mloc, gloc, ut, tv, s1m, s1g, st2, r2, st3, r3, st4, r4, ur,
           dnst, dn2, uyi, dn1, uloc, x1b, zq, zq_low, load, send, recv, tvrecv):
    loads = [pltpu.make_async_copy(h, v, load.at[k]) for k, (h, v) in enumerate(((ci_h, ci), (cq_h, cq), (mg_h, mg), (co_h, co), (src_h, src)))]
    for copy in loads:
        copy.start()

    gx, gy = lax.axis_index("gx"), lax.axis_index("gy")
    lx, ly = gx % 4, gy % 4
    x0, y0 = gx - lx, gy - ly
    bx, by, cx, cy = lx % 2, ly % 2, lx // 2, ly // 2
    px, py = (bx + cx) % 2, (by + cy) % 2

    def at(i, j):
        return (x0 + i, y0 + j)

    barrier = pltpu.get_barrier_semaphore()
    for i in range(4):
        for j in range(4):
            if i or j:
                pl.semaphore_signal(barrier, 1, device_id=at((lx + i) % 4, (ly + j) % 4), device_id_type=MESH)

    def remote(k, source, target, device):
        return pltpu.make_async_remote_copy(src_ref=source, dst_ref=target, send_sem=send.at[k], recv_sem=recv.at[k],
                                            device_id=device, device_id_type=MESH)

    def rows(ref, start, count):
        return ref.at[pl.ds(start, count), :]

    mate = (gx, gy + 1 - 2 * by)
    pair = (gx + 1 - 2 * bx, gy)
    cross = (gx + 1 - 2 * bx, gy + 1 - 2 * by)
    side_y = at(lx, 3 - ly)
    side_x = at(3 - lx, ly)

    on = eye_mask(256)
    loads[0].wait()
    a = ci[...]
    inner = jnp.where(on, 0.0, 0.5 * (a + a.T))
    loads[1].wait()
    loads[2].wait()
    q = cq[...]
    margin = mg[...]
    m_in = jnp.sum(jnp.where(on, jnp.broadcast_to(margin[:, :256], (256, 256)), 0.0), axis=1, keepdims=True)
    m_out = jnp.sum(jnp.where(on, jnp.broadcast_to(margin[:, 256:], (256, 256)), 0.0), axis=1, keepdims=True)
    d_in = (jnp.sum(inner, 1, keepdims=True) + jnp.sum(q, 1, keepdims=True)) * (1.0 + m_in)
    di = 1.0 / d_in

    di0 = di[:128]
    open0 = inverse_of(inner[:128, :128] * di0, LEAF_RHO, LEAF_STEPS)
    across_t = inner[128:, :128]
    lifted0 = lift(open0[1], cat(inner[:128, 128:], q[:128], axis=1) * di0)
    second = open0[2] * mm(mm(across_t, open0[0]), lifted0)
    rest = q[128:] + second[:, 128:]

    pl.semaphore_wait(barrier, 15)
    on_x = 1 - lx // 2
    top_sends = []
    for k in range(4):
        dx = on_x * lx * 3 + (1 - on_x) * k
        dy = on_x * k + (1 - on_x) * (lx - 2) * 3
        away = (dx - lx) * (dx - lx) + (dy - ly) * (dy - ly) > 0
        piece = top.at[:, pl.ds((k // 2) * 128, 128)]
        slot = tv.at[lx // 2, pl.ds(pl.multiple_of(ly * 32, 32), 32), :]
        copy = pltpu.make_async_remote_copy(src_ref=piece, dst_ref=slot, send_sem=send.at[k], recv_sem=tvrecv.at[lx // 2, ly],
                                            device_id=at(dx, dy), device_id_type=MESH)
        here = pltpu.make_async_copy(piece, slot, load.at[5])
        top_sends.append((away, copy, here))

        @pl.when(away)
        def _():
            copy.start()

        @pl.when(jnp.logical_not(away))
        def _():
            here.start()

    qt = q.T
    loads[3].wait()
    o = co[...]
    outer = jnp.where(on, 0.0, 0.5 * (o + o.T))
    d_out = (jnp.sum(outer, 1, keepdims=True) + jnp.sum(qt, 1, keepdims=True)) * (1.0 + m_out)
    e_out = jnp.where(on, d_out, -outer)
    first = open0[2] * mm(open0[0], lifted0)
    across, y_q = first[:, :128], first[:, 128:]
    e_out = e_out - mm(qt[:, :128], y_q)
    open1, di1 = face_inverse(jnp.where(on[:128, :128], d_in[128:], 0.0) - inner[128:, 128:] - second[:, :128], LEAF_RHO, LEAF_STEPS)
    lifted1 = lift(open1[1], rest * di1)
    m = e_out - open1[2] * mm(mm(rest.T, open1[0]), lifted1)
    t0, t1 = m[:, :128], m[:, 128:]
    t0 = jnp.where(bx == 0, half_swap(t0), t0)
    t1 = jnp.where(by == 0, half_swap(t1), t1)
    places = [pl.multiple_of(p, 64) for p in (64 * (1 - bx), 64 * bx, 128 + 64 * (1 - by), 128 + 64 * by)]
    for k in range(4):
        mloc[pl.ds(places[k], 64), :] = cat(t0[64 * k : 64 * k + 64], t1[64 * k : 64 * k + 64], axis=1)

    up1 = [
        remote(4, rows(mloc, 128, 64), rows(s1m, 128, 64), mate),
        remote(5, rows(mloc, 0, 128), rows(s1m, 0, 128), mate),
        remote(6, rows(gloc, 0, 192), s1g, mate),
    ]
    down1 = [
        remote(7, rows(ur, 64, 64), rows(dn1, 0, 64), mate),
        remote(8, rows(ur, 192, 64), rows(dn1, 64, 64), mate),
        remote(9, uyi, rows(dn1, 128, 64), mate),
    ]
    down2 = [
        remote(13, rows(dnst, 0, 64), uyi, pair),
        remote(22, rows(dnst, 64, 64), rows(dn1, 0, 64), cross),
        remote(23, rows(dnst, 128, 128), dn2, pair),
    ]
    left = lax.broadcasted_iota(jnp.int32, (64, 128), 1) < 64
    zero = jnp.zeros((64, 128), F32)

    @pl.when(py == 0)
    def _():
        up1[0].start()
        up1[1].start()

    def leaf_flux():
        s0, s1 = closed(*open0), closed(*open1)
        z1 = open1[2] * mm(open1[0], lifted1)
        zq[...], zq_low[...] = split(cat(y_q + mm(across, z1), z1))
        loads[4].wait()
        y0 = mm(s0, src[:128, :] * di0)
        z1 = mm(s1, (src[128:256, :] + mm(across_t, y0)) * di1)
        z = cat(y0 + mm(across, z1), z1)
        g = src[256:, :] + mm(qt, z)
        for k in range(4):
            gloc[pl.ds(places[k], 64), :] = g[64 * k : 64 * k + 64]
        src[:256, :] = z
        ut[...] = jnp.zeros_like(ut)
        for away, _, here in top_sends:

            @pl.when(jnp.logical_not(away))
            def _():
                here.wait()

        for side in range(2):
            known = (1 - px) if side == 0 else (1 - py)

            @pl.when(known == 1)
            def _():
                origin = cx if side == 0 else 2 + cy
                for j in range(4):
                    mine = (lx - origin) * (lx - origin) + (ly - j) * (ly - j) > 0

                    @pl.when(mine)
                    def _():
                        piece = tv.at[side, pl.ds(j * 32, 32), :]
                        pltpu.make_async_remote_copy(src_ref=piece, dst_ref=piece, send_sem=send.at[0], recv_sem=tvrecv.at[side, j],
                                                     device_id=mate, device_id_type=MESH).wait_recv()

                flipped = tv[side].T
                b = by if side == 0 else bx
                ut[64 + 128 * side : 128 + 128 * side, :] = jnp.where(b == 0, flipped[:64], flipped[64:])

        gloc[...] = gloc[...] - mm(mloc[...], ut[...])

    @pl.when(py == 0)
    def _():
        leaf_flux()
        up1[2].start()

        @pl.when(px == 1)
        def _():
            down1[0].wait_recv()
            down1[1].wait_recv()
            uloc[64:128, :] = dn1[64:128, :]

        @pl.when(px == 0)
        def _():
            down2[1].wait_recv()
            uloc[64:128, :] = zero

        down1[2].wait_recv()
        uloc[0:64, :] = dn1[0:64, :]
        uloc[128:192, :] = dn1[128:192, :]
        uloc[192:256, :] = zero
        for copy in up1:
            copy.wait_send()

    @pl.when(py == 1)
    def _():
        up1[0].wait_recv()
        v1 = mloc[128:192, 128:256] + s1m[128:192, 128:256]
        open_1, d1 = face_inverse(v1[:, :64], FIRST_RHO, NEAR_STEPS)
        up1[1].wait_recv()

        def left_of(x):
            return jnp.where(left, x, 0.0)

        def wide_root(k):
            x, y = mloc[k : k + 64, :128], mloc[k : k + 64, 128:]
            return cat(left_of(x), left_of(half_swap(x)), left_of(half_swap(y)), axis=1)

        def wide_mate(k):
            x = s1m[k : k + 64, :128]
            return cat(jnp.where(left, 0.0, half_swap(x)), jnp.where(left, 0.0, x), zero, axis=1)

        gt1 = (wide_root(128) + wide_mate(128)) * d1
        g1 = cat(mloc[0:64, 128:256], s1m[0:64, 128:256], mloc[64:128, 128:256], s1m[64:128, 128:256], mloc[192:256, 128:256])[:, :64]
        half1 = open_1[2] * mm(g1, open_1[0])
        lifted1a = lift(open_1[1], gt1[:, :128])
        shared1 = cat(wide_root(0)[:, :128], wide_mate(0)[:, :128]) - mm(half1[:128], lifted1a)
        up2 = [
            remote(10, rows(st2, 0, 128), rows(r2, 0, 128), pair),
            remote(11, rows(st2, 128, 128), rows(r2, 128, 128), pair),
            remote(12, rows(st2, 256, 192), rows(r2, 256, 192), pair),
            remote(21, rows(st2, 448, 192), rows(r2, 448, 192), pair),
        ]

        @pl.when(px == 0)
        def _():
            st2[0:128, :] = shared1
            up2[0].start()

        lifted1b = lift(open_1[1], gt1[:, 128:])
        p1l, p1r = mm(half1[128:], lifted1a), mm(half1, lifted1b)
        k1 = closed(*open_1)
        x1a = mm(k1, gt1[:, :128])
        x1r = cat(x1a, mm(k1, gt1[:, 128:]), axis=1)
        m1 = cat(
            cat(shared1, cat(wide_root(64)[:, :128], wide_mate(64)[:, :128], wide_root(192)[:, :128]) - p1l),
            cat(*[w[:, 128:] for w in (wide_root(0), wide_mate(0), wide_root(64), wide_mate(64), wide_root(192))]) - p1r,
            axis=1)

        def flux1():
            leaf_flux()
            up1[2].wait_recv()
            b1 = mm(k1, (gloc[128:192, :] + s1g[128:192, :]) * d1)
            x1b[...] = b1
            return cat(gloc[0:64, :], s1g[0:64, :], gloc[64:128, :], s1g[64:128, :], gloc[192:256, :]) - mm(g1, b1)

        @pl.when(px == 0)
        def _():
            st2[128:192, :] = m1[256:320, :128]
            st2[192:256, :] = half_swap(m1[256:320, 256:])
            up2[1].start()
            f1 = flux1()
            st2[256:384, :] = f1[0:128]
            st2[384:448, :] = f1[256:320]
            up2[2].start()
            st2[448:512, :] = x1a
            st2[512:576, :] = half_swap(x1r[:, 256:])
            st2[576:640, :] = x1b[...]
            up2[3].start()
            down2[0].wait_recv()
            down1[2].start()
            down2[2].wait_recv()
            uloc[0:64, :] = dn2[0:64, :]
            uloc[64:128, :] = zero
            uloc[128:192, :] = uyi[...]
            uloc[192:256, :] = dn2[64:128, :]
            down1[2].wait_send()
            for copy in up2:
                copy.wait_send()

        @pl.when(px == 1)
        def _():
            f1 = flux1()
            up2[0].wait_recv()
            open_2, d2 = face_inverse(m1[0:128, :128] + r2[0:128, :], SECOND_RHO, NEAR_STEPS)
            up2[1].wait_recv()
            w0 = r2[128:192, :]
            gt2 = cat(m1[0:128, 128:256], m1[0:128, 256:] + cat(zero, w0).T, axis=1)
            gt2 = gt2 * d2
            lifted2y = lift(open_2[1], gt2[:, 128:])

            up3 = [
                remote(14, rows(st3, 0, 128), rows(r3, 0, 128), side_y),
                remote(15, rows(st3, 128, 128), rows(r3, 128, 128), side_y),
                remote(16, rows(st3, 256, 128), rows(r3, 256, 128), side_y),
                remote(17, rows(st3, 384, 256), rows(r3, 384, 256), side_y),
            ]
            g2y = cat(m1[256:320, :128], w0)
            base2y = cat(m1[256:320, 128:], cat(zero, r2[192:256, :], axis=1))
            half2y = open_2[2] * mm(g2y, open_2[0])
            m2yy = base2y[:, 128:] - mm(half2y, lifted2y)
            st3[0:128, :] = m2yy
            up3[0].start()
            m2yx = base2y[:, :128] - mm(half2y, lift(open_2[1], gt2[:, :128]))
            st3[128:256, :] = m2yx
            up3[1].start()
            k2 = closed(*open_2)
            x2r = mm(k2, gt2)
            g2x = m1[128:256, :128]
            m2x = m1[128:256, 128:] - mm(g2x, x2r)
            st3[256:384, :] = m2x[:, :128]
            up3[2].start()
            up2[2].wait_recv()
            b2 = mm(k2, (f1[0:128] + r2[256:384, :]) * d2)
            f2y = cat(f1[256:320], r2[384:448, :]) - mm(g2y, b2)
            f2x = f1[128:256] - mm(g2x, b2)
            st3[384:512, :] = f2y
            st3[512:640, :] = f2x
            up3[3].start()
            up3[0].wait_recv()
            open_3, d3 = face_inverse(m2yy + r3[0:128, :], THIRD_RHO, NEAR_STEPS)
            up3[1].wait_recv()
            yx = r3[128:256, :]
            gt3 = cat(m2yx, yx, axis=1) * d3
            g3 = cat(m2x[:, 128:], yx.T)
            p3 = open_3[2] * mm(mm(g3, open_3[0]), lift(open_3[1], gt3))

            up4 = [
                remote(18, rows(st4, 0, 136), rows(r4, 0, 136), side_x),
                remote(19, rows(st4, 136, 128), rows(r4, 136, 128), side_x),
                remote(20, rows(st4, 264, 256), rows(r4, 264, 256), side_x),
            ]
            m00, m01 = m2x[:, :128] - p3[:128, :128], -p3[:128, 128:]
            st4[136:264, :] = m01
            up3[2].wait_recv()
            m11 = r3[256:384, :] - p3[128:, 128:]
            on128 = eye_mask(128)
            lower = lax.broadcasted_iota(jnp.int32, (128, 128), 0) >= lax.broadcasted_iota(jnp.int32, (128, 128), 1)
            st4[0:128, :] = jnp.where(lower, m00, m11)
            st4[128:136, :] = jnp.broadcast_to(jnp.sum(jnp.where(on128, m11, 0.0), axis=0, keepdims=True), (8, 128))
            up4[0].start()
            up4[1].start()
            up3[3].wait_recv()
            k3 = closed(*open_3)
            x3r = mm(k3, gt3)
            b3 = mm(k3, (f2y + r3[384:512, :]) * d3)
            f3 = cat(f2x, r3[512:640, :]) - mm(g3, b3)
            st4[264:520, :] = f3
            up4[2].start()
            back = mm(x2r[:, 128:], cat(x3r, b3, axis=1))
            near_map = cat(x3r[:, :128], x2r[:, :128] - back[:, :128])
            far_map = cat(x3r[:, 128:], -back[:, 128:256])
            down_free = cat(b3, b2 - back[:, 256:])
            up2[3].wait_recv()
            outer_map = cat(r2[512:576, :], r2[448:512, :], axis=1)
            outer_part = mm(outer_map, cat(near_map, far_map, down_free, axis=1))
            near_map = cat(near_map, -outer_part[:, :128])
            far_map = cat(far_map, -outer_part[:, 128:256])
            down_free = cat(down_free, r2[576:640, :] - outer_part[:, 256:])
            up4[0].wait_recv()
            mix = r4[0:128, :]
            mix_t = mix.T
            open_4, d4 = face_inverse(m00 + jnp.where(lower, mix, mix_t))
            up4[1].wait_recv()
            v01 = m01 + r4[136:264, :]
            v10 = v01.T
            lifted4 = lift(open_4[1], v01 * d4)
            far_block = m11 + jnp.where(on128, jnp.broadcast_to(r4[128:129, :], (128, 128)), jnp.where(lower, mix_t, mix))
            open_5, d5 = face_inverse(far_block - open_4[2] * mm(mm(v10, open_4[0]), lifted4))
            k4 = closed(*open_4)
            x4 = open_4[2] * mm(open_4[0], lifted4)
            x4t = x4.T
            far_map = far_map - mm(near_map, x4)
            up4[2].wait_recv()
            k5 = closed(*open_5)
            h4 = f3[:128] + r4[264:392, :]
            y4 = mm(k4, h4 * d4)
            u_far = mm(k5, (f3[128:] + r4[392:520, :] - mm(x4t, h4)) * d5)
            u_base = down_free - mm(near_map, y4)
            last_far = split(u_far)
            u_last = u_base[192:] - mm_split(split(far_map[192:]), last_far)
            dnst[0:64, :] = u_last[64:]
            dnst[64:128, :] = u_last[:64]
            down2[0].start()
            down2[1].start()
            u_mid = u_base[64:192] - mm_split(split(far_map[64:192]), last_far)
            dnst[128:192, :] = u_mid[64:]
            dnst[192:256, :] = u_mid[:64]
            down2[2].start()
            u_own = cat(y4, u_base[:64]) - mm_split(split(cat(x4, far_map[:64])), last_far)
            ur[0:64, :] = u_mid[64:]
            ur[64:128, :] = u_last[:64]
            ur[128:256, :] = u_own[:128]
            ur[256:320, :] = u_own[128:]
            ur[320:384, :] = zero
            down1[0].start()
            down1[1].start()
            u_yi = x1b[...] - mm(x1r, ur[...])
            uyi[...] = u_yi
            down1[2].start()
            uloc[0:64, :] = ur[0:64, :]
            uloc[64:128, :] = ur[128:192, :]
            uloc[128:192, :] = u_yi
            uloc[192:256, :] = ur[256:320, :]
            for copy in up3 + up4 + down2 + down1:
                copy.wait_send()

    uloc[...] = uloc[...] + ut[...]
    u_b = cat(*[uloc[pl.ds(p, 64), :] for p in places])
    out_b[...] = u_b
    out_in[...] = src[:256, :] + mm_split((zq[...], zq_low[...]), split(u_b))
    for away, copy, _ in top_sends:

        @pl.when(away)
        def _():
            copy.wait_send()


def store(a, b, out_a, out_b, sem):
    copies = [pltpu.make_async_copy(x, y, sem.at[k]) for k, (x, y) in enumerate(((a, out_a), (b, out_b)))]
    for copy in copies:
        copy.start()
    for copy in copies:
        copy.wait()


def solution(mesh):
    def local(couple_inner, couple_cross, couple_outer, margin, sources, top_values):
        vmem = pl.BlockSpec(memory_space=pltpu.VMEM)
        anywhere = pl.BlockSpec(memory_space=pl.ANY)
        shapes = [(256, 256)] * 3 + [(1, 512), (512, 128), (256, 256), (256, 128), (256, 128), (2, 128, 128), (192, 256), (192, 128),
                  (640, 128), (640, 128), (640, 128), (640, 128), (640, 128), (640, 128), (384, 128), (256, 128), (128, 128), (64, 128),
                  (192, 128), (256, 128), (64, 128)]
        dma = pltpu.SemaphoreType.DMA
        interior, boundary = pl.pallas_call(
            kernel,
            out_shape=(pltpu.VMEM((256, 128), F32), pltpu.VMEM((256, 128), F32)),
            in_specs=[anywhere] * 6,
            out_specs=(vmem, vmem),
            scratch_shapes=[pltpu.VMEM(shape, F32) for shape in shapes] + [pltpu.VMEM((256, 256), BF16)] * 2 + [dma((6,)), dma((24,)), dma((24,)), dma((2, 4))],
            compiler_params=pltpu.CompilerParams(collective_id=0, has_side_effects=True),
        )(
            couple_inner.reshape(256, 256),
            couple_cross.reshape(256, 256),
            couple_outer.reshape(256, 256),
            margin.reshape(1, 512),
            sources.reshape(512, 128),
            top_values,
        )
        interior, boundary = pl.pallas_call(
            store,
            out_shape=(jax.ShapeDtypeStruct((256, 128), F32),) * 2,
            in_specs=[vmem, vmem],
            out_specs=(anywhere, anywhere),
            scratch_shapes=[dma((2,))],
        )(pltpu.with_memory_space_constraint(interior, pltpu.VMEM), pltpu.with_memory_space_constraint(boundary, pltpu.VMEM))
        return interior[None, None], boundary[None, None]

    spec = P("gx", "gy", None, None)
    return jax.shard_map(
        local,
        mesh=mesh,
        in_specs=(spec, spec, spec, P("gx", "gy", None), spec, P("gy", "gx")),
        out_specs=(spec, spec),
        check_vma=False,
    )
```

```python
import jax
import jax.numpy as jnp
from jax import lax
from jax.experimental import pallas as pl
from jax.experimental.pallas import tpu as pltpu
from jax.sharding import PartitionSpec as P

F32 = jnp.float32
BF16 = jnp.bfloat16
MESH = pl.DeviceIdType.MESH

LEAF_RHO = (255 * 0.003515625) / (255 * 0.003515625 + 256 * 0.000390625) / 1.05
FACE_RHO = 1.0 / 1.05
FIRST_RHO = (64 * 9) / (64 * 9 + 192) / 1.05
SECOND_RHO = (64 * 9) / (64 * 9 + 128) / 1.05
THIRD_RHO = (64 * 9) / (64 * 9 + 64) / 1.05
NEAR_STEPS = 5
LEAF_STEPS = 5
FACE_STEPS = 6


def split(x):
    high = x.astype(BF16)
    low = (x - high.astype(F32)).astype(BF16)
    return high, low


def dot(a, b):
    return jnp.dot(a, b, preferred_element_type=F32)


def mm_split(a, b):
    depth, width = b[0].shape
    if depth % 128:
        return dot(a[0], b[0]) + (dot(a[0], b[1]) + dot(a[1], b[0]))
    if width == 128 and depth == 128:
        wide = jnp.concatenate([b[0], b[1]], 1)
        out = dot(jnp.concatenate([a[0], a[1]], 1), jnp.concatenate([wide, wide], 0))
        return out[:, :128] + out[:, 128:]
    if width == 128:
        out = dot(a[0], jnp.concatenate([b[0], b[1]], 1))
        return out[:, :128] + (out[:, 128:] + dot(a[1], b[0]))
    return dot(jnp.concatenate([a[0], a[0], a[1]], 1), jnp.concatenate([b[0], b[1], b[0]], 0))


def mm(a, b):
    return mm_split(split(a), split(b))


def eye_mask(n):
    return lax.broadcasted_iota(jnp.int32, (n, n), 0) == lax.broadcasted_iota(jnp.int32, (n, n), 1)


def inverse_of(h, rho, steps):
    n = h.shape[0]
    eye = jnp.where(eye_mask(n), 1.0, 0.0).astype(F32)
    t = 1.0 / rho
    s, r = None, h
    for k in range(steps):
        square = 2.0 * t * t
        alpha = square / (square - 1.0)
        if k == steps - 1:
            return s, r, alpha
        if k == steps - 2:
            rs = split(r)
            p = mm_split(split(s), rs)
            r = alpha * dot(rs[0], rs[0]) - (alpha - 1.0) * eye
            s = alpha * (s + p)
        elif s is None:
            rs = split(r)
            s = alpha * (eye + r)
            r = alpha * mm_split(rs, rs) - (alpha - 1.0) * eye
        else:
            ss, rs = split(s), split(r)
            p = mm_split((jnp.concatenate([rs[0], ss[0]], 0), jnp.concatenate([rs[1], ss[1]], 0)), rs)
            r = alpha * p[:n] - (alpha - 1.0) * eye
            s = alpha * (s + p[n:])
        t = square - 1.0


def lift(r, x):
    return x + dot(r.astype(BF16), x.astype(BF16))


def closed(s, r, alpha):
    return alpha * (s + dot(s.astype(BF16), r.astype(BF16)))


def face_inverse(v, rho=FACE_RHO, steps=FACE_STEPS):
    n = v.shape[0]
    on = eye_mask(n)
    di = 1.0 / jnp.sum(jnp.where(on, v, 0.0), axis=1, keepdims=True)
    h = jnp.where(on, 0.0, -v * di)
    return inverse_of(h, rho, steps), di


def half_swap(x):
    return pltpu.roll(x, 64, 1)


def cat(*parts, axis=0):
    return jnp.concatenate(parts, axis)


def kernel(ci_h, cq_h, co_h, mg_h, src_h, top, out_in, out_b, ci, cq, co, mg, src, mloc, gloc, ut, tv, s1m, s1g, st2, r2, st3, r3, st4, r4, ur,
           dnst, dn2, uyi, dn1, uloc, x1b, zq, zq_low, load, send, recv, tvrecv):
    loads = [pltpu.make_async_copy(h, v, load.at[k]) for k, (h, v) in enumerate(((ci_h, ci), (cq_h, cq), (mg_h, mg), (co_h, co), (src_h, src)))]
    for copy in loads:
        copy.start()

    gx, gy = lax.axis_index("gx"), lax.axis_index("gy")
    lx, ly = gx % 4, gy % 4
    x0, y0 = gx - lx, gy - ly
    bx, by, cx, cy = lx % 2, ly % 2, lx // 2, ly // 2
    px, py = (bx + cx) % 2, (by + cy) % 2

    def at(i, j):
        return (x0 + i, y0 + j)

    barrier = pltpu.get_barrier_semaphore()
    for i in range(4):
        for j in range(4):
            if i or j:
                pl.semaphore_signal(barrier, 1, device_id=at((lx + i) % 4, (ly + j) % 4), device_id_type=MESH)

    def remote(k, source, target, device):
        return pltpu.make_async_remote_copy(src_ref=source, dst_ref=target, send_sem=send.at[k], recv_sem=recv.at[k],
                                            device_id=device, device_id_type=MESH)

    def rows(ref, start, count):
        return ref.at[pl.ds(start, count), :]

    mate = (gx, gy + 1 - 2 * by)
    pair = (gx + 1 - 2 * bx, gy)
    cross = (gx + 1 - 2 * bx, gy + 1 - 2 * by)
    side_y = at(lx, 3 - ly)
    side_x = at(3 - lx, ly)

    on = eye_mask(256)
    loads[0].wait()
    a = ci[...]
    inner = jnp.where(on, 0.0, 0.5 * (a + a.T))
    loads[1].wait()
    loads[2].wait()
    q = cq[...]
    margin = mg[...]
    m_in = jnp.sum(jnp.where(on, jnp.broadcast_to(margin[:, :256], (256, 256)), 0.0), axis=1, keepdims=True)
    m_out = jnp.sum(jnp.where(on, jnp.broadcast_to(margin[:, 256:], (256, 256)), 0.0), axis=1, keepdims=True)
    d_in = (jnp.sum(inner, 1, keepdims=True) + jnp.sum(q, 1, keepdims=True)) * (1.0 + m_in)
    di = 1.0 / d_in

    di0 = di[:128]
    open0 = inverse_of(inner[:128, :128] * di0, LEAF_RHO, LEAF_STEPS)
    across_t = inner[128:, :128]
    lifted0 = lift(open0[1], cat(inner[:128, 128:], q[:128], axis=1) * di0)
    second = open0[2] * mm(mm(across_t, open0[0]), lifted0)
    rest = q[128:] + second[:, 128:]

    qt = q.T
    loads[3].wait()
    o = co[...]
    outer = jnp.where(on, 0.0, 0.5 * (o + o.T))
    d_out = (jnp.sum(outer, 1, keepdims=True) + jnp.sum(qt, 1, keepdims=True)) * (1.0 + m_out)
    e_out = jnp.where(on, d_out, -outer)
    first = open0[2] * mm(open0[0], lifted0)
    across, y_q = first[:, :128], first[:, 128:]
    e_out = e_out - mm(qt[:, :128], y_q)
    open1, di1 = face_inverse(jnp.where(on[:128, :128], d_in[128:], 0.0) - inner[128:, 128:] - second[:, :128], LEAF_RHO, LEAF_STEPS)
    lifted1 = lift(open1[1], rest * di1)
    pl.semaphore_wait(barrier, 15)
    on_x = 1 - lx // 2
    top_sends = []
    for k in range(4):
        dx = on_x * lx * 3 + (1 - on_x) * k
        dy = on_x * k + (1 - on_x) * (lx - 2) * 3
        away = (dx - lx) * (dx - lx) + (dy - ly) * (dy - ly) > 0
        piece = top.at[:, pl.ds((k // 2) * 128, 128)]
        slot = tv.at[lx // 2, pl.ds(pl.multiple_of(ly * 32, 32), 32), :]
        copy = pltpu.make_async_remote_copy(src_ref=piece, dst_ref=slot, send_sem=send.at[k], recv_sem=tvrecv.at[lx // 2, ly],
                                            device_id=at(dx, dy), device_id_type=MESH)
        here = pltpu.make_async_copy(piece, slot, load.at[5])
        top_sends.append((away, copy, here))

        @pl.when(away)
        def _():
            copy.start()

        @pl.when(jnp.logical_not(away))
        def _():
            here.start()

    places = [pl.multiple_of(p, 64) for p in (64 * (1 - bx), 64 * bx, 128 + 64 * (1 - by), 128 + 64 * by)]
    rest_t = open1[2] * rest.T
    half_y = mm(rest_t[128:], open1[0])
    m_yy = e_out[128:, 128:] - mm(half_y, lifted1[:, 128:])
    m_yy = jnp.where(by == 0, half_swap(m_yy), m_yy)
    for k in range(2):
        mloc[pl.ds(places[2 + k], 64), 128:256] = m_yy[64 * k : 64 * k + 64]

    def up1_block(k, row, height, column):
        where = (pl.ds(row, height), pl.ds(column, 128))
        return remote(k, mloc.at[where], s1m.at[where], mate)

    up1 = [
        up1_block(4, 128, 64, 128),
        up1_block(5, 0, 192, 0),
        up1_block(24, 0, 128, 128),
        remote(6, rows(gloc, 0, 192), s1g, mate),
    ]
    down1 = [
        remote(7, rows(ur, 64, 64), rows(dn1, 0, 64), mate),
        remote(8, rows(ur, 192, 64), rows(dn1, 64, 64), mate),
        remote(9, uyi, rows(dn1, 128, 64), mate),
    ]
    down2 = [
        remote(13, rows(dnst, 0, 64), uyi, pair),
        remote(22, rows(dnst, 64, 64), rows(dn1, 0, 64), cross),
        remote(23, rows(dnst, 128, 128), dn2, pair),
    ]
    left = lax.broadcasted_iota(jnp.int32, (64, 128), 1) < 64
    zero = jnp.zeros((64, 128), F32)

    @pl.when(py == 0)
    def _():
        up1[0].start()

    m_yx = e_out[128:, :128] - mm(half_y, lifted1[:, :128])
    m_x = e_out[:128] - mm(mm(rest_t[:128], open1[0]), lifted1)
    m_xx, m_xy = m_x[:, :128], m_x[:, 128:]
    m_xx = jnp.where(bx == 0, half_swap(m_xx), m_xx)
    m_yx = jnp.where(bx == 0, half_swap(m_yx), m_yx)
    m_xy = jnp.where(by == 0, half_swap(m_xy), m_xy)
    for k in range(2):
        mloc[pl.ds(places[k], 64), :] = cat(m_xx[64 * k : 64 * k + 64], m_xy[64 * k : 64 * k + 64], axis=1)
        mloc[pl.ds(places[2 + k], 64), 0:128] = m_yx[64 * k : 64 * k + 64]

    @pl.when(py == 0)
    def _():
        up1[1].start()
        up1[2].start()

    def leaf_flux():
        s0, s1 = closed(*open0), closed(*open1)
        z1 = open1[2] * mm(open1[0], lifted1)
        zq[...], zq_low[...] = split(cat(y_q + mm(across, z1), z1))
        loads[4].wait()
        y0 = mm(s0, src[:128, :] * di0)
        z1 = mm(s1, (src[128:256, :] + mm(across_t, y0)) * di1)
        z = cat(y0 + mm(across, z1), z1)
        g = src[256:, :] + mm(qt, z)
        for k in range(4):
            gloc[pl.ds(places[k], 64), :] = g[64 * k : 64 * k + 64]
        src[:256, :] = z
        ut[...] = jnp.zeros_like(ut)
        for away, _, here in top_sends:

            @pl.when(jnp.logical_not(away))
            def _():
                here.wait()

        for side in range(2):
            known = (1 - px) if side == 0 else (1 - py)

            @pl.when(known == 1)
            def _():
                origin = cx if side == 0 else 2 + cy
                for j in range(4):
                    mine = (lx - origin) * (lx - origin) + (ly - j) * (ly - j) > 0

                    @pl.when(mine)
                    def _():
                        piece = tv.at[side, pl.ds(j * 32, 32), :]
                        pltpu.make_async_remote_copy(src_ref=piece, dst_ref=piece, send_sem=send.at[0], recv_sem=tvrecv.at[side, j],
                                                     device_id=mate, device_id_type=MESH).wait_recv()

                flipped = tv[side].T
                b = by if side == 0 else bx
                ut[64 + 128 * side : 128 + 128 * side, :] = jnp.where(b == 0, flipped[:64], flipped[64:])

        gloc[...] = gloc[...] - mm(mloc[...], ut[...])

    @pl.when(py == 0)
    def _():
        leaf_flux()
        up1[3].start()

        @pl.when(px == 1)
        def _():
            down1[0].wait_recv()
            down1[1].wait_recv()
            uloc[64:128, :] = dn1[64:128, :]

        @pl.when(px == 0)
        def _():
            down2[1].wait_recv()
            uloc[64:128, :] = zero

        down1[2].wait_recv()
        uloc[0:64, :] = dn1[0:64, :]
        uloc[128:192, :] = dn1[128:192, :]
        uloc[192:256, :] = zero
        for copy in up1:
            copy.wait_send()

    @pl.when(py == 1)
    def _():
        up1[0].wait_recv()
        v1 = mloc[128:192, 128:256] + s1m[128:192, 128:256]
        open_1, d1 = face_inverse(v1[:, :64], FIRST_RHO, NEAR_STEPS)
        up1[1].wait_recv()
        up1[2].wait_recv()

        def left_of(x):
            return jnp.where(left, x, 0.0)

        def wide_root(k):
            x, y = mloc[k : k + 64, :128], mloc[k : k + 64, 128:]
            return cat(left_of(x), left_of(half_swap(x)), left_of(half_swap(y)), axis=1)

        def wide_mate(k):
            x = s1m[k : k + 64, :128]
            return cat(jnp.where(left, 0.0, half_swap(x)), jnp.where(left, 0.0, x), zero, axis=1)

        gt1 = (wide_root(128) + wide_mate(128)) * d1
        g1 = cat(mloc[0:64, 128:256], s1m[0:64, 128:256], mloc[64:128, 128:256], s1m[64:128, 128:256], mloc[192:256, 128:256])[:, :64]
        half1 = open_1[2] * mm(g1, open_1[0])
        lifted1a = lift(open_1[1], gt1[:, :128])
        shared1 = cat(wide_root(0)[:, :128], wide_mate(0)[:, :128]) - mm(half1[:128], lifted1a)
        up2 = [
            remote(10, rows(st2, 0, 128), rows(r2, 0, 128), pair),
            remote(11, rows(st2, 128, 128), rows(r2, 128, 128), pair),
            remote(12, rows(st2, 256, 192), rows(r2, 256, 192), pair),
            remote(21, rows(st2, 448, 192), rows(r2, 448, 192), pair),
        ]

        @pl.when(px == 0)
        def _():
            st2[0:128, :] = shared1
            up2[0].start()

        lifted1b = lift(open_1[1], gt1[:, 128:])
        p1l, p1r = mm(half1[128:], lifted1a), mm(half1, lifted1b)
        k1 = closed(*open_1)
        x1a = mm(k1, gt1[:, :128])
        x1r = cat(x1a, mm(k1, gt1[:, 128:]), axis=1)
        m1 = cat(
            cat(shared1, cat(wide_root(64)[:, :128], wide_mate(64)[:, :128], wide_root(192)[:, :128]) - p1l),
            cat(*[w[:, 128:] for w in (wide_root(0), wide_mate(0), wide_root(64), wide_mate(64), wide_root(192))]) - p1r,
            axis=1)

        def flux1():
            leaf_flux()
            up1[3].wait_recv()
            b1 = mm(k1, (gloc[128:192, :] + s1g[128:192, :]) * d1)
            x1b[...] = b1
            return cat(gloc[0:64, :], s1g[0:64, :], gloc[64:128, :], s1g[64:128, :], gloc[192:256, :]) - mm(g1, b1)

        @pl.when(px == 0)
        def _():
            st2[128:192, :] = m1[256:320, :128]
            st2[192:256, :] = half_swap(m1[256:320, 256:])
            up2[1].start()
            f1 = flux1()
            st2[256:384, :] = f1[0:128]
            st2[384:448, :] = f1[256:320]
            up2[2].start()
            st2[448:512, :] = x1a
            st2[512:576, :] = half_swap(x1r[:, 256:])
            st2[576:640, :] = x1b[...]
            up2[3].start()
            down2[0].wait_recv()
            down1[2].start()
            down2[2].wait_recv()
            uloc[0:64, :] = dn2[0:64, :]
            uloc[64:128, :] = zero
            uloc[128:192, :] = uyi[...]
            uloc[192:256, :] = dn2[64:128, :]
            down1[2].wait_send()
            for copy in up2:
                copy.wait_send()

        @pl.when(px == 1)
        def _():
            f1 = flux1()
            up2[0].wait_recv()
            open_2, d2 = face_inverse(m1[0:128, :128] + r2[0:128, :], SECOND_RHO, NEAR_STEPS)
            up2[1].wait_recv()
            w0 = r2[128:192, :]
            gt2 = cat(m1[0:128, 128:256], m1[0:128, 256:] + cat(zero, w0).T, axis=1)
            gt2 = gt2 * d2
            lifted2y = lift(open_2[1], gt2[:, 128:])

            up3 = [
                remote(14, rows(st3, 0, 128), rows(r3, 0, 128), side_y),
                remote(15, rows(st3, 128, 128), rows(r3, 128, 128), side_y),
                remote(16, rows(st3, 256, 128), rows(r3, 256, 128), side_y),
                remote(17, rows(st3, 384, 256), rows(r3, 384, 256), side_y),
            ]
            g2y = cat(m1[256:320, :128], w0)
            base2y = cat(m1[256:320, 128:], cat(zero, r2[192:256, :], axis=1))
            half2y = open_2[2] * mm(g2y, open_2[0])
            m2yy = base2y[:, 128:] - mm(half2y, lifted2y)
            st3[0:128, :] = m2yy
            up3[0].start()
            m2yx = base2y[:, :128] - mm(half2y, lift(open_2[1], gt2[:, :128]))
            st3[128:256, :] = m2yx
            up3[1].start()
            g2x = m1[128:256, :128]
            half2x = open_2[2] * mm(g2x, open_2[0])
            m2x = m1[128:256, 128:] - mm(half2x, lift(open_2[1], gt2))
            st3[256:384, :] = m2x[:, :128]
            up3[2].start()
            k2 = closed(*open_2)
            x2r = mm(k2, gt2)
            up2[2].wait_recv()
            b2 = mm(k2, (f1[0:128] + r2[256:384, :]) * d2)
            f2y = cat(f1[256:320], r2[384:448, :]) - mm(g2y, b2)
            f2x = f1[128:256] - mm(g2x, b2)
            st3[384:512, :] = f2y
            st3[512:640, :] = f2x
            up3[3].start()
            up3[0].wait_recv()
            open_3, d3 = face_inverse(m2yy + r3[0:128, :], THIRD_RHO, NEAR_STEPS)
            up3[1].wait_recv()
            yx = r3[128:256, :]
            gt3 = cat(m2yx, yx, axis=1) * d3
            g3 = cat(m2x[:, 128:], yx.T)
            p3 = open_3[2] * mm(mm(g3, open_3[0]), lift(open_3[1], gt3))

            up4 = [
                remote(18, rows(st4, 0, 136), rows(r4, 0, 136), side_x),
                remote(19, rows(st4, 136, 128), rows(r4, 136, 128), side_x),
                remote(20, rows(st4, 264, 256), rows(r4, 264, 256), side_x),
            ]
            m00, m01 = m2x[:, :128] - p3[:128, :128], -p3[:128, 128:]
            st4[136:264, :] = m01
            up3[2].wait_recv()
            m11 = r3[256:384, :] - p3[128:, 128:]
            on128 = eye_mask(128)
            lower = lax.broadcasted_iota(jnp.int32, (128, 128), 0) >= lax.broadcasted_iota(jnp.int32, (128, 128), 1)
            st4[0:128, :] = jnp.where(lower, m00, m11)
            st4[128:136, :] = jnp.broadcast_to(jnp.sum(jnp.where(on128, m11, 0.0), axis=0, keepdims=True), (8, 128))
            up4[0].start()
            up4[1].start()
            up3[3].wait_recv()
            k3 = closed(*open_3)
            x3r = mm(k3, gt3)
            b3 = mm(k3, (f2y + r3[384:512, :]) * d3)
            f3 = cat(f2x, r3[512:640, :]) - mm(g3, b3)
            st4[264:520, :] = f3
            up4[2].start()
            back = mm(x2r[:, 128:], cat(x3r, b3, axis=1))
            near_map = cat(x3r[:, :128], x2r[:, :128] - back[:, :128])
            far_map = cat(x3r[:, 128:], -back[:, 128:256])
            down_free = cat(b3, b2 - back[:, 256:])
            up2[3].wait_recv()
            outer_map = cat(r2[512:576, :], r2[448:512, :], axis=1)
            outer_part = mm(outer_map, cat(near_map, far_map, down_free, axis=1))
            near_map = cat(near_map, -outer_part[:, :128])
            far_map = cat(far_map, -outer_part[:, 128:256])
            down_free = cat(down_free, r2[576:640, :] - outer_part[:, 256:])
            up4[0].wait_recv()
            mix = r4[0:128, :]
            mix_t = mix.T
            open_4, d4 = face_inverse(m00 + jnp.where(lower, mix, mix_t))
            up4[1].wait_recv()
            v01 = m01 + r4[136:264, :]
            v10 = v01.T
            lifted4 = lift(open_4[1], v01 * d4)
            far_block = m11 + jnp.where(on128, jnp.broadcast_to(r4[128:129, :], (128, 128)), jnp.where(lower, mix_t, mix))
            open_5, d5 = face_inverse(far_block - open_4[2] * mm(mm(v10, open_4[0]), lifted4))
            k4 = closed(*open_4)
            x4 = open_4[2] * mm(open_4[0], lifted4)
            x4t = x4.T
            far_map = far_map - mm(near_map, x4)
            up4[2].wait_recv()
            k5 = closed(*open_5)
            h4 = f3[:128] + r4[264:392, :]
            y4 = mm(k4, h4 * d4)
            u_far = mm(k5, (f3[128:] + r4[392:520, :] - mm(x4t, h4)) * d5)
            u_base = down_free - mm(near_map, y4)
            last_far = split(u_far)
            u_last = u_base[192:] - mm_split(split(far_map[192:]), last_far)
            dnst[0:64, :] = u_last[64:]
            dnst[64:128, :] = u_last[:64]
            down2[0].start()
            down2[1].start()
            u_mid = u_base[64:192] - mm_split(split(far_map[64:192]), last_far)
            dnst[128:192, :] = u_mid[64:]
            dnst[192:256, :] = u_mid[:64]
            down2[2].start()
            u_own = cat(y4, u_base[:64]) - mm_split(split(cat(x4, far_map[:64])), last_far)
            ur[0:64, :] = u_mid[64:]
            ur[64:128, :] = u_last[:64]
            ur[128:256, :] = u_own[:128]
            ur[256:320, :] = u_own[128:]
            ur[320:384, :] = zero
            down1[0].start()
            down1[1].start()
            u_yi = x1b[...] - mm(x1r, ur[...])
            uyi[...] = u_yi
            down1[2].start()
            uloc[0:64, :] = ur[0:64, :]
            uloc[64:128, :] = ur[128:192, :]
            uloc[128:192, :] = u_yi
            uloc[192:256, :] = ur[256:320, :]
            for copy in up3 + up4 + down2 + down1:
                copy.wait_send()

    uloc[...] = uloc[...] + ut[...]
    u_b = cat(*[uloc[pl.ds(p, 64), :] for p in places])
    out_b[...] = u_b
    out_in[...] = src[:256, :] + mm_split((zq[...], zq_low[...]), split(u_b))
    for away, copy, _ in top_sends:

        @pl.when(away)
        def _():
            copy.wait_send()


def store(a, b, out_a, out_b, sem):
    copies = [pltpu.make_async_copy(x, y, sem.at[k]) for k, (x, y) in enumerate(((a, out_a), (b, out_b)))]
    for copy in copies:
        copy.start()
    for copy in copies:
        copy.wait()


def solution(mesh):
    def local(couple_inner, couple_cross, couple_outer, margin, sources, top_values):
        vmem = pl.BlockSpec(memory_space=pltpu.VMEM)
        anywhere = pl.BlockSpec(memory_space=pl.ANY)
        shapes = [(256, 256)] * 3 + [(1, 512), (512, 128), (256, 256), (256, 128), (256, 128), (2, 128, 128), (192, 256), (192, 128),
                  (640, 128), (640, 128), (640, 128), (640, 128), (640, 128), (640, 128), (384, 128), (256, 128), (128, 128), (64, 128),
                  (192, 128), (256, 128), (64, 128)]
        dma = pltpu.SemaphoreType.DMA
        interior, boundary = pl.pallas_call(
            kernel,
            out_shape=(pltpu.VMEM((256, 128), F32), pltpu.VMEM((256, 128), F32)),
            in_specs=[anywhere] * 6,
            out_specs=(vmem, vmem),
            scratch_shapes=[pltpu.VMEM(shape, F32) for shape in shapes] + [pltpu.VMEM((256, 256), BF16)] * 2 + [dma((6,)), dma((25,)), dma((25,)), dma((2, 4))],
            compiler_params=pltpu.CompilerParams(collective_id=0, has_side_effects=True),
        )(
            couple_inner.reshape(256, 256),
            couple_cross.reshape(256, 256),
            couple_outer.reshape(256, 256),
            margin.reshape(1, 512),
            sources.reshape(512, 128),
            top_values,
        )
        interior, boundary = pl.pallas_call(
            store,
            out_shape=(jax.ShapeDtypeStruct((256, 128), F32),) * 2,
            in_specs=[vmem, vmem],
            out_specs=(anywhere, anywhere),
            scratch_shapes=[dma((2,))],
        )(pltpu.with_memory_space_constraint(interior, pltpu.VMEM), pltpu.with_memory_space_constraint(boundary, pltpu.VMEM))
        return interior[None, None], boundary[None, None]

    spec = P("gx", "gy", None, None)
    return jax.shard_map(
        local,
        mesh=mesh,
        in_specs=(spec, spec, spec, P("gx", "gy", None), spec, P("gy", "gx")),
        out_specs=(spec, spec),
        check_vma=False,
    )
```

```python
import jax
import jax.numpy as jnp
from jax import lax
from jax.experimental import pallas as pl
from jax.experimental.pallas import tpu as pltpu
from jax.sharding import PartitionSpec as P

F32 = jnp.float32
BF16 = jnp.bfloat16
MESH = pl.DeviceIdType.MESH

LEAF_RHO = (255 * 0.003515625) / (255 * 0.003515625 + 256 * 0.000390625) / 1.05
FACE_RHO = 1.0 / 1.05
FIRST_RHO = (64 * 9) / (64 * 9 + 192) / 1.05
SECOND_RHO = (64 * 9) / (64 * 9 + 128) / 1.05
THIRD_RHO = (64 * 9) / (64 * 9 + 64) / 1.05
NEAR_STEPS = 5
LEAF_STEPS = 5
FACE_STEPS = 6


def split(x):
    high = x.astype(BF16)
    low = (x - high.astype(F32)).astype(BF16)
    return high, low


def dot(a, b):
    return jnp.dot(a, b, preferred_element_type=F32)


def mm_split(a, b):
    depth, width = b[0].shape
    if depth % 128:
        return dot(a[0], b[0]) + (dot(a[0], b[1]) + dot(a[1], b[0]))
    if width == 128 and depth == 128:
        wide = jnp.concatenate([b[0], b[1]], 1)
        out = dot(jnp.concatenate([a[0], a[1]], 1), jnp.concatenate([wide, wide], 0))
        return out[:, :128] + out[:, 128:]
    if width == 128:
        out = dot(a[0], jnp.concatenate([b[0], b[1]], 1))
        return out[:, :128] + (out[:, 128:] + dot(a[1], b[0]))
    return dot(jnp.concatenate([a[0], a[0], a[1]], 1), jnp.concatenate([b[0], b[1], b[0]], 0))


def mm(a, b):
    return mm_split(split(a), split(b))


def eye_mask(n):
    return lax.broadcasted_iota(jnp.int32, (n, n), 0) == lax.broadcasted_iota(jnp.int32, (n, n), 1)


def inverse_of(h, rho, steps):
    n = h.shape[0]
    eye = jnp.where(eye_mask(n), 1.0, 0.0).astype(F32)
    t = 1.0 / rho
    s, r = None, h
    for k in range(steps):
        square = 2.0 * t * t
        alpha = square / (square - 1.0)
        if k == steps - 1:
            return s, r, alpha
        if k == steps - 2:
            rs = split(r)
            p = mm_split(split(s), rs)
            r = alpha * dot(rs[0], rs[0]) - (alpha - 1.0) * eye
            s = alpha * (s + p)
        elif s is None:
            rs = split(r)
            s = alpha * (eye + r)
            r = alpha * mm_split(rs, rs) - (alpha - 1.0) * eye
        else:
            ss, rs = split(s), split(r)
            p = mm_split((jnp.concatenate([rs[0], ss[0]], 0), jnp.concatenate([rs[1], ss[1]], 0)), rs)
            r = alpha * p[:n] - (alpha - 1.0) * eye
            s = alpha * (s + p[n:])
        t = square - 1.0


def lift(r, x):
    return x + dot(r.astype(BF16), x.astype(BF16))


def closed(s, r, alpha):
    return alpha * (s + dot(s.astype(BF16), r.astype(BF16)))


def face_inverse(v, rho=FACE_RHO, steps=FACE_STEPS):
    n = v.shape[0]
    on = eye_mask(n)
    di = 1.0 / jnp.sum(jnp.where(on, v, 0.0), axis=1, keepdims=True)
    h = jnp.where(on, 0.0, -v * di)
    return inverse_of(h, rho, steps), di


def half_swap(x):
    return pltpu.roll(x, 64, 1)


def cat(*parts, axis=0):
    return jnp.concatenate(parts, axis)


def kernel(ci_h, cq_h, co_h, mg_h, src_h, top, out_in, out_b, ci, cq, co, mg, src, mloc, gloc, ut, tv, s1m, s1g, st2, r2, st3, r3, st4, r4, ur,
           dnst, dn2, uyi, dn1, uloc, x1b, zq, zq_low, load, send, recv, tvrecv):
    loads = [pltpu.make_async_copy(h, v, load.at[k]) for k, (h, v) in enumerate(((ci_h, ci), (cq_h, cq), (mg_h, mg), (co_h, co), (src_h, src)))]
    for copy in loads:
        copy.start()

    gx, gy = lax.axis_index("gx"), lax.axis_index("gy")
    lx, ly = gx % 4, gy % 4
    x0, y0 = gx - lx, gy - ly
    bx, by, cx, cy = lx % 2, ly % 2, lx // 2, ly // 2
    px, py = (bx + cx) % 2, (by + cy) % 2

    def at(i, j):
        return (x0 + i, y0 + j)

    barrier = pltpu.get_barrier_semaphore()
    for i in range(4):
        for j in range(4):
            if i or j:
                pl.semaphore_signal(barrier, 1, device_id=at((lx + i) % 4, (ly + j) % 4), device_id_type=MESH)

    def remote(k, source, target, device):
        return pltpu.make_async_remote_copy(src_ref=source, dst_ref=target, send_sem=send.at[k], recv_sem=recv.at[k],
                                            device_id=device, device_id_type=MESH)

    def rows(ref, start, count):
        return ref.at[pl.ds(start, count), :]

    mate = (gx, gy + 1 - 2 * by)
    pair = (gx + 1 - 2 * bx, gy)
    cross = (gx + 1 - 2 * bx, gy + 1 - 2 * by)
    side_y = at(lx, 3 - ly)
    side_x = at(3 - lx, ly)

    on = eye_mask(256)
    loads[0].wait()
    a = ci[...]
    inner = jnp.where(on, 0.0, 0.5 * (a + a.T))
    loads[1].wait()
    loads[2].wait()
    q = cq[...]
    margin = mg[...]
    m_in = jnp.sum(jnp.where(on, jnp.broadcast_to(margin[:, :256], (256, 256)), 0.0), axis=1, keepdims=True)
    m_out = jnp.sum(jnp.where(on, jnp.broadcast_to(margin[:, 256:], (256, 256)), 0.0), axis=1, keepdims=True)
    d_in = (jnp.sum(inner, 1, keepdims=True) + jnp.sum(q, 1, keepdims=True)) * (1.0 + m_in)
    di = 1.0 / d_in

    di0 = di[:128]
    open0 = inverse_of(inner[:128, :128] * di0, LEAF_RHO, LEAF_STEPS)
    across_t = inner[128:, :128]
    lifted0 = lift(open0[1], cat(inner[:128, 128:], q[:128], axis=1) * di0)
    second = open0[2] * mm(mm(across_t, open0[0]), lifted0)
    rest = q[128:] + second[:, 128:]

    qt = q.T
    loads[3].wait()
    o = co[...]
    outer = jnp.where(on, 0.0, 0.5 * (o + o.T))
    d_out = (jnp.sum(outer, 1, keepdims=True) + jnp.sum(qt, 1, keepdims=True)) * (1.0 + m_out)
    e_out = jnp.where(on, d_out, -outer)
    first = open0[2] * mm(open0[0], lifted0)
    across, y_q = first[:, :128], first[:, 128:]
    e_out = e_out - mm(qt[:, :128], y_q)
    open1, di1 = face_inverse(jnp.where(on[:128, :128], d_in[128:], 0.0) - inner[128:, 128:] - second[:, :128], LEAF_RHO, LEAF_STEPS)
    lifted1 = lift(open1[1], rest * di1)
    pl.semaphore_wait(barrier, 15)
    on_x = 1 - lx // 2
    top_sends = []
    for k in range(4):
        dx = on_x * lx * 3 + (1 - on_x) * k
        dy = on_x * k + (1 - on_x) * (lx - 2) * 3
        away = (dx - lx) * (dx - lx) + (dy - ly) * (dy - ly) > 0
        piece = top.at[:, pl.ds((k // 2) * 128, 128)]
        slot = tv.at[lx // 2, pl.ds(pl.multiple_of(ly * 32, 32), 32), :]
        copy = pltpu.make_async_remote_copy(src_ref=piece, dst_ref=slot, send_sem=send.at[k], recv_sem=tvrecv.at[lx // 2, ly],
                                            device_id=at(dx, dy), device_id_type=MESH)
        here = pltpu.make_async_copy(piece, slot, load.at[5])
        top_sends.append((away, copy, here))

        @pl.when(away)
        def _():
            copy.start()

        @pl.when(jnp.logical_not(away))
        def _():
            here.start()

    m = e_out - open1[2] * mm(mm(rest.T, open1[0]), lifted1)
    t0, t1 = m[:, :128], m[:, 128:]
    t0 = jnp.where(bx == 0, half_swap(t0), t0)
    t1 = jnp.where(by == 0, half_swap(t1), t1)
    places = [pl.multiple_of(p, 64) for p in (64 * (1 - bx), 64 * bx, 128 + 64 * (1 - by), 128 + 64 * by)]
    for k in range(4):
        mloc[pl.ds(places[k], 64), :] = cat(t0[64 * k : 64 * k + 64], t1[64 * k : 64 * k + 64], axis=1)

    up1 = [
        remote(4, rows(mloc, 128, 64), rows(s1m, 128, 64), mate),
        remote(5, rows(mloc, 0, 128), rows(s1m, 0, 128), mate),
        remote(6, rows(gloc, 0, 192), s1g, mate),
    ]
    down1 = [
        remote(7, rows(ur, 64, 64), rows(dn1, 0, 64), mate),
        remote(8, rows(ur, 192, 64), rows(dn1, 64, 64), mate),
        remote(9, uyi, rows(dn1, 128, 64), mate),
    ]
    down2 = [
        remote(13, rows(dnst, 0, 64), uyi, pair),
        remote(22, rows(dnst, 64, 64), rows(dn1, 0, 64), cross),
        remote(23, rows(dnst, 128, 128), dn2, pair),
    ]
    left = lax.broadcasted_iota(jnp.int32, (64, 128), 1) < 64
    zero = jnp.zeros((64, 128), F32)

    @pl.when(py == 0)
    def _():
        up1[0].start()
        up1[1].start()

    def leaf_flux():
        s0, s1 = closed(*open0), closed(*open1)
        z1 = open1[2] * mm(open1[0], lifted1)
        zq[...], zq_low[...] = split(cat(y_q + mm(across, z1), z1))
        loads[4].wait()
        y0 = mm(s0, src[:128, :] * di0)
        z1 = mm(s1, (src[128:256, :] + mm(across_t, y0)) * di1)
        z = cat(y0 + mm(across, z1), z1)
        g = src[256:, :] + mm(qt, z)
        for k in range(4):
            gloc[pl.ds(places[k], 64), :] = g[64 * k : 64 * k + 64]
        src[:256, :] = z
        ut[...] = jnp.zeros_like(ut)
        for away, _, here in top_sends:

            @pl.when(jnp.logical_not(away))
            def _():
                here.wait()

        for side in range(2):
            known = (1 - px) if side == 0 else (1 - py)

            @pl.when(known == 1)
            def _():
                origin = cx if side == 0 else 2 + cy
                for j in range(4):
                    mine = (lx - origin) * (lx - origin) + (ly - j) * (ly - j) > 0

                    @pl.when(mine)
                    def _():
                        piece = tv.at[side, pl.ds(j * 32, 32), :]
                        pltpu.make_async_remote_copy(src_ref=piece, dst_ref=piece, send_sem=send.at[0], recv_sem=tvrecv.at[side, j],
                                                     device_id=mate, device_id_type=MESH).wait_recv()

                flipped = tv[side].T
                b = by if side == 0 else bx
                ut[64 + 128 * side : 128 + 128 * side, :] = jnp.where(b == 0, flipped[:64], flipped[64:])

        gloc[...] = gloc[...] - mm(mloc[...], ut[...])

    @pl.when(py == 0)
    def _():
        leaf_flux()
        up1[2].start()

        @pl.when(px == 1)
        def _():
            down1[0].wait_recv()
            down1[1].wait_recv()
            uloc[64:128, :] = dn1[64:128, :]

        @pl.when(px == 0)
        def _():
            down2[1].wait_recv()
            uloc[64:128, :] = zero

        down1[2].wait_recv()
        uloc[0:64, :] = dn1[0:64, :]
        uloc[128:192, :] = dn1[128:192, :]
        uloc[192:256, :] = zero
        for copy in up1:
            copy.wait_send()

    @pl.when(py == 1)
    def _():
        up1[0].wait_recv()
        v1 = mloc[128:192, 128:256] + s1m[128:192, 128:256]
        open_1, d1 = face_inverse(v1[:, :64], FIRST_RHO, NEAR_STEPS)
        up1[1].wait_recv()

        def left_of(x):
            return jnp.where(left, x, 0.0)

        def wide_root(k):
            x, y = mloc[k : k + 64, :128], mloc[k : k + 64, 128:]
            return cat(left_of(x), left_of(half_swap(x)), left_of(half_swap(y)), axis=1)

        def wide_mate(k):
            x = s1m[k : k + 64, :128]
            return cat(jnp.where(left, 0.0, half_swap(x)), jnp.where(left, 0.0, x), zero, axis=1)

        gt1 = (wide_root(128) + wide_mate(128)) * d1
        g1 = cat(mloc[0:64, 128:256], s1m[0:64, 128:256], mloc[64:128, 128:256], s1m[64:128, 128:256], mloc[192:256, 128:256])[:, :64]
        half1 = open_1[2] * mm(g1, open_1[0])
        lifted1a = lift(open_1[1], gt1[:, :128])
        shared1 = cat(wide_root(0)[:, :128], wide_mate(0)[:, :128]) - mm(half1[:128], lifted1a)
        up2 = [
            remote(10, rows(st2, 0, 128), rows(r2, 0, 128), pair),
            remote(11, rows(st2, 128, 128), rows(r2, 128, 128), pair),
            remote(12, rows(st2, 256, 192), rows(r2, 256, 192), pair),
            remote(21, rows(st2, 448, 192), rows(r2, 448, 192), pair),
        ]

        @pl.when(px == 0)
        def _():
            st2[0:128, :] = shared1
            up2[0].start()

        lifted1b = lift(open_1[1], gt1[:, 128:])
        p1l, p1r = mm(half1[128:], lifted1a), mm(half1, lifted1b)
        k1 = closed(*open_1)
        x1a = mm(k1, gt1[:, :128])
        x1r = cat(x1a, mm(k1, gt1[:, 128:]), axis=1)
        m1 = cat(
            cat(shared1, cat(wide_root(64)[:, :128], wide_mate(64)[:, :128], wide_root(192)[:, :128]) - p1l),
            cat(*[w[:, 128:] for w in (wide_root(0), wide_mate(0), wide_root(64), wide_mate(64), wide_root(192))]) - p1r,
            axis=1)

        def flux1():
            leaf_flux()
            up1[2].wait_recv()
            b1 = mm(k1, (gloc[128:192, :] + s1g[128:192, :]) * d1)
            x1b[...] = b1
            return cat(gloc[0:64, :], s1g[0:64, :], gloc[64:128, :], s1g[64:128, :], gloc[192:256, :]) - mm(g1, b1)

        @pl.when(px == 0)
        def _():
            st2[128:192, :] = m1[256:320, :128]
            st2[192:256, :] = half_swap(m1[256:320, 256:])
            up2[1].start()
            f1 = flux1()
            st2[256:384, :] = f1[0:128]
            st2[384:448, :] = f1[256:320]
            up2[2].start()
            st2[448:512, :] = x1a
            st2[512:576, :] = half_swap(x1r[:, 256:])
            st2[576:640, :] = x1b[...]
            up2[3].start()
            down2[0].wait_recv()
            down1[2].start()
            down2[2].wait_recv()
            uloc[0:64, :] = dn2[0:64, :]
            uloc[64:128, :] = zero
            uloc[128:192, :] = uyi[...]
            uloc[192:256, :] = dn2[64:128, :]
            down1[2].wait_send()
            for copy in up2:
                copy.wait_send()

        @pl.when(px == 1)
        def _():
            f1 = flux1()
            up2[0].wait_recv()
            open_2, d2 = face_inverse(m1[0:128, :128] + r2[0:128, :], SECOND_RHO, NEAR_STEPS)
            up2[1].wait_recv()
            w0 = r2[128:192, :]
            gt2 = cat(m1[0:128, 128:256], m1[0:128, 256:] + cat(zero, w0).T, axis=1)
            gt2 = gt2 * d2
            lifted2y = lift(open_2[1], gt2[:, 128:])

            up3 = [
                remote(14, rows(st3, 0, 128), rows(r3, 0, 128), side_y),
                remote(15, rows(st3, 128, 128), rows(r3, 128, 128), side_y),
                remote(16, rows(st3, 256, 128), rows(r3, 256, 128), side_y),
                remote(17, rows(st3, 384, 256), rows(r3, 384, 256), side_y),
            ]
            g2y = cat(m1[256:320, :128], w0)
            base2y = cat(m1[256:320, 128:], cat(zero, r2[192:256, :], axis=1))
            half2y = open_2[2] * mm(g2y, open_2[0])
            m2yy = base2y[:, 128:] - mm(half2y, lifted2y)
            st3[0:128, :] = m2yy
            up3[0].start()
            m2yx = base2y[:, :128] - mm(half2y, lift(open_2[1], gt2[:, :128]))
            st3[128:256, :] = m2yx
            up3[1].start()
            k2 = closed(*open_2)
            x2r = mm(k2, gt2)
            g2x = m1[128:256, :128]
            m2x = m1[128:256, 128:] - mm(g2x, x2r)
            st3[256:384, :] = m2x[:, :128]
            up3[2].start()
            up2[2].wait_recv()
            b2 = mm(k2, (f1[0:128] + r2[256:384, :]) * d2)
            f2y = cat(f1[256:320], r2[384:448, :]) - mm(g2y, b2)
            f2x = f1[128:256] - mm(g2x, b2)
            st3[384:512, :] = f2y
            st3[512:640, :] = f2x
            up3[3].start()
            up3[0].wait_recv()
            open_3, d3 = face_inverse(m2yy + r3[0:128, :], THIRD_RHO, NEAR_STEPS)
            up3[1].wait_recv()
            yx = r3[128:256, :]
            gt3 = cat(m2yx, yx, axis=1) * d3
            g3 = cat(m2x[:, 128:], yx.T)
            p3 = open_3[2] * mm(mm(g3, open_3[0]), lift(open_3[1], gt3))

            up4 = [
                remote(18, rows(st4, 0, 136), rows(r4, 0, 136), side_x),
                remote(19, rows(st4, 136, 128), rows(r4, 136, 128), side_x),
                remote(20, rows(st4, 264, 256), rows(r4, 264, 256), side_x),
            ]
            m00, m01 = m2x[:, :128] - p3[:128, :128], -p3[:128, 128:]
            st4[136:264, :] = m01
            up3[2].wait_recv()
            m11 = r3[256:384, :] - p3[128:, 128:]
            on128 = eye_mask(128)
            lower = lax.broadcasted_iota(jnp.int32, (128, 128), 0) >= lax.broadcasted_iota(jnp.int32, (128, 128), 1)
            st4[0:128, :] = jnp.where(lower, m00, m11)
            st4[128:136, :] = jnp.broadcast_to(jnp.sum(jnp.where(on128, m11, 0.0), axis=0, keepdims=True), (8, 128))
            up4[0].start()
            up4[1].start()
            up3[3].wait_recv()
            k3 = closed(*open_3)
            x3r = mm(k3, gt3)
            b3 = mm(k3, (f2y + r3[384:512, :]) * d3)
            f3 = cat(f2x, r3[512:640, :]) - mm(g3, b3)
            st4[264:520, :] = f3
            up4[2].start()
            back = mm(x2r[:, 128:], cat(x3r, b3, axis=1))
            near_map = cat(x3r[:, :128], x2r[:, :128] - back[:, :128])
            far_map = cat(x3r[:, 128:], -back[:, 128:256])
            down_free = cat(b3, b2 - back[:, 256:])
            up2[3].wait_recv()
            outer_map = cat(r2[512:576, :], r2[448:512, :], axis=1)
            outer_part = mm(outer_map, cat(near_map, far_map, down_free, axis=1))
            near_map = cat(near_map, -outer_part[:, :128])
            far_map = cat(far_map, -outer_part[:, 128:256])
            down_free = cat(down_free, r2[576:640, :] - outer_part[:, 256:])
            up4[0].wait_recv()
            mix = r4[0:128, :]
            mix_t = mix.T
            open_4, d4 = face_inverse(m00 + jnp.where(lower, mix, mix_t))
            up4[1].wait_recv()
            v01 = m01 + r4[136:264, :]
            v10 = v01.T
            lifted4 = lift(open_4[1], v01 * d4)
            far_block = m11 + jnp.where(on128, jnp.broadcast_to(r4[128:129, :], (128, 128)), jnp.where(lower, mix_t, mix))
            open_5, d5 = face_inverse(far_block - open_4[2] * mm(mm(v10, open_4[0]), lifted4))
            k4 = closed(*open_4)
            x4 = open_4[2] * mm(open_4[0], lifted4)
            x4t = x4.T
            far_map = far_map - mm(near_map, x4)
            up4[2].wait_recv()
            k5 = closed(*open_5)
            h4 = f3[:128] + r4[264:392, :]
            y4 = mm(k4, h4 * d4)
            u_far = mm(k5, (f3[128:] + r4[392:520, :] - mm(x4t, h4)) * d5)
            u_base = down_free - mm(near_map, y4)
            last_far = split(u_far)
            u_last = u_base[192:] - mm_split(split(far_map[192:]), last_far)
            dnst[0:64, :] = u_last[64:]
            dnst[64:128, :] = u_last[:64]
            down2[0].start()
            down2[1].start()
            u_mid = u_base[64:192] - mm_split(split(far_map[64:192]), last_far)
            dnst[128:192, :] = u_mid[64:]
            dnst[192:256, :] = u_mid[:64]
            down2[2].start()
            u_own = cat(y4, u_base[:64]) - mm_split(split(cat(x4, far_map[:64])), last_far)
            ur[0:64, :] = u_mid[64:]
            ur[64:128, :] = u_last[:64]
            ur[128:256, :] = u_own[:128]
            ur[256:320, :] = u_own[128:]
            ur[320:384, :] = zero
            down1[0].start()
            down1[1].start()
            u_yi = x1b[...] - mm(x1r, ur[...])
            uyi[...] = u_yi
            down1[2].start()
            uloc[0:64, :] = ur[0:64, :]
            uloc[64:128, :] = ur[128:192, :]
            uloc[128:192, :] = u_yi
            uloc[192:256, :] = ur[256:320, :]
            for copy in up3 + up4 + down2 + down1:
                copy.wait_send()

    uloc[...] = uloc[...] + ut[...]
    u_b = cat(*[uloc[pl.ds(p, 64), :] for p in places])
    out_b[...] = u_b
    out_in[...] = src[:256, :] + mm_split((zq[...], zq_low[...]), split(u_b))
    for away, copy, _ in top_sends:

        @pl.when(away)
        def _():
            copy.wait_send()


def store(a, b, out_a, out_b, sem):
    copies = [pltpu.make_async_copy(x, y, sem.at[k]) for k, (x, y) in enumerate(((a, out_a), (b, out_b)))]
    for copy in copies:
        copy.start()
    for copy in copies:
        copy.wait()


def solution(mesh):
    def local(couple_inner, couple_cross, couple_outer, margin, sources, top_values):
        vmem = pl.BlockSpec(memory_space=pltpu.VMEM)
        anywhere = pl.BlockSpec(memory_space=pl.ANY)
        shapes = [(256, 256)] * 3 + [(1, 512), (512, 128), (256, 256), (256, 128), (256, 128), (2, 128, 128), (192, 256), (192, 128),
                  (640, 128), (640, 128), (640, 128), (640, 128), (640, 128), (640, 128), (384, 128), (256, 128), (128, 128), (64, 128),
                  (192, 128), (256, 128), (64, 128)]
        dma = pltpu.SemaphoreType.DMA
        interior, boundary = pl.pallas_call(
            kernel,
            out_shape=(pltpu.VMEM((256, 128), F32), pltpu.VMEM((256, 128), F32)),
            in_specs=[anywhere] * 6,
            out_specs=(vmem, vmem),
            scratch_shapes=[pltpu.VMEM(shape, F32) for shape in shapes] + [pltpu.VMEM((256, 256), BF16)] * 2 + [dma((6,)), dma((24,)), dma((24,)), dma((2, 4))],
            compiler_params=pltpu.CompilerParams(collective_id=0, has_side_effects=True),
        )(
            couple_inner.reshape(256, 256),
            couple_cross.reshape(256, 256),
            couple_outer.reshape(256, 256),
            margin.reshape(1, 512),
            sources.reshape(512, 128),
            top_values,
        )
        interior, boundary = pl.pallas_call(
            store,
            out_shape=(jax.ShapeDtypeStruct((256, 128), F32),) * 2,
            in_specs=[vmem, vmem],
            out_specs=(anywhere, anywhere),
            scratch_shapes=[dma((2,))],
        )(pltpu.with_memory_space_constraint(interior, pltpu.VMEM), pltpu.with_memory_space_constraint(boundary, pltpu.VMEM))
        return interior[None, None], boundary[None, None]

    spec = P("gx", "gy", None, None)
    return jax.shard_map(
        local,
        mesh=mesh,
        in_specs=(spec, spec, spec, P("gx", "gy", None), spec, P("gy", "gx")),
        out_specs=(spec, spec),
        check_vma=False,
    )
```
